512 devices in a mesh: tile: 128 (over z_lo, y, x, core), head: 4 (over z_hi).
Axes of the slice: x: 4, y: 4, z: 16 (z_hi: 4, z_lo: 4; z = z_hi * 4 + z_lo), core: 2. Of those that a mesh axis runs over, the one named last changes fastest.
Arguments:
- self_query: bfloat16 [16384, 5120], P('tile', 'head')
- self_key: bfloat16 [16384, 5120], P('tile', 'head')
- self_value: bfloat16 [16384, 5120], P('tile', 'head'), may hold values from -6 to 6
- cross_query: bfloat16 [16384, 5120], P('tile', 'head')
- text_key: bfloat16 [32768, 5120], P('tile', 'head'), as said below
- text_value: bfloat16 [32768, 5120], P('tile', 'head'), as said below
- query_gain: float32 [5120], P('head'), may hold values from 0.5 to 1.5
- key_gain: float32 [5120], P('head'), may hold values from 0.5 to 1.5
- cross_gain: float32 [5120], P('head'), may hold values from 0.5 to 1.5
- text_gain: float32 [5120], P('head'), may hold values from 0.5 to 1.5
- tile_item: int32 [128], replicated, may hold values from 0 to 63, as said below
- row_count: int32 [128], replicated, may hold values from 32 to 128, as said below
- text_len: int32 [128], replicated, may hold values from 2 to 256, as said below
Outputs:
- attended: bfloat16 [16384, 5120], P('tile', 'head')
The draws below stay inside these ranges and needn't reach their ends.
Inputs may be any that keep to these rules, and one draw needn't show every extreme that they name: `tile_item`: never falling and 0 on the first tile; every item holds 1 to 7 consecutive tiles, some item holds exactly 7, and there are 64 items. `row_count`: some tile holds exactly 128. `text_len`: entries past the last item are not used; some item has exactly 256. `text_key`: tiles of one item hold the same text rows. `text_value`: tiles of one item hold the same text rows.
All inputs are finite; a program needn't handle non-finite values.
Results may differ from the reference program's by a relative error of at most 0.0015.
The reference program's roundings to bfloat16 on the way count: a program that leaves them out, or rounds other values in their place, can miss the bound.
Values may be sent and summed in bfloat16 or wider, within the bound.
No kernel may reach another device: no remote copies, remote signals or barrier semaphores. Data moves between devices by JAX's collectives and lax.ppermute only.
A program may use at most 64 MiB of HBM per device.

```python
import math
import jax
import jax.numpy as jnp
from jax import lax

D = 5120
HEADS = 40
HD = 128
ROWS = 128
TXT = 256
HGT = 30
WID = 52
SPAN = 7
TILES = 128
TOKENS = 16384


def layout(key):
    groups = TILES // 2
    pool = (groups - 1) * (SPAN - 1)
    extra = TILES - SPAN - (groups - 1)
    order = jax.random.permutation(jax.random.fold_in(key, 11), pool)
    marked = (order < extra).astype(jnp.int32).reshape(groups - 1, SPAN - 1)
    rest = (1 + jnp.sum(marked, axis=1)).astype(jnp.int32)
    chosen = jax.random.randint(jax.random.fold_in(key, 16), (), 0, groups)
    group_ids = jnp.arange(groups)
    pick = jnp.clip(jnp.where(group_ids < chosen, group_ids, group_ids - 1), 0, groups - 2)
    spans = jnp.where(group_ids == chosen, SPAN, rest[pick]).astype(jnp.int32)
    ends = jnp.cumsum(spans)
    tile_ids = jnp.arange(TILES)
    owner = jnp.sum((ends[None, :] <= tile_ids[:, None]).astype(jnp.int32), axis=1)
    return owner.astype(jnp.int32)


def draw_self_query(key, part):
    base = jax.random.normal(jax.random.fold_in(key, 31), (TOKENS, D), jnp.float32)
    return base.astype(jnp.bfloat16)


def draw_self_key(key, part):
    base = jax.random.normal(jax.random.fold_in(key, 41), (TOKENS, D), jnp.float32)
    return base.astype(jnp.bfloat16)


def draw_cross_query(key, part):
    base = jax.random.normal(jax.random.fold_in(key, 51), (TOKENS, D), jnp.float32)
    return base.astype(jnp.bfloat16)


def draw_text_key(key, part):
    owner = layout(key)
    base = jax.random.normal(jax.random.fold_in(key, 61), (TILES * TXT, D), jnp.float32)
    return base.reshape(TILES, TXT, D)[owner].reshape(TILES * TXT, D).astype(jnp.bfloat16)


def draw_text_value(key, part):
    owner = layout(key)
    base = jax.random.normal(jax.random.fold_in(key, 71), (TILES, TXT, D), jnp.float32)
    return base[owner].reshape(TILES * TXT, D).astype(jnp.bfloat16)


def draw_tile_item(key, part):
    return layout(key)


def draw_row_count(key, part):
    counts = jax.random.randint(jax.random.fold_in(key, 14), (TILES,), ROWS // 4, ROWS + 1)
    chosen = jax.random.randint(jax.random.fold_in(key, 15), (), 0, TILES)
    return jnp.where(jnp.arange(TILES) == chosen, ROWS, counts).astype(jnp.int32)


def draw_text_len(key, part):
    owner = layout(key)
    items = owner[TILES - 1] + 1
    lengths = jax.random.randint(jax.random.fold_in(key, 12), (TILES,), 2, TXT + 1)
    chosen = jax.random.randint(jax.random.fold_in(key, 13), (), 0, items)
    return jnp.where(jnp.arange(TILES) == chosen, TXT, lengths).astype(jnp.int32)


def steps_of(key, shape, shards, least, largest):
    def one(dim, blocks):
        heights = jax.random.uniform(jax.random.fold_in(jax.random.fold_in(key, 6), dim), (blocks,), jnp.float32, least / len(shards), largest / len(shards))
        return jnp.repeat(jnp.exp(heights), shape[dim] // blocks).reshape((-1,) + (1,) * (len(shape) - dim - 1))

    level = one(*shards[0])
    for cut in shards[1:]:
        level = level * one(*cut)
    return level


def bell_draw(own_key, dims, width, bound, shards=(), kind=jnp.bfloat16):
    array = jax.random.normal(own_key, dims, jnp.float32) * width
    if len(shards) > 0:
        array = steps_of(own_key, dims, shards, -0.22, 0.18) * array
    return jnp.clip(array, min=-bound, max=bound).astype(kind)


def setup_inputs(seed: int = 0) -> dict:
    seeds = jax.random.split(jax.random.key(seed), 14)
    self_query = draw_self_query(jax.random.fold_in(seeds[13], 71), 0)
    self_key = draw_self_key(jax.random.fold_in(seeds[13], 71), 0)
    self_value = bell_draw(seeds[2], (TOKENS, D), 1.0, 6.0, ((0, 128), (1, 4)))
    cross_query = draw_cross_query(jax.random.fold_in(seeds[13], 71), 0)
    text_key = draw_text_key(jax.random.fold_in(seeds[13], 71), 0)
    text_value = draw_text_value(jax.random.fold_in(seeds[13], 71), 0)
    query_gain = jnp.clip(1.0 + 0.1 * jax.random.normal(seeds[6], (D,), jnp.float32), 0.5, 1.5)
    key_gain = jnp.clip(1.0 + 0.1 * jax.random.normal(seeds[7], (D,), jnp.float32), 0.5, 1.5)
    cross_gain = jnp.clip(1.0 + 0.1 * jax.random.normal(seeds[8], (D,), jnp.float32), 0.5, 1.5)
    text_gain = jnp.clip(1.0 + 0.1 * jax.random.normal(seeds[9], (D,), jnp.float32), 0.5, 1.5)
    tile_item = draw_tile_item(jax.random.fold_in(seeds[13], 71), 0)
    row_count = draw_row_count(jax.random.fold_in(seeds[13], 71), 0)
    text_len = draw_text_len(jax.random.fold_in(seeds[13], 71), 0)
    return {"self_query": self_query, "self_key": self_key, "self_value": self_value, "cross_query": cross_query, "text_key": text_key, "text_value": text_value, "query_gain": query_gain, "key_gain": key_gain, "cross_gain": cross_gain, "text_gain": text_gain, "tile_item": tile_item, "row_count": row_count, "text_len": text_len}


EPSILON = 1e-06

def frequencies(amount, dimension):
    return 1.0 / 10000.0 ** (jnp.arange(amount, dtype=jnp.float32) * 2.0 / dimension)

def rope_angles(positions):
    spatial = HD // 6
    temporal = HD // 2 - 2 * spatial
    frame = (positions // (HGT * WID)).astype(jnp.float32)
    height = (positions // WID % HGT).astype(jnp.float32)
    across = (positions % WID).astype(jnp.float32)
    return jnp.concatenate([frame[:, None] * frequencies(temporal, 2 * temporal)[None, :], height[:, None] * frequencies(spatial, 2 * spatial)[None, :], across[:, None] * frequencies(spatial, 2 * spatial)[None, :]], axis=1)

def pair_partner(matrix):
    index = jnp.arange(matrix.shape[-1])
    return jnp.where(index % 2 == 0, -jnp.roll(matrix, -1, axis=-1), jnp.roll(matrix, 1, axis=-1))

def rotate(matrix, angle):
    cosine = jnp.repeat(jnp.cos(angle), 2, axis=1)
    sine = jnp.repeat(jnp.sin(angle), 2, axis=1)
    shaped = matrix.reshape(matrix.shape[0], matrix.shape[1] // HD, HD)
    turned = shaped * cosine[:, None, :] + pair_partner(shaped) * sine[:, None, :]
    return turned.reshape(matrix.shape)

def normalize(matrix, gain):
    values = matrix.astype(jnp.float32)
    mean_square = lax.optimization_barrier(jnp.sum(values * values, axis=1)) / D
    return values * lax.rsqrt(mean_square[:, None] + EPSILON) * gain.astype(jnp.float32)[None, :]

def attend(query, key_rows, value_rows, live):
    scale = 1.0 / math.sqrt(HD)
    query_heads = query.astype(jnp.float32).reshape(query.shape[0], HEADS, HD)
    key_heads = key_rows.astype(jnp.float32).reshape(key_rows.shape[0], HEADS, HD)
    value_heads = value_rows.astype(jnp.float32).reshape(value_rows.shape[0], HEADS, HD)
    scores = jnp.einsum('qhd,khd->hqk', query_heads, key_heads) * scale
    scores = jnp.where(live[None, None, :], scores, -1e+30)
    highest = lax.optimization_barrier(jnp.max(scores, axis=2, keepdims=True))
    weights = jnp.exp(scores - highest)
    total = lax.optimization_barrier(jnp.sum(weights, axis=2, keepdims=True))
    rounded = lax.optimization_barrier(weights.astype(jnp.bfloat16)).astype(jnp.float32)
    mixed = jnp.einsum('hqk,khd->qhd', rounded, value_heads) / jnp.moveaxis(total, 0, 1)
    return mixed.reshape(query.shape[0], HEADS * HD)

def reference(self_query, self_key, self_value, cross_query, text_key, text_value, query_gain, key_gain, cross_gain, text_gain, tile_item, row_count, text_len):
    tile_ids = jnp.arange(TILES, dtype=jnp.int32)
    first_tile = lax.optimization_barrier(jnp.sum((tile_item[None, :] < tile_item[:, None]).astype(jnp.int32), axis=1))
    positions = ((tile_ids - first_tile)[:, None] * ROWS + jnp.arange(ROWS, dtype=jnp.int32)[None, :]).reshape(TOKENS)
    angle = rope_angles(positions)
    queries = rotate(normalize(self_query, query_gain), angle).astype(jnp.bfloat16)
    keys = rotate(normalize(self_key, key_gain), angle).astype(jnp.bfloat16)
    cross = normalize(cross_query, cross_gain).astype(jnp.bfloat16)
    texts = normalize(text_key, text_gain).astype(jnp.bfloat16)
    reach = SPAN - 1
    window = 2 * SPAN - 1
    keys_padded = jnp.pad(keys, ((reach * ROWS, reach * ROWS), (0, 0)))
    values_padded = jnp.pad(self_value, ((reach * ROWS, reach * ROWS), (0, 0)))
    items_padded = jnp.pad(tile_item, (reach, reach), constant_values=-1)
    counts_padded = jnp.pad(row_count, (reach, reach))

    def one_tile(tile_index):
        start = (tile_index * ROWS).astype(jnp.int32)
        query = lax.dynamic_slice_in_dim(queries, start, ROWS, 0)
        near_keys = lax.dynamic_slice_in_dim(keys_padded, start, window * ROWS, 0)
        near_values = lax.dynamic_slice_in_dim(values_padded, start, window * ROWS, 0)
        near_items = lax.dynamic_slice_in_dim(items_padded, tile_index.astype(jnp.int32), window, 0)
        near_counts = lax.dynamic_slice_in_dim(counts_padded, tile_index.astype(jnp.int32), window, 0)
        item_here = tile_item[tile_index]
        live = ((near_items == item_here)[:, None] & (jnp.arange(ROWS, dtype=jnp.int32)[None, :] < near_counts[:, None])).reshape(window * ROWS)
        self_part = attend(query, near_keys, near_values, live)
        text_start = (tile_index * TXT).astype(jnp.int32)
        cross_rows = lax.dynamic_slice_in_dim(cross, start, ROWS, 0)
        text_rows = lax.dynamic_slice_in_dim(texts, text_start, TXT, 0)
        text_vals = lax.dynamic_slice_in_dim(text_value, text_start, TXT, 0)
        text_live = jnp.arange(TXT, dtype=jnp.int32) < text_len[item_here]
        text_part = attend(cross_rows, text_rows, text_vals, text_live)
        return (self_part + text_part).astype(jnp.bfloat16)
    return lax.map(one_tile, tile_ids).reshape(TOKENS, D)
```

```python
import math

import jax
import jax.numpy as jnp
import numpy as np
from jax import lax
from jax.experimental import pallas as pl
from jax.experimental.pallas import tpu as pltpu
from jax.sharding import PartitionSpec as P

D = 5120
HD = 128
HGT = 30
WID = 52
SPAN = 7
ROWS = 128
EPSILON = 1e-06
SCALE = 1.0 / math.sqrt(HD)
NEG = -1e30


def rope_tables():
    spatial = HD // 6
    temporal = HD // 2 - 2 * spatial
    positions = np.arange(SPAN * ROWS)

    def freq(amount):
        exponent = np.arange(amount, dtype=np.float64) * 2.0 / (2 * amount)
        return (1.0 / 10000.0**exponent).astype(np.float32)

    def part(values, amount):
        return values.astype(np.float32)[:, None] * freq(amount)[None, :]

    angle = np.concatenate(
        [
            part(positions // (HGT * WID), temporal),
            part(positions // WID % HGT, spatial),
            part(positions % WID, spatial),
        ],
        axis=1,
    ).astype(np.float64)
    cosine = np.repeat(np.cos(angle), 2, axis=1).astype(np.float32)
    sine = np.stack([-np.sin(angle), np.sin(angle)], axis=2)
    return cosine, sine.reshape(SPAN * ROWS, HD).astype(np.float32)


def shifted(value, by):
    peers = lax.axis_size("tile")
    return lax.ppermute(
        value, "tile", [(i, i + by) for i in range(peers) if 0 <= i + by < peers]
    )


def swapped(value):
    peers = lax.axis_size("tile")
    return lax.ppermute(value, "tile", [(i, i ^ 1) for i in range(peers)])


def by_rows(total_row):
    factor = lax.rsqrt(total_row / D + EPSILON)
    return jnp.transpose(jnp.broadcast_to(factor, (ROWS, ROWS)))


def rotated(normal, cosine, sine, even):
    partner = jnp.where(even, pltpu.roll(normal, HD - 1, 1), pltpu.roll(normal, 1, 1))
    return normal * cosine + partner * sine


def prefix_live(shape, count):
    return lax.broadcasted_iota(jnp.int32, shape, 1) < count


def sums_kernel(q_ref, k_ref, c_ref, t_ref, out_ref):

    def total(ref, first):
        rows = None
        for head in range(ref.shape[1] // HD):
            x = ref[first : first + ROWS, head * HD : (head + 1) * HD].astype(jnp.float32)
            rows = x * x if rows is None else rows + x * x
        return jnp.sum(jnp.transpose(rows), axis=0, keepdims=True)

    out_ref[0:1, :] = total(q_ref, 0)
    out_ref[1:2, :] = total(k_ref, 0)
    out_ref[2:3, :] = total(c_ref, 0)
    out_ref[3:4, :] = total(t_ref, 0)
    out_ref[4:5, :] = total(t_ref, ROWS)
    out_ref[5:8, :] = jnp.zeros((3, ROWS), jnp.float32)


def cross_kernel(item_ref, len_ref, here_ref, sums_ref, q_ref, k_ref, v_ref, qg_ref, kg_ref, out_ref):
    count = len_ref[item_ref[here_ref[0]]]
    q_factor = by_rows(sums_ref[2:3, :])
    k_factor = [by_rows(sums_ref[3:4, :]), by_rows(sums_ref[4:5, :])]
    live = prefix_live((ROWS, 2 * ROWS), count)
    for head in range(q_ref.shape[1] // HD):
        cols = slice(head * HD, (head + 1) * HD)
        q = (q_ref[:, cols].astype(jnp.float32) * q_factor * qg_ref[:, cols]).astype(jnp.bfloat16)
        keys = [
            (
                k_ref[h * ROWS : (h + 1) * ROWS, cols].astype(jnp.float32)
                * k_factor[h]
                * kg_ref[:, cols]
            ).astype(jnp.bfloat16)
            for h in range(2)
        ]
        k = jnp.concatenate(keys, axis=0)
        s = lax.dot_general(q, k, (((1,), (1,)), ((), ())), preferred_element_type=jnp.float32)
        s = jnp.where(live, s * SCALE, NEG)
        w = jnp.exp(s - jnp.max(s, axis=1, keepdims=True))
        total = jnp.sum(w, axis=1, keepdims=True)
        o = jnp.dot(w.astype(jnp.bfloat16), v_ref[:, cols], preferred_element_type=jnp.float32)
        out_ref[:, cols] = o / total


def self_kernel(
    item_ref,
    count_ref,
    here_ref,
    sums_ref,
    q0_ref,
    q1_ref,
    b0,
    b1,
    b2,
    b3,
    b4,
    b5,
    b6,
    qg_ref,
    kg_ref,
    cos_ref,
    sin_ref,
    out0_ref,
    out1_ref,
    keys,
    values,
    queries,
    scores,
):
    blocks = (b0, b1, b2, b3, b4, b5, b6)
    heads = q0_ref.shape[1] // HD
    here = here_ref[0]
    core = lax.rem(here, 2)
    left = here - core
    base = left - 6
    tiles = item_ref.shape[0]
    even = lax.rem(lax.broadcasted_iota(jnp.int32, (ROWS, HD), 1), 2) == 0

    def extent(tile):
        item = item_ref[tile]
        before = jnp.int32(0)
        after = jnp.int32(0)
        for d in range(1, SPAN):
            lower = item_ref[jnp.maximum(tile - d, 0)] == item
            upper = item_ref[jnp.minimum(tile + d, tiles - 1)] == item
            before += jnp.where(jnp.logical_and(lower, tile - d >= 0), 1, 0)
            after += jnp.where(jnp.logical_and(upper, tile + d < tiles), 1, 0)
        return tile - before, tile + after

    first_a, last_a = extent(left)
    first_b, last_b = extent(left + 1)

    def turn(ref, rows, factor, gain_ref, start, dest, slot):
        cosine = cos_ref[pl.ds(start, ROWS), :]
        sine = sin_ref[pl.ds(start, ROWS), :]
        for head in range(heads):
            cols = slice(head * HD, (head + 1) * HD)
            x = ref[rows, cols].astype(jnp.float32) * factor * gain_ref[:, cols]
            dest[slot, :, cols] = rotated(x, cosine, sine, even).astype(jnp.bfloat16)

    for w in range(14):
        tile = base + w
        parity = w % 2

        @pl.when(jnp.logical_and(tile >= first_a, tile <= last_b))
        def _(w=w, tile=tile, parity=parity):
            first = jnp.where(tile <= last_a, first_a, first_b)
            start = pl.multiple_of((tile - first) * ROWS, ROWS)
            slot = jnp.where(core == parity, 0, 1)
            row = pl.multiple_of(slot * 2 * ROWS, 2 * ROWS)
            block = blocks[w // 2]
            factor = by_rows(sums_ref[pl.ds(2 * (w // 2) + slot, 1), :])
            turn(block, pl.ds(row, ROWS), factor, kg_ref, start, keys, w)
            values[w] = block[pl.ds(row + ROWS, ROWS), :]

    for which, (q_ref, out_ref) in enumerate(((q0_ref, out0_ref), (q1_ref, out1_ref))):
        is_a = core == which
        tile = jnp.where(is_a, left, left + 1)
        first = jnp.where(is_a, first_a, first_b)
        last = jnp.where(is_a, last_a, last_b)
        factor = by_rows(sums_ref[14 + which : 15 + which, :])
        start = pl.multiple_of((tile - first) * ROWS, ROWS)
        turn(q_ref, slice(None), factor, qg_ref, start, queries, 0)
        low, high = first - base, last - base + 1

        def score(w, tops):
            live = prefix_live((ROWS, ROWS), count_ref[base + w])
            found = []
            for head in range(heads):
                cols = slice(head * HD, (head + 1) * HD)
                s = lax.dot_general(
                    queries[0, :, cols],
                    keys[w, :, cols],
                    (((1,), (1,)), ((), ())),
                    preferred_element_type=jnp.float32,
                )
                s = jnp.where(live, s * SCALE, NEG)
                scores[w - low, :, cols] = s
                found.append(jnp.maximum(tops[head], s))
            return tuple(found)

        empty = jnp.full((ROWS, ROWS), NEG, jnp.float32)
        tops = lax.fori_loop(low, high, score, (empty,) * heads)
        tops = [jnp.max(t, axis=1, keepdims=True) for t in tops]

        def mix(w, carry):
            mixed, totals = [], []
            for head in range(heads):
                cols = slice(head * HD, (head + 1) * HD)
                weight = jnp.exp(scores[w - low, :, cols] - tops[head])
                totals.append(carry[1][head] + weight)
                mixed.append(
                    carry[0][head]
                    + jnp.dot(
                        weight.astype(jnp.bfloat16),
                        values[w, :, cols],
                        preferred_element_type=jnp.float32,
                    )
                )
            return tuple(mixed), tuple(totals)

        zero = jnp.zeros((ROWS, ROWS), jnp.float32)
        mixed, totals = lax.fori_loop(low, high, mix, ((zero,) * heads, (zero,) * heads))
        for head in range(heads):
            cols = slice(head * HD, (head + 1) * HD)
            out_ref[:, cols] = mixed[head] / jnp.sum(totals[head], axis=1, keepdims=True)


def join_kernel(here_ref, own_ref, other_ref, text_ref, out_ref):
    core = lax.rem(here_ref[0], 2)
    width = own_ref.shape[1]
    mine = pl.multiple_of(core * width, HD)
    theirs = pl.multiple_of((1 - core) * width, HD)
    out_ref[:, pl.ds(mine, width)] = (own_ref[...] + text_ref[:, pl.ds(mine, width)]).astype(
        jnp.bfloat16
    )
    out_ref[:, pl.ds(theirs, width)] = (other_ref[...] + text_ref[:, pl.ds(theirs, width)]).astype(
        jnp.bfloat16
    )


def call(kernel, out_shape, specs, scratch=(), flops=1000000, limit=40):
    return pl.pallas_call(
        kernel,
        out_shape=out_shape,
        in_specs=specs,
        out_specs=jax.tree.map(lambda _: pl.BlockSpec(memory_space=pltpu.VMEM), out_shape),
        scratch_shapes=list(scratch),
        compiler_params=pltpu.CompilerParams(vmem_limit_bytes=limit << 20),
        cost_estimate=pl.CostEstimate(flops=flops, bytes_accessed=4000000, transcendentals=0),
    )


def per_device(
    self_query,
    self_key,
    self_value,
    cross_query,
    text_key,
    text_value,
    query_gain,
    key_gain,
    cross_gain,
    text_gain,
    tile_item,
    row_count,
    text_len,
):
    smem = pl.BlockSpec(memory_space=pltpu.SMEM)
    vmem = pl.BlockSpec(memory_space=pltpu.VMEM)
    f32 = jnp.float32
    width = self_query.shape[1]
    half = width // 2
    here = lax.axis_index("tile").astype(jnp.int32)
    core = lax.rem(here, 2)
    where = here.reshape(1)

    stacked = jnp.concatenate([self_key, self_value, self_query], axis=0)
    mine = lax.dynamic_slice_in_dim(stacked, core * half, half, 1)
    theirs = lax.dynamic_slice_in_dim(stacked, (1 - core) * half, half, 1)
    got = swapped(theirs)
    block = jnp.concatenate([mine[: 2 * ROWS], got[: 2 * ROWS]], axis=0)
    from_left = shifted(block, 2)
    from_right = shifted(block, -2)
    from_left3 = shifted(block, 6)
    from_right3 = shifted(block, -6)

    sums = call(
        sums_kernel, jax.ShapeDtypeStruct((8, ROWS), f32), [vmem] * 4
    )(self_query, self_key, cross_query, text_key)
    sums = lax.psum(sums, "head")

    from_left2 = shifted(from_left, 2)
    from_right2 = shifted(from_right, -2)

    both = jnp.stack([sums[:2], swapped(sums[:2])])
    k_sums = both[:, 1]
    left_sums = shifted(k_sums, 2)
    right_sums = shifted(k_sums, -2)
    left_far = shifted(jnp.concatenate([left_sums, k_sums]), 4)
    right_far = shifted(jnp.concatenate([k_sums, right_sums]), -4)
    all_sums = jnp.concatenate([left_far, left_sums, k_sums, right_sums, right_far, both[:, 0]])

    text_out = call(
        cross_kernel, jax.ShapeDtypeStruct((ROWS, width), f32), [smem] * 3 + [vmem] * 6, flops=400000000
    )(
        tile_item,
        text_len,
        where,
        sums,
        cross_query,
        text_key,
        text_value,
        cross_gain[None, :],
        text_gain[None, :],
    )

    cosine, sine = rope_tables()
    my_gain = lax.dynamic_slice_in_dim(jnp.stack([query_gain, key_gain]), core * half, half, 1)
    own, other = call(
        self_kernel,
        (jax.ShapeDtypeStruct((ROWS, half), f32),) * 2,
        [smem] * 3 + [vmem] * 14,
        scratch=[
            pltpu.VMEM((14, ROWS, half), jnp.bfloat16),
            pltpu.VMEM((14, ROWS, half), jnp.bfloat16),
            pltpu.VMEM((1, ROWS, half), jnp.bfloat16),
            pltpu.VMEM((SPAN, ROWS, half), f32),
        ],
        flops=600000000,
    )(
        tile_item,
        row_count,
        where,
        all_sums,
        mine[2 * ROWS :],
        got[2 * ROWS :],
        from_left3,
        from_left2,
        from_left,
        block,
        from_right,
        from_right2,
        from_right3,
        my_gain[0:1],
        my_gain[1:2],
        jnp.asarray(cosine),
        jnp.asarray(sine),
    )
    rest = swapped(other)
    return call(
        join_kernel, jax.ShapeDtypeStruct((ROWS, width), jnp.bfloat16), [smem] + [vmem] * 3
    )(where, own, rest, text_out)


def solution(mesh):
    spread = P("tile", "head")
    in_specs = (spread,) * 6 + (P("head"),) * 4 + (P(),) * 3
    return jax.shard_map(
        per_device, mesh=mesh, in_specs=in_specs, out_specs=spread, check_vma=False
    )
```

```python
import functools
import math

import jax
import jax.numpy as jnp
import numpy as np
from jax import lax
from jax.experimental import pallas as pl
from jax.experimental.pallas import tpu as pltpu
from jax.sharding import PartitionSpec as P

D = 5120
HD = 128
HGT = 30
WID = 52
SPAN = 7
ROWS = 128
EPSILON = 1e-06
SCALE = 1.0 / math.sqrt(HD)
NEG = -1e30


def rope_tables():
    spatial = HD // 6
    temporal = HD // 2 - 2 * spatial
    positions = np.arange(SPAN * ROWS)

    def freq(amount):
        exponent = np.arange(amount, dtype=np.float64) * 2.0 / (2 * amount)
        return (1.0 / 10000.0**exponent).astype(np.float32)

    def part(values, amount):
        return values.astype(np.float32)[:, None] * freq(amount)[None, :]

    angle = np.concatenate(
        [
            part(positions // (HGT * WID), temporal),
            part(positions // WID % HGT, spatial),
            part(positions % WID, spatial),
        ],
        axis=1,
    ).astype(np.float64)
    cosine = np.repeat(np.cos(angle), 2, axis=1).astype(np.float32)
    sine = np.stack([-np.sin(angle), np.sin(angle)], axis=2)
    return cosine, sine.reshape(SPAN * ROWS, HD).astype(np.float32)


def shifted(value, by):
    peers = lax.axis_size("tile")
    return lax.ppermute(
        value, "tile", [(i, i + by) for i in range(peers) if 0 <= i + by < peers]
    )


def swapped(value):
    peers = lax.axis_size("tile")
    return lax.ppermute(value, "tile", [(i, i ^ 1) for i in range(peers)])


def by_rows(total_row):
    factor = lax.rsqrt(total_row / D + EPSILON)
    return jnp.transpose(jnp.broadcast_to(factor, (ROWS, ROWS)))


def rotated(normal, cosine, sine, even):
    partner = jnp.where(even, pltpu.roll(normal, HD - 1, 1), pltpu.roll(normal, 1, 1))
    return normal * cosine + partner * sine


def prefix_live(shape, count):
    return lax.broadcasted_iota(jnp.int32, shape, 1) < count


def pack_kernel(here_ref, q_ref, k_ref, v_ref, c_ref, t_ref, mine_ref, theirs_ref, sums_ref):
    def total(ref, first):
        rows = None
        for head in range(ref.shape[1] // HD):
            x = ref[first : first + ROWS, head * HD : (head + 1) * HD].astype(jnp.float32)
            rows = x * x if rows is None else rows + x * x
        return jnp.sum(jnp.transpose(rows), axis=0, keepdims=True)

    sums_ref[0:1, :] = total(q_ref, 0)
    sums_ref[1:2, :] = total(k_ref, 0)
    sums_ref[2:3, :] = total(c_ref, 0)
    sums_ref[3:4, :] = total(t_ref, 0)
    sums_ref[4:5, :] = total(t_ref, ROWS)
    sums_ref[5:8, :] = jnp.zeros((3, ROWS), jnp.float32)
    core = lax.rem(here_ref[0], 2)
    half = mine_ref.shape[1]
    for index, ref in enumerate((k_ref, v_ref, q_ref)):
        rows = slice(index * ROWS, (index + 1) * ROWS)
        low, high = ref[:, :half], ref[:, half:]
        mine_ref[rows, :] = jnp.where(core == 0, low, high)
        theirs_ref[rows, :] = jnp.where(core == 0, high, low)


def cross_kernel(item_ref, len_ref, here_ref, sums_ref, q_ref, k_ref, v_ref, qg_ref, kg_ref, out_ref):
    count = len_ref[item_ref[here_ref[0]]]
    q_factor = by_rows(sums_ref[2:3, :])
    k_factor = [by_rows(sums_ref[3:4, :]), by_rows(sums_ref[4:5, :])]
    live = prefix_live((ROWS, 2 * ROWS), count)
    for head in range(q_ref.shape[1] // HD):
        cols = slice(head * HD, (head + 1) * HD)
        q = (q_ref[:, cols].astype(jnp.float32) * q_factor * qg_ref[:, cols]).astype(jnp.bfloat16)
        keys = [
            (
                k_ref[h * ROWS : (h + 1) * ROWS, cols].astype(jnp.float32)
                * k_factor[h]
                * kg_ref[:, cols]
            ).astype(jnp.bfloat16)
            for h in range(2)
        ]
        k = jnp.concatenate(keys, axis=0)
        s = lax.dot_general(q, k, (((1,), (1,)), ((), ())), preferred_element_type=jnp.float32)
        s = jnp.where(live, s * SCALE, NEG)
        w = jnp.exp(s - jnp.max(s, axis=1, keepdims=True))
        total = jnp.sum(w, axis=1, keepdims=True)
        o = jnp.dot(w.astype(jnp.bfloat16), v_ref[:, cols], preferred_element_type=jnp.float32)
        out_ref[:, cols] = o / total


def extent(item_ref, tile):
    tiles = item_ref.shape[0]
    item = item_ref[tile]
    before = jnp.int32(0)
    after = jnp.int32(0)
    for d in range(1, SPAN):
        lower = item_ref[jnp.maximum(tile - d, 0)] == item
        upper = item_ref[jnp.minimum(tile + d, tiles - 1)] == item
        before += jnp.where(jnp.logical_and(lower, tile - d >= 0), 1, 0)
        after += jnp.where(jnp.logical_and(upper, tile + d < tiles), 1, 0)
    return tile - before, tile + after


def turn(ref, rows, factor, gain_ref, cos_ref, sin_ref, start, dest_ref, slot):
    even = lax.rem(lax.broadcasted_iota(jnp.int32, (ROWS, HD), 1), 2) == 0
    cosine = cos_ref[pl.ds(start, ROWS), :]
    sine = sin_ref[pl.ds(start, ROWS), :]
    for head in range(ref.shape[1] // HD):
        cols = slice(head * HD, (head + 1) * HD)
        x = ref[rows, cols].astype(jnp.float32) * factor * gain_ref[:, cols]
        dest_ref[slot, :, cols] = rotated(x, cosine, sine, even).astype(jnp.bfloat16)


def keys_kernel(chips, item_ref, here_ref, sums_ref, gain_ref, cos_ref, sin_ref, *rest):
    blocks, keys_ref = rest[:-1], rest[-1]
    here = here_ref[0]
    core = lax.rem(here, 2)
    left = here - core
    first_a, last_a = extent(item_ref, left)
    first_b, last_b = extent(item_ref, left + 1)
    for index, (chip, block) in enumerate(zip(chips, blocks)):
        for parity in range(2):
            tile = left + 2 * chip + parity

            @pl.when(jnp.logical_and(tile >= first_a, tile <= last_b))
            def _(index=index, parity=parity, tile=tile, block=block):
                first = jnp.where(tile <= last_a, first_a, first_b)
                start = pl.multiple_of((tile - first) * ROWS, ROWS)
                slot = jnp.where(core == parity, 0, 1)
                row = pl.multiple_of(slot * 2 * ROWS, 2 * ROWS)
                factor = by_rows(sums_ref[pl.ds(2 * index + slot, 1), :])
                rows = pl.ds(row, ROWS)
                turn(block, rows, factor, gain_ref, cos_ref, sin_ref, start, keys_ref, 2 * index + parity)


def attend_kernel(
    other,
    item_ref,
    count_ref,
    here_ref,
    sums_ref,
    q_ref,
    near_ref,
    far_ref,
    b0,
    b1,
    b2,
    b3,
    b4,
    b5,
    b6,
    gain_ref,
    cos_ref,
    sin_ref,
    out_ref,
    keys,
    values,
    queries,
    scores,
):
    blocks = (b0, b1, b2, b3, b4, b5, b6)
    heads = q_ref.shape[1] // HD
    here = here_ref[0]
    core = lax.rem(here, 2)
    left = here - core
    base = left - 6
    tile = left + (1 - core if other else core)
    first, last = extent(item_ref, tile)
    factor = by_rows(sums_ref[0:1, :])
    start = pl.multiple_of((tile - first) * ROWS, ROWS)
    turn(q_ref, slice(None), factor, gain_ref, cos_ref, sin_ref, start, queries, 0)
    low, high = first - base, last - base + 1

    for w in range(14):

        @pl.when(jnp.logical_and(w >= low, w < high))
        def _(w=w):
            chip, parity = w // 2, w % 2
            slot = jnp.where(core == parity, 0, 1)
            row = pl.multiple_of(slot * 2 * ROWS + ROWS, ROWS)
            values[w] = blocks[chip][pl.ds(row, ROWS), :]
            keys[w] = near_ref[w - 4] if chip in (2, 3, 4) else far_ref[w if chip < 2 else w - 6]

    def score(w, tops):
        live = prefix_live((ROWS, ROWS), count_ref[base + w])
        found = []
        for head in range(heads):
            cols = slice(head * HD, (head + 1) * HD)
            s = lax.dot_general(
                queries[0, :, cols],
                keys[w, :, cols],
                (((1,), (1,)), ((), ())),
                preferred_element_type=jnp.float32,
            )
            s = jnp.where(live, s * SCALE, NEG)
            scores[w - low, :, cols] = s
            found.append(jnp.maximum(tops[head], s))
        return tuple(found)

    empty = jnp.full((ROWS, ROWS), NEG, jnp.float32)
    tops = lax.fori_loop(low, high, score, (empty,) * heads)
    tops = [jnp.max(t, axis=1, keepdims=True) for t in tops]

    def mix(w, carry):
        mixed, totals = [], []
        for head in range(heads):
            cols = slice(head * HD, (head + 1) * HD)
            weight = jnp.exp(scores[w - low, :, cols] - tops[head])
            totals.append(carry[1][head] + weight)
            mixed.append(
                carry[0][head]
                + jnp.dot(
                    weight.astype(jnp.bfloat16),
                    values[w, :, cols],
                    preferred_element_type=jnp.float32,
                )
            )
        return tuple(mixed), tuple(totals)

    zero = jnp.zeros((ROWS, ROWS), jnp.float32)
    mixed, totals = lax.fori_loop(low, high, mix, ((zero,) * heads, (zero,) * heads))
    for head in range(heads):
        cols = slice(head * HD, (head + 1) * HD)
        out_ref[:, cols] = mixed[head] / jnp.sum(totals[head], axis=1, keepdims=True)


def join_kernel(here_ref, own_ref, other_ref, text_ref, out_ref):
    core = lax.rem(here_ref[0], 2)
    width = own_ref.shape[1]
    mine = pl.multiple_of(core * width, HD)
    theirs = pl.multiple_of((1 - core) * width, HD)
    out_ref[:, pl.ds(mine, width)] = (own_ref[...] + text_ref[:, pl.ds(mine, width)]).astype(
        jnp.bfloat16
    )
    out_ref[:, pl.ds(theirs, width)] = (other_ref[...] + text_ref[:, pl.ds(theirs, width)]).astype(
        jnp.bfloat16
    )


def call(kernel, out_shape, specs, scratch=(), flops=1000000, limit=40):
    return pl.pallas_call(
        kernel,
        out_shape=out_shape,
        in_specs=specs,
        out_specs=jax.tree.map(lambda _: pl.BlockSpec(memory_space=pltpu.VMEM), out_shape),
        scratch_shapes=list(scratch),
        compiler_params=pltpu.CompilerParams(vmem_limit_bytes=limit << 20),
        cost_estimate=pl.CostEstimate(flops=flops, bytes_accessed=4000000, transcendentals=0),
    )


def per_device(
    self_query,
    self_key,
    self_value,
    cross_query,
    text_key,
    text_value,
    query_gain,
    key_gain,
    cross_gain,
    text_gain,
    tile_item,
    row_count,
    text_len,
):
    smem = pl.BlockSpec(memory_space=pltpu.SMEM)
    vmem = pl.BlockSpec(memory_space=pltpu.VMEM)
    f32 = jnp.float32
    width = self_query.shape[1]
    half = width // 2
    here = lax.axis_index("tile").astype(jnp.int32)
    core = lax.rem(here, 2)
    where = here.reshape(1)

    mine, theirs, sums = call(
        pack_kernel,
        (
            jax.ShapeDtypeStruct((3 * ROWS, half), jnp.bfloat16),
            jax.ShapeDtypeStruct((3 * ROWS, half), jnp.bfloat16),
            jax.ShapeDtypeStruct((8, ROWS), f32),
        ),
        [smem] + [vmem] * 5,
    )(where, self_query, self_key, self_value, cross_query, text_key)
    got = swapped(theirs)
    sums = jnp.concatenate([sums[:5], swapped(sums[:2]), sums[7:]])
    block = jnp.concatenate([mine[: 2 * ROWS], got[: 2 * ROWS]], axis=0)
    from_left = shifted(block, 2)
    from_right = shifted(block, -2)
    from_left3 = shifted(block, 6)
    from_right3 = shifted(block, -6)

    sums = lax.psum(sums, "head")
    k_sums = jnp.concatenate([sums[1:2], sums[6:7]])
    left_sums = shifted(k_sums, 2)
    right_sums = shifted(k_sums, -2)

    from_left, from_right, from_left3, from_right3, left_sums, right_sums = lax.optimization_barrier(
        (from_left, from_right, from_left3, from_right3, left_sums, right_sums)
    )
    from_left2 = shifted(from_left, 2)
    from_right2 = shifted(from_right, -2)
    left_far = shifted(jnp.concatenate([left_sums, k_sums]), 4)
    right_far = shifted(jnp.concatenate([k_sums, right_sums]), -4)

    text_out = call(
        cross_kernel, jax.ShapeDtypeStruct((ROWS, width), f32), [smem] * 3 + [vmem] * 6, flops=400000000
    )(
        tile_item,
        text_len,
        where,
        sums,
        cross_query,
        text_key,
        text_value,
        cross_gain[None, :],
        text_gain[None, :],
    )

    cosine, sine = (jnp.asarray(t) for t in rope_tables())
    my_gain = lax.dynamic_slice_in_dim(jnp.stack([query_gain, key_gain]), core * half, half, 1)

    def turned(chips, block_sums, blocks):
        return call(
            functools.partial(keys_kernel, chips),
            jax.ShapeDtypeStruct((2 * len(chips), ROWS, half), jnp.bfloat16),
            [smem] * 2 + [vmem] * (4 + len(chips)),
            flops=200000000,
        )(tile_item, where, block_sums, my_gain[1:2], cosine, sine, *blocks)

    near = turned(
        (-1, 0, 1), jnp.concatenate([left_sums, k_sums, right_sums]), (from_left, block, from_right)
    )
    far = turned(
        (-3, -2, 2, 3),
        jnp.concatenate([left_far, right_far]),
        (from_left3, from_left2, from_right2, from_right3),
    )

    def attended(other, query, query_sums):
        return call(
            functools.partial(attend_kernel, other),
            jax.ShapeDtypeStruct((ROWS, half), f32),
            [smem] * 3 + [vmem] * 14,
            scratch=[
                pltpu.VMEM((14, ROWS, half), jnp.bfloat16),
                pltpu.VMEM((14, ROWS, half), jnp.bfloat16),
                pltpu.VMEM((1, ROWS, half), jnp.bfloat16),
                pltpu.VMEM((SPAN, ROWS, half), f32),
            ],
            flops=300000000,
        )(
            tile_item,
            row_count,
            where,
            query_sums,
            query,
            near,
            far,
            from_left3,
            from_left2,
            from_left,
            block,
            from_right,
            from_right2,
            from_right3,
            my_gain[0:1],
            cosine,
            sine,
        )

    rest = swapped(attended(True, got[2 * ROWS :], sums[5:6]))
    own = attended(False, mine[2 * ROWS :], sums[0:1])
    return call(
        join_kernel, jax.ShapeDtypeStruct((ROWS, width), jnp.bfloat16), [smem] + [vmem] * 3
    )(where, own, rest, text_out)


def solution(mesh):
    spread = P("tile", "head")
    in_specs = (spread,) * 6 + (P("head"),) * 4 + (P(),) * 3
    return jax.shard_map(
        per_device, mesh=mesh, in_specs=in_specs, out_specs=spread, check_vma=False
    )
```

```python
import functools
import math

import jax
import jax.numpy as jnp
import numpy as np
from jax import lax
from jax.experimental import pallas as pl
from jax.experimental.pallas import tpu as pltpu
from jax.sharding import PartitionSpec as P

D = 5120
HD = 128
HGT = 30
WID = 52
SPAN = 7
ROWS = 128
EPSILON = 1e-06
SCALE = 1.0 / math.sqrt(HD)
NEG = -1e30


def rope_tables():
    spatial = HD // 6
    temporal = HD // 2 - 2 * spatial
    positions = np.arange(SPAN * ROWS)

    def freq(amount):
        exponent = np.arange(amount, dtype=np.float64) * 2.0 / (2 * amount)
        return (1.0 / 10000.0**exponent).astype(np.float32)

    def part(values, amount):
        return values.astype(np.float32)[:, None] * freq(amount)[None, :]

    angle = np.concatenate(
        [
            part(positions // (HGT * WID), temporal),
            part(positions // WID % HGT, spatial),
            part(positions % WID, spatial),
        ],
        axis=1,
    ).astype(np.float64)
    cosine = np.repeat(np.cos(angle), 2, axis=1).astype(np.float32)
    sine = np.stack([-np.sin(angle), np.sin(angle)], axis=2)
    return cosine, sine.reshape(SPAN * ROWS, HD).astype(np.float32)


def shifted(value, by):
    peers = lax.axis_size("tile")
    return lax.ppermute(
        value, "tile", [(i, i + by) for i in range(peers) if 0 <= i + by < peers]
    )


def swapped(value):
    peers = lax.axis_size("tile")
    return lax.ppermute(value, "tile", [(i, i ^ 1) for i in range(peers)])


def by_rows(total_row):
    factor = lax.rsqrt(total_row / D + EPSILON)
    return jnp.transpose(jnp.broadcast_to(factor, (ROWS, ROWS)))


def rotated(normal, cosine, sine, even):
    partner = jnp.where(even, pltpu.roll(normal, HD - 1, 1), pltpu.roll(normal, 1, 1))
    return normal * cosine + partner * sine


def prefix_live(shape, count):
    return lax.broadcasted_iota(jnp.int32, shape, 1) < count


def pack_kernel(
    here_ref, q_hbm, k_hbm, v_hbm, c_hbm, t_hbm, kv_ref, theirs_ref, q_mine_ref, sums_ref,
    q_ref, k_ref, v_ref, c_ref, t_ref, arrived
):
    pairs = ((k_hbm, k_ref), (v_hbm, v_ref), (q_hbm, q_ref), (c_hbm, c_ref), (t_hbm, t_ref))
    copies = [
        pltpu.make_async_copy(source, target, arrived.at[index])
        for index, (source, target) in enumerate(pairs)
    ]
    for copy in copies:
        copy.start()
    core = lax.rem(here_ref[0], 2)
    half = theirs_ref.shape[1]

    def total(ref, first):
        rows = None
        for head in range(ref.shape[1] // HD):
            x = ref[first : first + ROWS, head * HD : (head + 1) * HD].astype(jnp.float32)
            rows = x * x if rows is None else rows + x * x
        return jnp.sum(jnp.transpose(rows), axis=0, keepdims=True)

    def split(ref, mine_ref, first, index):
        low, high = ref[:, :half], ref[:, half:]
        mine_ref[first : first + ROWS, :] = jnp.where(core == 0, low, high)
        theirs_ref[index * ROWS : (index + 1) * ROWS, :] = jnp.where(core == 0, high, low)

    sums_ref[...] = jnp.zeros((8, ROWS), jnp.float32)
    copies[0].wait()
    split(k_ref, kv_ref, 0, 0)
    sums_ref[0:1, :] = total(k_ref, 0)
    copies[1].wait()
    split(v_ref, kv_ref, ROWS, 1)
    copies[2].wait()
    split(q_ref, q_mine_ref, 0, 2)
    sums_ref[1:2, :] = total(q_ref, 0)
    copies[3].wait()
    sums_ref[2:3, :] = total(c_ref, 0)
    copies[4].wait()
    sums_ref[3:4, :] = total(t_ref, 0)
    sums_ref[4:5, :] = total(t_ref, ROWS)


def cross_kernel(item_ref, len_ref, here_ref, sums_ref, q_ref, k_ref, v_ref, qg_ref, kg_ref, out_ref):
    count = len_ref[item_ref[here_ref[0]]]
    q_factor = by_rows(sums_ref[2:3, :])
    k_factor = [by_rows(sums_ref[3:4, :]), by_rows(sums_ref[4:5, :])]
    live = prefix_live((ROWS, 2 * ROWS), count)
    for head in range(q_ref.shape[1] // HD):
        cols = slice(head * HD, (head + 1) * HD)
        q = (q_ref[:, cols].astype(jnp.float32) * q_factor * qg_ref[:, cols]).astype(jnp.bfloat16)
        keys = [
            (
                k_ref[h * ROWS : (h + 1) * ROWS, cols].astype(jnp.float32)
                * k_factor[h]
                * kg_ref[:, cols]
            ).astype(jnp.bfloat16)
            for h in range(2)
        ]
        k = jnp.concatenate(keys, axis=0)
        s = lax.dot_general(q, k, (((1,), (1,)), ((), ())), preferred_element_type=jnp.float32)
        s = jnp.where(live, s * SCALE, NEG)
        w = jnp.exp(s - jnp.max(s, axis=1, keepdims=True))
        total = jnp.sum(w, axis=1, keepdims=True)
        o = jnp.dot(w.astype(jnp.bfloat16), v_ref[:, cols], preferred_element_type=jnp.float32)
        out_ref[:, cols] = o / total


def extent(item_ref, tile):
    tiles = item_ref.shape[0]
    item = item_ref[tile]
    before = jnp.int32(0)
    after = jnp.int32(0)
    for d in range(1, SPAN):
        lower = item_ref[jnp.maximum(tile - d, 0)] == item
        upper = item_ref[jnp.minimum(tile + d, tiles - 1)] == item
        before += jnp.where(jnp.logical_and(lower, tile - d >= 0), 1, 0)
        after += jnp.where(jnp.logical_and(upper, tile + d < tiles), 1, 0)
    return tile - before, tile + after


def turn(ref, rows, factor, gain_ref, cos_ref, sin_ref, start, dest_ref, slot):
    even = lax.rem(lax.broadcasted_iota(jnp.int32, (ROWS, HD), 1), 2) == 0
    cosine = cos_ref[pl.ds(start, ROWS), :]
    sine = sin_ref[pl.ds(start, ROWS), :]
    for head in range(ref.shape[1] // HD):
        cols = slice(head * HD, (head + 1) * HD)
        x = ref[rows, cols].astype(jnp.float32) * factor * gain_ref[:, cols]
        dest_ref[slot, :, cols] = rotated(x, cosine, sine, even).astype(jnp.bfloat16)


def keys_kernel(item_ref, here_ref, gain_ref, cos_ref, sin_ref, *rest):
    blocks, keys_ref = rest[:7], rest[12]
    left_far, left_sums, own_sums, right_sums, right_far = rest[7:12]
    sums = (left_far, left_far, left_sums, own_sums, right_sums, right_far, right_far)
    starts = (0, 8, 0, 0, 0, 0, 8)
    here = here_ref[0]
    core = lax.rem(here, 2)
    left = here - core
    first_a, last_a = extent(item_ref, left)
    first_b, last_b = extent(item_ref, left + 1)
    half = keys_ref.shape[2]
    for w in range(14):
        tile = left - 6 + w

        @pl.when(jnp.logical_and(tile >= first_a, tile <= last_b))
        def _(w=w, tile=tile):
            chip, parity = w // 2, w % 2
            first = jnp.where(tile <= last_a, first_a, first_b)
            start = pl.multiple_of((tile - first) * ROWS, ROWS)
            slot = jnp.where(core == parity, 0, 1)
            row = pl.multiple_of(slot * 2 * ROWS, 2 * ROWS)
            factor = by_rows(sums[chip][pl.ds(starts[chip] + 5 * slot, 1), :])
            gains = gain_ref.at[:, pl.ds(pl.multiple_of(core * half, HD), half)]
            turn(blocks[chip], pl.ds(row, ROWS), factor, gains, cos_ref, sin_ref, start, keys_ref, w)


def attend_kernel(
    other,
    item_ref,
    count_ref,
    here_ref,
    sums_ref,
    q_ref,
    keys,
    b0,
    b1,
    b2,
    b3,
    b4,
    b5,
    b6,
    gain_ref,
    cos_ref,
    sin_ref,
    out_ref,
    values,
    queries,
    scores,
):
    blocks = (b0, b1, b2, b3, b4, b5, b6)
    half = q_ref.shape[1]
    heads = half // HD
    here = here_ref[0]
    core = lax.rem(here, 2)
    left = here - core
    base = left - 6
    tile = left + (1 - core if other else core)
    first, last = extent(item_ref, tile)
    factor = by_rows(sums_ref[6:7, :] if other else sums_ref[1:2, :])
    start = pl.multiple_of((tile - first) * ROWS, ROWS)
    rows = slice(2 * ROWS, 3 * ROWS) if other else slice(0, ROWS)
    gains = gain_ref.at[:, pl.ds(pl.multiple_of(core * half, HD), half)]
    turn(q_ref, rows, factor, gains, cos_ref, sin_ref, start, queries, 0)
    low, high = first - base, last - base + 1

    for w in range(14):

        @pl.when(jnp.logical_and(w >= low, w < high))
        def _(w=w):
            chip, parity = w // 2, w % 2
            slot = jnp.where(core == parity, 0, 1)
            row = pl.multiple_of(slot * 2 * ROWS + ROWS, ROWS)
            values[w] = blocks[chip][pl.ds(row, ROWS), :]

    def score(w, tops):
        live = prefix_live((ROWS, ROWS), count_ref[base + w])
        found = []
        for head in range(heads):
            cols = slice(head * HD, (head + 1) * HD)
            s = lax.dot_general(
                queries[0, :, cols],
                keys[w, :, cols],
                (((1,), (1,)), ((), ())),
                preferred_element_type=jnp.float32,
            )
            s = jnp.where(live, s * SCALE, NEG)
            scores[w - low, :, cols] = s
            found.append(jnp.maximum(tops[head], s))
        return tuple(found)

    empty = jnp.full((ROWS, ROWS), NEG, jnp.float32)
    tops = lax.fori_loop(low, high, score, (empty,) * heads)
    tops = [jnp.max(t, axis=1, keepdims=True) for t in tops]

    def mix(w, carry):
        mixed, totals = [], []
        for head in range(heads):
            cols = slice(head * HD, (head + 1) * HD)
            weight = jnp.exp(scores[w - low, :, cols] - tops[head])
            totals.append(carry[1][head] + weight)
            mixed.append(
                carry[0][head]
                + jnp.dot(
                    weight.astype(jnp.bfloat16),
                    values[w, :, cols],
                    preferred_element_type=jnp.float32,
                )
            )
        return tuple(mixed), tuple(totals)

    zero = jnp.zeros((ROWS, ROWS), jnp.float32)
    mixed, totals = lax.fori_loop(low, high, mix, ((zero,) * heads, (zero,) * heads))
    for head in range(heads):
        cols = slice(head * HD, (head + 1) * HD)
        out_ref[:, cols] = mixed[head] / jnp.sum(totals[head], axis=1, keepdims=True)


def join_kernel(here_ref, own_ref, other_ref, text_ref, out_ref):
    core = lax.rem(here_ref[0], 2)
    width = own_ref.shape[1]
    mine = pl.multiple_of(core * width, HD)
    theirs = pl.multiple_of((1 - core) * width, HD)
    out_ref[:, pl.ds(mine, width)] = (own_ref[...] + text_ref[:, pl.ds(mine, width)]).astype(
        jnp.bfloat16
    )
    out_ref[:, pl.ds(theirs, width)] = (other_ref[...] + text_ref[:, pl.ds(theirs, width)]).astype(
        jnp.bfloat16
    )


def call(kernel, out_shape, specs, scratch=(), flops=1000000, limit=40):
    return pl.pallas_call(
        kernel,
        out_shape=out_shape,
        in_specs=specs,
        out_specs=jax.tree.map(lambda _: pl.BlockSpec(memory_space=pltpu.VMEM), out_shape),
        scratch_shapes=list(scratch),
        compiler_params=pltpu.CompilerParams(vmem_limit_bytes=limit << 20),
        cost_estimate=pl.CostEstimate(flops=flops, bytes_accessed=4000000, transcendentals=0),
    )


def per_device(
    self_query,
    self_key,
    self_value,
    cross_query,
    text_key,
    text_value,
    query_gain,
    key_gain,
    cross_gain,
    text_gain,
    tile_item,
    row_count,
    text_len,
):
    smem = pl.BlockSpec(memory_space=pltpu.SMEM)
    vmem = pl.BlockSpec(memory_space=pltpu.VMEM)
    f32 = jnp.float32
    width = self_query.shape[1]
    half = width // 2
    here = lax.axis_index("tile").astype(jnp.int32)
    core = lax.rem(here, 2)
    where = here.reshape(1)

    bf16 = jnp.bfloat16
    hbm = pl.BlockSpec(memory_space=pltpu.HBM)
    kv, theirs, q_mine, sums = call(
        pack_kernel,
        (
            jax.ShapeDtypeStruct((2 * ROWS, half), bf16),
            jax.ShapeDtypeStruct((3 * ROWS, half), bf16),
            jax.ShapeDtypeStruct((ROWS, half), bf16),
            jax.ShapeDtypeStruct((8, ROWS), f32),
        ),
        [smem] + [hbm] * 5,
        scratch=[pltpu.VMEM((ROWS, width), bf16)] * 4
        + [pltpu.VMEM((2 * ROWS, width), bf16), pltpu.SemaphoreType.DMA((5,))],
    )(where, self_query, self_key, self_value, cross_query, text_key)
    got = swapped(theirs)
    sums = jnp.concatenate([sums[:5], swapped(sums[:2]), sums[7:]])
    block = jnp.concatenate([kv, got[: 2 * ROWS]], axis=0)
    near = [shifted(block, -2 * chip) for chip in (-1, 1, -3, 3)]

    sums = lax.psum(sums, "head")
    left_sums = shifted(sums, 2)
    right_sums = shifted(sums, -2)
    left, right, left3, right3, left_sums, right_sums = lax.optimization_barrier(
        (*near, left_sums, right_sums)
    )
    left2 = shifted(left, 2)
    right2 = shifted(right, -2)
    left_far = shifted(jnp.concatenate([left_sums, sums]), 4)
    right_far = shifted(jnp.concatenate([sums, right_sums]), -4)

    text_out = call(
        cross_kernel, jax.ShapeDtypeStruct((ROWS, width), f32), [smem] * 3 + [vmem] * 6, flops=400000000
    )(
        tile_item,
        text_len,
        where,
        sums,
        cross_query,
        text_key,
        text_value,
        cross_gain[None, :],
        text_gain[None, :],
    )
    q_gain, k_gain = query_gain[None, :], key_gain[None, :]
    left_far, right_far, text_out, q_gain, k_gain = lax.optimization_barrier(
        (left_far, right_far, text_out, q_gain, k_gain)
    )
    all_sums = [left_far, left_sums, sums, right_sums, right_far]

    cosine, sine = (jnp.asarray(t) for t in rope_tables())
    blocks = [left3, left2, left, block, right, right2, right3]
    keys = call(
        keys_kernel,
        jax.ShapeDtypeStruct((14, ROWS, half), bf16),
        [smem] * 2 + [vmem] * 15,
        flops=200000000,
    )(tile_item, where, k_gain, cosine, sine, *blocks, *all_sums)

    def attended(other, query):
        return call(
            functools.partial(attend_kernel, other),
            jax.ShapeDtypeStruct((ROWS, half), f32),
            [smem] * 3 + [vmem] * 13,
            scratch=[
                pltpu.VMEM((14, ROWS, half), bf16),
                pltpu.VMEM((1, ROWS, half), bf16),
                pltpu.VMEM((SPAN, ROWS, half), f32),
            ],
            flops=300000000,
        )(
            tile_item,
            row_count,
            where,
            sums,
            query,
            keys,
            *blocks,
            q_gain,
            cosine,
            sine,
        )

    rest = swapped(attended(True, got))
    own = attended(False, q_mine)
    return call(
        join_kernel, jax.ShapeDtypeStruct((ROWS, width), bf16), [smem] + [vmem] * 3
    )(where, own, rest, text_out)


def solution(mesh):
    spread = P("tile", "head")
    in_specs = (spread,) * 6 + (P("head"),) * 4 + (P(),) * 3
    return jax.shard_map(
        per_device, mesh=mesh, in_specs=in_specs, out_specs=spread, check_vma=False
    )
```

```python
import functools
import math

import jax
import jax.numpy as jnp
import numpy as np
from jax import lax
from jax.experimental import pallas as pl
from jax.experimental.pallas import tpu as pltpu
from jax.sharding import PartitionSpec as P

D = 5120
HD = 128
HGT = 30
WID = 52
SPAN = 7
ROWS = 128
EPSILON = 1e-06
SCALE = 1.0 / math.sqrt(HD)
NEG = -1e30
KEY_LINES = (5, 6, 7, 0, 8, 9, 10)


def rope_tables():
    spatial = HD // 6
    temporal = HD // 2 - 2 * spatial
    positions = np.arange(SPAN * ROWS)

    def freq(amount):
        exponent = np.arange(amount, dtype=np.float64) * 2.0 / (2 * amount)
        return (1.0 / 10000.0**exponent).astype(np.float32)

    def part(values, amount):
        return values.astype(np.float32)[:, None] * freq(amount)[None, :]

    angle = np.concatenate(
        [
            part(positions // (HGT * WID), temporal),
            part(positions // WID % HGT, spatial),
            part(positions % WID, spatial),
        ],
        axis=1,
    ).astype(np.float64)
    cosine = np.repeat(np.cos(angle), 2, axis=1).astype(np.float32)
    sine = np.stack([-np.sin(angle), np.sin(angle)], axis=2)
    return cosine, sine.reshape(SPAN * ROWS, HD).astype(np.float32)


def shifted(value, by):
    peers = lax.axis_size("tile")
    return lax.ppermute(
        value, "tile", [(i, i + by) for i in range(peers) if 0 <= i + by < peers]
    )


def swapped(value):
    peers = lax.axis_size("tile")
    return lax.ppermute(value, "tile", [(i, i ^ 1) for i in range(peers)])


def by_rows(total_row):
    factor = lax.rsqrt(total_row / D + EPSILON)
    return jnp.transpose(jnp.broadcast_to(factor, (ROWS, ROWS)))


def rotated(normal, cosine, sine, even):
    partner = jnp.where(even, pltpu.roll(normal, HD - 1, 1), pltpu.roll(normal, 1, 1))
    return normal * cosine + partner * sine


def prefix_live(shape, count):
    return lax.broadcasted_iota(jnp.int32, shape, 1) < count


def pack_kernel(
    here_ref, q_hbm, k_hbm, v_hbm, c_hbm, t_hbm, kv_ref, theirs_ref, q_mine_ref, sums_ref,
    q_ref, k_ref, v_ref, c_ref, t_ref, arrived
):
    pairs = ((k_hbm, k_ref), (v_hbm, v_ref), (q_hbm, q_ref), (c_hbm, c_ref), (t_hbm, t_ref))
    copies = [
        pltpu.make_async_copy(source, target, arrived.at[index])
        for index, (source, target) in enumerate(pairs)
    ]
    for copy in copies:
        copy.start()
    core = lax.rem(here_ref[0], 2)
    half = theirs_ref.shape[1]

    def total(ref, first):
        rows = None
        for head in range(ref.shape[1] // HD):
            x = ref[first : first + ROWS, head * HD : (head + 1) * HD].astype(jnp.float32)
            rows = x * x if rows is None else rows + x * x
        return jnp.sum(jnp.transpose(rows), axis=0, keepdims=True)

    def split(ref, mine_ref, first, index):
        low, high = ref[:, :half], ref[:, half:]
        mine_ref[first : first + ROWS, :] = jnp.where(core == 0, low, high)
        theirs_ref[index * ROWS : (index + 1) * ROWS, :] = jnp.where(core == 0, high, low)

    sums_ref[...] = jnp.zeros((8, ROWS), jnp.float32)
    copies[0].wait()
    split(k_ref, kv_ref, 0, 0)
    sums_ref[0:1, :] = total(k_ref, 0)
    copies[1].wait()
    split(v_ref, kv_ref, ROWS, 1)
    copies[2].wait()
    split(q_ref, q_mine_ref, 0, 2)
    sums_ref[1:2, :] = total(q_ref, 0)
    copies[3].wait()
    sums_ref[2:3, :] = total(c_ref, 0)
    copies[4].wait()
    sums_ref[3:4, :] = total(t_ref, 0)
    sums_ref[4:5, :] = total(t_ref, ROWS)


def table_kernel(own_ref, left_ref, right_ref, left_far_ref, right_far_ref, out_ref):
    out_ref[0:8, :] = own_ref[...]
    out_ref[8:16, :] = jnp.zeros((8, ROWS), jnp.float32)
    out_ref[5:6, :] = left_far_ref[0:1, :]
    out_ref[6:7, :] = left_far_ref[8:9, :]
    out_ref[7:8, :] = left_ref[0:1, :]
    out_ref[8:9, :] = right_ref[0:1, :]
    out_ref[9:10, :] = right_far_ref[0:1, :]
    out_ref[10:11, :] = right_far_ref[8:9, :]


def cross_kernel(item_ref, len_ref, here_ref, sums_ref, q_ref, k_ref, v_ref, qg_ref, kg_ref, out_ref):
    count = len_ref[item_ref[here_ref[0]]]
    q_factor = by_rows(sums_ref[2:3, :])
    k_factor = [by_rows(sums_ref[3:4, :]), by_rows(sums_ref[4:5, :])]
    live = prefix_live((ROWS, 2 * ROWS), count)
    for head in range(q_ref.shape[1] // HD):
        cols = slice(head * HD, (head + 1) * HD)
        q = (q_ref[:, cols].astype(jnp.float32) * q_factor * qg_ref[:, cols]).astype(jnp.bfloat16)
        keys = [
            (
                k_ref[h * ROWS : (h + 1) * ROWS, cols].astype(jnp.float32)
                * k_factor[h]
                * kg_ref[:, cols]
            ).astype(jnp.bfloat16)
            for h in range(2)
        ]
        k = jnp.concatenate(keys, axis=0)
        s = lax.dot_general(q, k, (((1,), (1,)), ((), ())), preferred_element_type=jnp.float32)
        s = jnp.where(live, s * SCALE, NEG)
        w = jnp.exp(s - jnp.max(s, axis=1, keepdims=True))
        total = jnp.sum(w, axis=1, keepdims=True)
        o = jnp.dot(w.astype(jnp.bfloat16), v_ref[:, cols], preferred_element_type=jnp.float32)
        out_ref[:, cols] = o / total


def extent(item_ref, tile):
    tiles = item_ref.shape[0]
    item = item_ref[tile]
    before = jnp.int32(0)
    after = jnp.int32(0)
    for d in range(1, SPAN):
        lower = item_ref[jnp.maximum(tile - d, 0)] == item
        upper = item_ref[jnp.minimum(tile + d, tiles - 1)] == item
        before += jnp.where(jnp.logical_and(lower, tile - d >= 0), 1, 0)
        after += jnp.where(jnp.logical_and(upper, tile + d < tiles), 1, 0)
    return tile - before, tile + after


def turn(ref, rows, factor, gain_ref, cos_ref, sin_ref, start, dest_ref, slot):
    even = lax.rem(lax.broadcasted_iota(jnp.int32, (ROWS, HD), 1), 2) == 0
    cosine = cos_ref[pl.ds(start, ROWS), :]
    sine = sin_ref[pl.ds(start, ROWS), :]
    for head in range(ref.shape[1] // HD):
        cols = slice(head * HD, (head + 1) * HD)
        x = ref[rows, cols].astype(jnp.float32) * factor * gain_ref[:, cols]
        dest_ref[slot, :, cols] = rotated(x, cosine, sine, even).astype(jnp.bfloat16)


def keys_kernel(item_ref, here_ref, gain_ref, cos_ref, sin_ref, *rest):
    blocks, own_ref, mate_ref, keys_ref = rest[:7], rest[7], rest[8], rest[9]
    here = here_ref[0]
    core = lax.rem(here, 2)
    left = here - core
    first_a, last_a = extent(item_ref, left)
    first_b, last_b = extent(item_ref, left + 1)
    half = keys_ref.shape[2]
    for w in range(14):
        tile = left - 6 + w

        @pl.when(jnp.logical_and(tile >= first_a, tile <= last_b))
        def _(w=w, tile=tile):
            chip, parity = w // 2, w % 2
            first = jnp.where(tile <= last_a, first_a, first_b)
            start = pl.multiple_of((tile - first) * ROWS, ROWS)
            slot = jnp.where(core == parity, 0, 1)
            row = pl.multiple_of(slot * 2 * ROWS, 2 * ROWS)
            line = KEY_LINES[chip]
            sums = jnp.where(core == parity, own_ref[line : line + 1, :], mate_ref[line : line + 1, :])
            factor = by_rows(sums)
            gains = gain_ref.at[:, pl.ds(pl.multiple_of(core * half, HD), half)]
            turn(blocks[chip], pl.ds(row, ROWS), factor, gains, cos_ref, sin_ref, start, keys_ref, w)


def attend_kernel(
    other,
    item_ref,
    count_ref,
    here_ref,
    sums_ref,
    q_ref,
    keys,
    b0,
    b1,
    b2,
    b3,
    b4,
    b5,
    b6,
    gain_ref,
    cos_ref,
    sin_ref,
    out_ref,
    values,
    queries,
    scores,
):
    blocks = (b0, b1, b2, b3, b4, b5, b6)
    half = q_ref.shape[1]
    heads = half // HD
    here = here_ref[0]
    core = lax.rem(here, 2)
    left = here - core
    base = left - 6
    tile = left + (1 - core if other else core)
    first, last = extent(item_ref, tile)
    factor = by_rows(sums_ref[1:2, :])
    start = pl.multiple_of((tile - first) * ROWS, ROWS)
    rows = slice(2 * ROWS, 3 * ROWS) if other else slice(0, ROWS)
    gains = gain_ref.at[:, pl.ds(pl.multiple_of(core * half, HD), half)]
    turn(q_ref, rows, factor, gains, cos_ref, sin_ref, start, queries, 0)
    low, high = first - base, last - base + 1

    for w in range(14):

        @pl.when(jnp.logical_and(w >= low, w < high))
        def _(w=w):
            chip, parity = w // 2, w % 2
            slot = jnp.where(core == parity, 0, 1)
            row = pl.multiple_of(slot * 2 * ROWS + ROWS, ROWS)
            values[w] = blocks[chip][pl.ds(row, ROWS), :]

    def score(w, tops):
        live = prefix_live((ROWS, ROWS), count_ref[base + w])
        found = []
        for head in range(heads):
            cols = slice(head * HD, (head + 1) * HD)
            s = lax.dot_general(
                queries[0, :, cols],
                keys[w, :, cols],
                (((1,), (1,)), ((), ())),
                preferred_element_type=jnp.float32,
            )
            s = jnp.where(live, s * SCALE, NEG)
            scores[w - low, :, cols] = s
            found.append(jnp.maximum(tops[head], s))
        return tuple(found)

    empty = jnp.full((ROWS, ROWS), NEG, jnp.float32)
    tops = lax.fori_loop(low, high, score, (empty,) * heads)
    tops = [jnp.max(t, axis=1, keepdims=True) for t in tops]

    def mix(w, carry):
        mixed, totals = [], []
        for head in range(heads):
            cols = slice(head * HD, (head + 1) * HD)
            weight = jnp.exp(scores[w - low, :, cols] - tops[head])
            totals.append(carry[1][head] + weight)
            mixed.append(
                carry[0][head]
                + jnp.dot(
                    weight.astype(jnp.bfloat16),
                    values[w, :, cols],
                    preferred_element_type=jnp.float32,
                )
            )
        return tuple(mixed), tuple(totals)

    zero = jnp.zeros((ROWS, ROWS), jnp.float32)
    mixed, totals = lax.fori_loop(low, high, mix, ((zero,) * heads, (zero,) * heads))
    for head in range(heads):
        cols = slice(head * HD, (head + 1) * HD)
        out_ref[:, cols] = mixed[head] / jnp.sum(totals[head], axis=1, keepdims=True)


def join_kernel(here_ref, own_ref, other_ref, text_ref, out_ref):
    core = lax.rem(here_ref[0], 2)
    width = own_ref.shape[1]
    mine = pl.multiple_of(core * width, HD)
    theirs = pl.multiple_of((1 - core) * width, HD)
    out_ref[:, pl.ds(mine, width)] = (own_ref[...] + text_ref[:, pl.ds(mine, width)]).astype(
        jnp.bfloat16
    )
    out_ref[:, pl.ds(theirs, width)] = (other_ref[...] + text_ref[:, pl.ds(theirs, width)]).astype(
        jnp.bfloat16
    )


def call(kernel, out_shape, specs, scratch=(), flops=1000000, limit=40):
    return pl.pallas_call(
        kernel,
        out_shape=out_shape,
        in_specs=specs,
        out_specs=jax.tree.map(lambda _: pl.BlockSpec(memory_space=pltpu.VMEM), out_shape),
        scratch_shapes=list(scratch),
        compiler_params=pltpu.CompilerParams(vmem_limit_bytes=limit << 20),
        cost_estimate=pl.CostEstimate(flops=flops, bytes_accessed=4000000, transcendentals=0),
    )


def per_device(
    self_query,
    self_key,
    self_value,
    cross_query,
    text_key,
    text_value,
    query_gain,
    key_gain,
    cross_gain,
    text_gain,
    tile_item,
    row_count,
    text_len,
):
    smem = pl.BlockSpec(memory_space=pltpu.SMEM)
    vmem = pl.BlockSpec(memory_space=pltpu.VMEM)
    f32 = jnp.float32
    width = self_query.shape[1]
    half = width // 2
    here = lax.axis_index("tile").astype(jnp.int32)
    core = lax.rem(here, 2)
    where = here.reshape(1)

    bf16 = jnp.bfloat16
    hbm = pl.BlockSpec(memory_space=pltpu.HBM)
    kv, theirs, q_mine, sums = call(
        pack_kernel,
        (
            jax.ShapeDtypeStruct((2 * ROWS, half), bf16),
            jax.ShapeDtypeStruct((3 * ROWS, half), bf16),
            jax.ShapeDtypeStruct((ROWS, half), bf16),
            jax.ShapeDtypeStruct((8, ROWS), f32),
        ),
        [smem] + [hbm] * 5,
        scratch=[pltpu.VMEM((ROWS, width), bf16)] * 4
        + [pltpu.VMEM((2 * ROWS, width), bf16), pltpu.SemaphoreType.DMA((5,))],
        limit=60,
    )(where, self_query, self_key, self_value, cross_query, text_key)
    got = swapped(theirs)
    left_sums = shifted(sums, 2)
    right_sums = shifted(sums, -2)
    block = jnp.concatenate([kv, got[: 2 * ROWS]], axis=0)
    left_far = shifted(jnp.concatenate([left_sums, sums]), 4)
    right_far = shifted(jnp.concatenate([sums, right_sums]), -4)
    table = call(table_kernel, jax.ShapeDtypeStruct((16, ROWS), f32), [vmem] * 5)(
        sums, left_sums, right_sums, left_far, right_far
    )
    block, table = lax.optimization_barrier((block, table))
    near = [shifted(block, -2 * chip) for chip in (-1, 1, -3, 3)]
    sums = lax.psum(table, "head")
    left, right, left3, right3, sums = lax.optimization_barrier((*near, sums))
    left2 = shifted(left, 2)
    right2 = shifted(right, -2)
    mate_sums = swapped(sums)

    text_out = call(
        cross_kernel, jax.ShapeDtypeStruct((ROWS, width), f32), [smem] * 3 + [vmem] * 6, flops=400000000
    )(
        tile_item,
        text_len,
        where,
        sums,
        cross_query,
        text_key,
        text_value,
        cross_gain[None, :],
        text_gain[None, :],
    )
    q_gain, k_gain = query_gain[None, :], key_gain[None, :]
    mate_sums, text_out, q_gain, k_gain = lax.optimization_barrier(
        (mate_sums, text_out, q_gain, k_gain)
    )

    cosine, sine = (jnp.asarray(t) for t in rope_tables())
    blocks = [left3, left2, left, block, right, right2, right3]
    keys = call(
        keys_kernel,
        jax.ShapeDtypeStruct((14, ROWS, half), bf16),
        [smem] * 2 + [vmem] * 12,
        flops=200000000,
    )(tile_item, where, k_gain, cosine, sine, *blocks, sums, mate_sums)

    def attended(other, query, query_sums):
        return call(
            functools.partial(attend_kernel, other),
            jax.ShapeDtypeStruct((ROWS, half), f32),
            [smem] * 3 + [vmem] * 13,
            scratch=[
                pltpu.VMEM((14, ROWS, half), bf16),
                pltpu.VMEM((1, ROWS, half), bf16),
                pltpu.VMEM((SPAN, ROWS, half), f32),
            ],
            flops=300000000,
        )(
            tile_item,
            row_count,
            where,
            query_sums,
            query,
            keys,
            *blocks,
            q_gain,
            cosine,
            sine,
        )

    rest = swapped(attended(True, got, mate_sums))
    own = attended(False, q_mine, sums)
    return call(
        join_kernel, jax.ShapeDtypeStruct((ROWS, width), bf16), [smem] + [vmem] * 3
    )(where, own, rest, text_out)


def solution(mesh):
    spread = P("tile", "head")
    in_specs = (spread,) * 6 + (P("head"),) * 4 + (P(),) * 3
    return jax.shard_map(
        per_device, mesh=mesh, in_specs=in_specs, out_specs=spread, check_vma=False
    )
```

```python
import functools
import math

import jax
import jax.numpy as jnp
import numpy as np
from jax import lax
from jax.experimental import pallas as pl
from jax.experimental.pallas import tpu as pltpu
from jax.sharding import PartitionSpec as P

D = 5120
HD = 128
HGT = 30
WID = 52
SPAN = 7
ROWS = 128
EPSILON = 1e-06
SCALE = 1.0 / math.sqrt(HD)
NEG = -1e30
KEY_LINES = (5, 6, 7, 0, 8, 9, 10)


def rope_tables():
    spatial = HD // 6
    temporal = HD // 2 - 2 * spatial
    positions = np.arange(SPAN * ROWS)

    def freq(amount):
        exponent = np.arange(amount, dtype=np.float64) * 2.0 / (2 * amount)
        return (1.0 / 10000.0**exponent).astype(np.float32)

    def part(values, amount):
        return values.astype(np.float32)[:, None] * freq(amount)[None, :]

    angle = np.concatenate(
        [
            part(positions // (HGT * WID), temporal),
            part(positions // WID % HGT, spatial),
            part(positions % WID, spatial),
        ],
        axis=1,
    ).astype(np.float64)
    cosine = np.repeat(np.cos(angle), 2, axis=1).astype(np.float32)
    sine = np.stack([-np.sin(angle), np.sin(angle)], axis=2)
    return cosine, sine.reshape(SPAN * ROWS, HD).astype(np.float32)


def shifted(value, by):
    peers = lax.axis_size("tile")
    return lax.ppermute(
        value, "tile", [(i, i + by) for i in range(peers) if 0 <= i + by < peers]
    )


def swapped(value):
    peers = lax.axis_size("tile")
    return lax.ppermute(value, "tile", [(i, i ^ 1) for i in range(peers)])


def by_rows(total_row):
    factor = lax.rsqrt(total_row / D + EPSILON)
    return jnp.transpose(jnp.broadcast_to(factor, (ROWS, ROWS)))


def rotated(normal, cosine, sine, even):
    partner = jnp.where(even, pltpu.roll(normal, HD - 1, 1), pltpu.roll(normal, 1, 1))
    return normal * cosine + partner * sine


def prefix_live(shape, count):
    return lax.broadcasted_iota(jnp.int32, shape, 1) < count


def pack_kernel(
    here_ref, q_hbm, k_hbm, v_hbm, c_hbm, t_hbm, kv_ref, theirs_ref, q_mine_ref, sums_ref,
    q_ref, k_ref, v_ref, c_ref, t_ref, arrived
):
    pairs = ((k_hbm, k_ref), (v_hbm, v_ref), (q_hbm, q_ref), (c_hbm, c_ref), (t_hbm, t_ref))
    copies = [
        pltpu.make_async_copy(source, target, arrived.at[index])
        for index, (source, target) in enumerate(pairs)
    ]
    for copy in copies:
        copy.start()
    core = lax.rem(here_ref[0], 2)
    half = theirs_ref.shape[1]

    def total(ref, first):
        rows = None
        for head in range(ref.shape[1] // HD):
            x = ref[first : first + ROWS, head * HD : (head + 1) * HD].astype(jnp.float32)
            rows = x * x if rows is None else rows + x * x
        return jnp.sum(jnp.transpose(rows), axis=0, keepdims=True)

    def split(ref, mine_ref, first, index):
        low, high = ref[:, :half], ref[:, half:]
        mine_ref[first : first + ROWS, :] = jnp.where(core == 0, low, high)
        theirs_ref[index * ROWS : (index + 1) * ROWS, :] = jnp.where(core == 0, high, low)

    sums_ref[...] = jnp.zeros((8, ROWS), jnp.float32)
    copies[0].wait()
    split(k_ref, kv_ref, 0, 0)
    sums_ref[0:1, :] = total(k_ref, 0)
    copies[1].wait()
    split(v_ref, kv_ref, ROWS, 1)
    copies[2].wait()
    split(q_ref, q_mine_ref, 0, 2)
    sums_ref[1:2, :] = total(q_ref, 0)
    copies[3].wait()
    sums_ref[2:3, :] = total(c_ref, 0)
    copies[4].wait()
    sums_ref[3:4, :] = total(t_ref, 0)
    sums_ref[4:5, :] = total(t_ref, ROWS)


def table_kernel(own_ref, left_ref, right_ref, left_far_ref, right_far_ref, out_ref):
    out_ref[0:8, :] = own_ref[...]
    out_ref[8:16, :] = jnp.zeros((8, ROWS), jnp.float32)
    out_ref[5:6, :] = left_far_ref[0:1, :]
    out_ref[6:7, :] = left_far_ref[8:9, :]
    out_ref[7:8, :] = left_ref[0:1, :]
    out_ref[8:9, :] = right_ref[0:1, :]
    out_ref[9:10, :] = right_far_ref[0:1, :]
    out_ref[10:11, :] = right_far_ref[8:9, :]


def cross_kernel(item_ref, len_ref, here_ref, sums_ref, q_ref, k_ref, v_ref, qg_ref, kg_ref, out_ref):
    count = len_ref[item_ref[here_ref[0]]]
    q_factor = by_rows(sums_ref[2:3, :])
    k_factor = [by_rows(sums_ref[3:4, :]), by_rows(sums_ref[4:5, :])]
    live = prefix_live((ROWS, 2 * ROWS), count)
    for head in range(q_ref.shape[1] // HD):
        cols = slice(head * HD, (head + 1) * HD)
        q = (q_ref[:, cols].astype(jnp.float32) * q_factor * qg_ref[:, cols]).astype(jnp.bfloat16)
        keys = [
            (
                k_ref[h * ROWS : (h + 1) * ROWS, cols].astype(jnp.float32)
                * k_factor[h]
                * kg_ref[:, cols]
            ).astype(jnp.bfloat16)
            for h in range(2)
        ]
        k = jnp.concatenate(keys, axis=0)
        s = lax.dot_general(q, k, (((1,), (1,)), ((), ())), preferred_element_type=jnp.float32)
        s = jnp.where(live, s * SCALE, NEG)
        w = jnp.exp(s - jnp.max(s, axis=1, keepdims=True))
        total = jnp.sum(w, axis=1, keepdims=True)
        o = jnp.dot(w.astype(jnp.bfloat16), v_ref[:, cols], preferred_element_type=jnp.float32)
        out_ref[:, cols] = o / total


def extent(item_ref, tile):
    tiles = item_ref.shape[0]
    item = item_ref[tile]
    before = jnp.int32(0)
    after = jnp.int32(0)
    for d in range(1, SPAN):
        lower = item_ref[jnp.maximum(tile - d, 0)] == item
        upper = item_ref[jnp.minimum(tile + d, tiles - 1)] == item
        before += jnp.where(jnp.logical_and(lower, tile - d >= 0), 1, 0)
        after += jnp.where(jnp.logical_and(upper, tile + d < tiles), 1, 0)
    return tile - before, tile + after


def turn(ref, rows, factor, gain_ref, cos_ref, sin_ref, start, dest_ref, goal):
    even = lax.rem(lax.broadcasted_iota(jnp.int32, (ROWS, HD), 1), 2) == 0
    cosine = cos_ref[pl.ds(start, ROWS), :]
    sine = sin_ref[pl.ds(start, ROWS), :]
    for head in range(ref.shape[1] // HD):
        cols = slice(head * HD, (head + 1) * HD)
        x = ref[rows, cols].astype(jnp.float32) * factor * gain_ref[:, cols]
        dest_ref[goal, cols] = rotated(x, cosine, sine, even).astype(jnp.bfloat16)


def gather_block(chip, block, core, left, bounds, sums, gains, tables, keys_ref, values_ref, place):
    first_a, last_a, first_b, last_b = bounds
    cos_ref, sin_ref = tables
    own_ref, mate_ref = sums
    line = KEY_LINES[chip + SPAN // 2]
    for parity in range(2):
        tile = left + 2 * chip + parity
        slot = jnp.where(core == parity, 0, 1)
        key_rows = pl.ds(pl.multiple_of(slot * 2 * ROWS, 2 * ROWS), ROWS)
        value_rows = pl.ds(pl.multiple_of(slot * 2 * ROWS + ROWS, ROWS), ROWS)
        goal = slice((place + parity) * ROWS, (place + parity + 1) * ROWS)
        values_ref[goal, :] = block[value_rows, :]

        @pl.when(jnp.logical_and(tile >= first_a, tile <= last_b))
        def _(parity=parity, tile=tile, key_rows=key_rows, goal=goal):
            first = jnp.where(tile <= last_a, first_a, first_b)
            start = pl.multiple_of((tile - first) * ROWS, ROWS)
            total = jnp.where(core == parity, own_ref[line : line + 1, :], mate_ref[line : line + 1, :])
            turn(block, key_rows, by_rows(total), gains, cos_ref, sin_ref, start, keys_ref, goal)


def near_kernel(chips, item_ref, here_ref, *rest):
    own_ref, mate_ref, k_gain_ref, q_gain_ref, cos_ref, sin_ref, q_own_ref, q_mate_ref = rest[:8]
    blocks = rest[8 : 8 + len(chips)]
    keys_ref, values_ref, own_turned_ref, mate_turned_ref = rest[8 + len(chips) :]
    core = lax.rem(here_ref[0], 2)
    left = here_ref[0] - core
    half = keys_ref.shape[1]
    bounds = (*extent(item_ref, left), *extent(item_ref, left + 1))
    part = pl.ds(pl.multiple_of(core * half, HD), half)
    k_gains, q_gains = k_gain_ref.at[:, part], q_gain_ref.at[:, part]
    for which, (source, rows, sums, goal) in enumerate(
        (
            (q_own_ref, slice(0, ROWS), own_ref, own_turned_ref),
            (q_mate_ref, slice(2 * ROWS, 3 * ROWS), mate_ref, mate_turned_ref),
        )
    ):
        is_a = core == which
        first = jnp.where(is_a, bounds[0], bounds[2])
        tile = jnp.where(is_a, left, left + 1)
        start = pl.multiple_of((tile - first) * ROWS, ROWS)
        factor = by_rows(sums[1:2, :])
        turn(source, rows, factor, q_gains, cos_ref, sin_ref, start, goal, slice(None))
    for index, (chip, block) in enumerate(zip(chips, blocks)):
        gather_block(
            chip, block, core, left, bounds, (own_ref, mate_ref), k_gains, (cos_ref, sin_ref),
            keys_ref, values_ref, 2 * index,
        )


def attend(mate, item_ref, count_ref, here_ref, q_ref, keys_ref, values_ref, out_ref):
    core = lax.rem(here_ref[0], 2)
    left = here_ref[0] - core
    tile = left + (1 - core if mate else core)
    first, last = extent(item_ref, tile)
    window = pl.ds(pl.multiple_of((first - left + 6) * ROWS, ROWS), SPAN * ROWS)
    tiles = item_ref.shape[0]
    lanes = lax.broadcasted_iota(jnp.int32, (ROWS, ROWS), 1)
    live = []
    for slot in range(SPAN):
        count = count_ref[jnp.minimum(first + slot, tiles - 1)]
        live.append(lanes < jnp.where(first + slot <= last, count, 0))
    for head in range(q_ref.shape[1] // HD):
        cols = slice(head * HD, (head + 1) * HD)
        s = lax.dot_general(
            q_ref[:, cols],
            keys_ref[window, cols],
            (((1,), (1,)), ((), ())),
            preferred_element_type=jnp.float32,
        )
        parts = [
            jnp.where(live[slot], s[:, slot * ROWS : (slot + 1) * ROWS] * SCALE, NEG)
            for slot in range(SPAN)
        ]
        top = functools.reduce(jnp.maximum, parts)
        top = jnp.max(top, axis=1, keepdims=True)
        parts = [jnp.exp(part - top) for part in parts]
        total = jnp.sum(functools.reduce(jnp.add, parts), axis=1, keepdims=True)
        weights = jnp.concatenate([part.astype(jnp.bfloat16) for part in parts], axis=1)
        mixed = jnp.dot(weights, values_ref[window, cols], preferred_element_type=jnp.float32)
        out_ref[:, cols] = mixed / total


def far_kernel(near_chips, far_chips, item_ref, count_ref, here_ref, *rest):
    own_ref, mate_ref, k_gain_ref, cos_ref, sin_ref, q_ref, near_keys_ref, near_values_ref = rest[:8]
    blocks = rest[8 : 8 + len(far_chips)]
    out_ref, keys_ref, values_ref = rest[8 + len(far_chips) :]
    core = lax.rem(here_ref[0], 2)
    left = here_ref[0] - core
    half = keys_ref.shape[1]
    bounds = (*extent(item_ref, left), *extent(item_ref, left + 1))
    k_gains = k_gain_ref.at[:, pl.ds(pl.multiple_of(core * half, HD), half)]
    for index, chip in enumerate(near_chips):
        source = slice(2 * index * ROWS, 2 * (index + 1) * ROWS)
        goal = slice(2 * (chip + 3) * ROWS, 2 * (chip + 4) * ROWS)
        keys_ref[goal, :] = near_keys_ref[source, :]
        values_ref[goal, :] = near_values_ref[source, :]
    for chip, block in zip(far_chips, blocks):
        gather_block(
            chip, block, core, left, bounds, (own_ref, mate_ref), k_gains, (cos_ref, sin_ref),
            keys_ref, values_ref, 2 * (chip + 3),
        )
    attend(True, item_ref, count_ref, here_ref, q_ref, keys_ref, values_ref, out_ref)


def join_kernel(here_ref, own_ref, other_ref, text_ref, out_ref):
    core = lax.rem(here_ref[0], 2)
    width = own_ref.shape[1]
    mine = pl.multiple_of(core * width, HD)
    theirs = pl.multiple_of((1 - core) * width, HD)
    out_ref[:, pl.ds(mine, width)] = (own_ref[...] + text_ref[:, pl.ds(mine, width)]).astype(
        jnp.bfloat16
    )
    out_ref[:, pl.ds(theirs, width)] = (other_ref[...] + text_ref[:, pl.ds(theirs, width)]).astype(
        jnp.bfloat16
    )


def call(kernel, out_shape, specs, scratch=(), flops=1000000, limit=40):
    return pl.pallas_call(
        kernel,
        out_shape=out_shape,
        in_specs=specs,
        out_specs=jax.tree.map(lambda _: pl.BlockSpec(memory_space=pltpu.VMEM), out_shape),
        scratch_shapes=list(scratch),
        compiler_params=pltpu.CompilerParams(vmem_limit_bytes=limit << 20),
        cost_estimate=pl.CostEstimate(flops=flops, bytes_accessed=4000000, transcendentals=0),
    )


def per_device(
    self_query,
    self_key,
    self_value,
    cross_query,
    text_key,
    text_value,
    query_gain,
    key_gain,
    cross_gain,
    text_gain,
    tile_item,
    row_count,
    text_len,
):
    smem = pl.BlockSpec(memory_space=pltpu.SMEM)
    vmem = pl.BlockSpec(memory_space=pltpu.VMEM)
    f32 = jnp.float32
    width = self_query.shape[1]
    half = width // 2
    here = lax.axis_index("tile").astype(jnp.int32)
    core = lax.rem(here, 2)
    where = here.reshape(1)

    bf16 = jnp.bfloat16
    hbm = pl.BlockSpec(memory_space=pltpu.HBM)
    kv, theirs, q_mine, sums = call(
        pack_kernel,
        (
            jax.ShapeDtypeStruct((2 * ROWS, half), bf16),
            jax.ShapeDtypeStruct((3 * ROWS, half), bf16),
            jax.ShapeDtypeStruct((ROWS, half), bf16),
            jax.ShapeDtypeStruct((8, ROWS), f32),
        ),
        [smem] + [hbm] * 5,
        scratch=[pltpu.VMEM((ROWS, width), bf16)] * 4
        + [pltpu.VMEM((2 * ROWS, width), bf16), pltpu.SemaphoreType.DMA((5,))],
        limit=60,
    )(where, self_query, self_key, self_value, cross_query, text_key)
    got = swapped(theirs)
    left_sums = shifted(sums, 2)
    right_sums = shifted(sums, -2)
    block = jnp.concatenate([kv, got[: 2 * ROWS]], axis=0)
    left_far = shifted(jnp.concatenate([left_sums, sums]), 4)
    right_far = shifted(jnp.concatenate([sums, right_sums]), -4)
    table = call(table_kernel, jax.ShapeDtypeStruct((16, ROWS), f32), [vmem] * 5)(
        sums, left_sums, right_sums, left_far, right_far
    )
    block, table = lax.optimization_barrier((block, table))
    near = [shifted(block, -2 * chip) for chip in (-1, 1, -3, 3)]
    sums = lax.psum(table, "head")
    left, right, left3, right3, sums = lax.optimization_barrier((*near, sums))
    left2 = shifted(left, 2)
    right2 = shifted(right, -2)
    mate_sums = swapped(sums)

    text_out = call(
        cross_kernel, jax.ShapeDtypeStruct((ROWS, width), f32), [smem] * 3 + [vmem] * 6, flops=400000000
    )(
        tile_item,
        text_len,
        where,
        sums,
        cross_query,
        text_key,
        text_value,
        cross_gain[None, :],
        text_gain[None, :],
    )
    q_gain, k_gain = query_gain[None, :], key_gain[None, :]
    mate_sums, text_out, q_gain, k_gain = lax.optimization_barrier(
        (mate_sums, text_out, q_gain, k_gain)
    )

    cosine, sine = (jnp.asarray(t) for t in rope_tables())
    arrived = {-3: left3, -2: left2, -1: left, 0: block, 1: right, 2: right2, 3: right3}
    near_chips, far_chips = (-3, -1, 0, 1, 3), (-2, 2)
    near_rows = 2 * len(near_chips) * ROWS
    near_keys, near_values, q_own, q_mate = call(
        functools.partial(near_kernel, near_chips),
        (jax.ShapeDtypeStruct((near_rows, half), bf16),) * 2
        + (jax.ShapeDtypeStruct((ROWS, half), bf16),) * 2,
        [smem] * 2 + [vmem] * (8 + len(near_chips)),
        flops=200000000,
    )(
        tile_item,
        where,
        sums,
        mate_sums,
        k_gain,
        q_gain,
        cosine,
        sine,
        q_mine,
        got,
        *[arrived[chip] for chip in near_chips],
    )
    window = jax.ShapeDtypeStruct((14 * ROWS, half), bf16)
    mate_out, keys, values = call(
        functools.partial(far_kernel, near_chips, far_chips),
        (jax.ShapeDtypeStruct((ROWS, half), f32), window, window),
        [smem] * 3 + [vmem] * (8 + len(far_chips)),
        flops=300000000,
    )(
        tile_item,
        row_count,
        where,
        sums,
        mate_sums,
        k_gain,
        cosine,
        sine,
        q_mate,
        near_keys,
        near_values,
        *[arrived[chip] for chip in far_chips],
    )
    rest = swapped(mate_out)
    own = call(
        functools.partial(attend, False),
        jax.ShapeDtypeStruct((ROWS, half), f32),
        [smem] * 3 + [vmem] * 3,
        flops=300000000,
    )(tile_item, row_count, where, q_own, keys, values)
    return call(
        join_kernel, jax.ShapeDtypeStruct((ROWS, width), bf16), [smem] + [vmem] * 3
    )(where, own, rest, text_out)


def solution(mesh):
    spread = P("tile", "head")
    in_specs = (spread,) * 6 + (P("head"),) * 4 + (P(),) * 3
    return jax.shard_map(
        per_device, mesh=mesh, in_specs=in_specs, out_specs=spread, check_vma=False
    )
```

```python
import functools
import math

import jax
import jax.numpy as jnp
import numpy as np
from jax import lax
from jax.experimental import pallas as pl
from jax.experimental.pallas import tpu as pltpu
from jax.sharding import PartitionSpec as P

D = 5120
HD = 128
HGT = 30
WID = 52
SPAN = 7
ROWS = 128
EPSILON = 1e-06
SCALE = 1.0 / math.sqrt(HD)
NEG = -1e30
KEY_LINES = {-1: (7, 8), 0: (0, 5), 1: (9, 10)}
SPARE = 16


def rope_tables():
    spatial = HD // 6
    temporal = HD // 2 - 2 * spatial
    positions = np.arange(SPAN * ROWS)

    def freq(amount):
        exponent = np.arange(amount, dtype=np.float64) * 2.0 / (2 * amount)
        return (1.0 / 10000.0**exponent).astype(np.float32)

    def part(values, amount):
        return values.astype(np.float32)[:, None] * freq(amount)[None, :]

    angle = np.concatenate(
        [
            part(positions // (HGT * WID), temporal),
            part(positions // WID % HGT, spatial),
            part(positions % WID, spatial),
        ],
        axis=1,
    ).astype(np.float64)
    cosine = np.repeat(np.cos(angle), 2, axis=1).astype(np.float32)
    sine = np.stack([-np.sin(angle), np.sin(angle)], axis=2)
    return cosine, sine.reshape(SPAN * ROWS, HD).astype(np.float32)


def shifted(value, by, wrapped=()):
    peers = lax.axis_size("tile")
    pairs = [(i, i + by) for i in range(peers) if 0 <= i + by < peers]
    return lax.ppermute(value, "tile", pairs + [(i, (i + by) % peers) for i in wrapped])


def swapped(value):
    peers = lax.axis_size("tile")
    return lax.ppermute(value, "tile", [(i, i ^ 1) for i in range(peers)])


def by_rows(total_row):
    factor = lax.rsqrt(total_row / D + EPSILON)
    return jnp.transpose(jnp.broadcast_to(factor, (ROWS, ROWS)))


def rotated(normal, cosine, sine, even):
    partner = jnp.where(even, pltpu.roll(normal, HD - 1, 1), pltpu.roll(normal, 1, 1))
    return normal * cosine + partner * sine


def prefix_live(shape, count):
    return lax.broadcasted_iota(jnp.int32, shape, 1) < count


def pack_kernel(
    here_ref, q_hbm, k_hbm, v_hbm, c_hbm, t_hbm, kv_ref, theirs_ref, q_mine_ref, sums_ref,
    q_ref, k_ref, v_ref, c_ref, t_ref, arrived
):
    pairs = ((k_hbm, k_ref), (v_hbm, v_ref), (q_hbm, q_ref), (c_hbm, c_ref), (t_hbm, t_ref))
    copies = [
        pltpu.make_async_copy(source, target, arrived.at[index])
        for index, (source, target) in enumerate(pairs)
    ]
    for copy in copies:
        copy.start()
    core = lax.rem(here_ref[0], 2)
    half = theirs_ref.shape[1]

    def total(ref, first):
        rows = None
        for head in range(ref.shape[1] // HD):
            x = ref[first : first + ROWS, head * HD : (head + 1) * HD].astype(jnp.float32)
            rows = x * x if rows is None else rows + x * x
        return jnp.sum(jnp.transpose(rows), axis=0, keepdims=True)

    def split(ref, mine_ref, first, index):
        low, high = ref[:, :half], ref[:, half:]
        mine_ref[first : first + ROWS, :] = jnp.where(core == 0, low, high)
        theirs_ref[index * ROWS : (index + 1) * ROWS, :] = jnp.where(core == 0, high, low)

    sums_ref[...] = jnp.zeros((8, ROWS), jnp.float32)
    copies[0].wait()
    split(k_ref, kv_ref, 0, 0)
    sums_ref[0:1, :] = total(k_ref, 0)
    copies[1].wait()
    split(v_ref, kv_ref, ROWS, 1)
    copies[2].wait()
    split(q_ref, q_mine_ref, 0, 2)
    sums_ref[1:2, :] = total(q_ref, 0)
    copies[3].wait()
    sums_ref[2:3, :] = total(c_ref, 0)
    copies[4].wait()
    sums_ref[3:4, :] = total(t_ref, 0)
    sums_ref[4:5, :] = total(t_ref, ROWS)


def mate_kernel(own_ref, mate_ref, out_ref):
    out_ref[...] = own_ref[...]
    out_ref[5:7, :] = mate_ref[0:2, :]


def table_kernel(own_ref, left_ref, right_ref, out_ref):
    out_ref[0:8, :] = own_ref[...]
    out_ref[8:16, :] = jnp.zeros((8, ROWS), jnp.float32)
    out_ref[7:8, :] = left_ref[0:1, :]
    out_ref[8:9, :] = left_ref[5:6, :]
    out_ref[9:10, :] = right_ref[0:1, :]
    out_ref[10:11, :] = right_ref[5:6, :]


def pieces_kernel(sums_ref, left_ref, right_ref):
    for chip, out_ref in ((-1, left_ref), (1, right_ref)):
        out_ref[...] = jnp.zeros(out_ref.shape, jnp.bfloat16)
        rows = []
        for line in KEY_LINES[chip]:
            rest = sums_ref[line : line + 1, :]
            for _ in range(3):
                piece = rest.astype(jnp.bfloat16)
                rows.append(piece.astype(jnp.float32))
                rest = rest - rows[-1]
        rows.append(jnp.zeros((SPARE - len(rows), ROWS), jnp.float32))
        out_ref[:, 0:ROWS] = jnp.concatenate(rows, axis=0).astype(jnp.bfloat16)


def cross_kernel(item_ref, len_ref, here_ref, sums_ref, q_ref, k_ref, v_ref, qg_ref, kg_ref, out_ref):
    count = len_ref[item_ref[here_ref[0]]]
    q_factor = by_rows(sums_ref[2:3, :])
    k_factor = [by_rows(sums_ref[3:4, :]), by_rows(sums_ref[4:5, :])]
    live = prefix_live((ROWS, 2 * ROWS), count)
    for head in range(q_ref.shape[1] // HD):
        cols = slice(head * HD, (head + 1) * HD)
        q = (q_ref[:, cols].astype(jnp.float32) * q_factor * qg_ref[:, cols]).astype(jnp.bfloat16)
        keys = [
            (
                k_ref[h * ROWS : (h + 1) * ROWS, cols].astype(jnp.float32)
                * k_factor[h]
                * kg_ref[:, cols]
            ).astype(jnp.bfloat16)
            for h in range(2)
        ]
        k = jnp.concatenate(keys, axis=0)
        s = lax.dot_general(q, k, (((1,), (1,)), ((), ())), preferred_element_type=jnp.float32)
        s = jnp.where(live, s * SCALE, NEG)
        w = jnp.exp(s - jnp.max(s, axis=1, keepdims=True))
        total = jnp.sum(w, axis=1, keepdims=True)
        o = jnp.dot(w.astype(jnp.bfloat16), v_ref[:, cols], preferred_element_type=jnp.float32)
        out_ref[:, cols] = o / total


def extent(item_ref, tile):
    tiles = item_ref.shape[0]
    item = item_ref[tile]
    before = jnp.int32(0)
    after = jnp.int32(0)
    for d in range(1, SPAN):
        lower = item_ref[jnp.maximum(tile - d, 0)] == item
        upper = item_ref[jnp.minimum(tile + d, tiles - 1)] == item
        before += jnp.where(jnp.logical_and(lower, tile - d >= 0), 1, 0)
        after += jnp.where(jnp.logical_and(upper, tile + d < tiles), 1, 0)
    return tile - before, tile + after


def turn(ref, rows, factor, gain_ref, cos_ref, sin_ref, start, dest_ref, goal):
    even = lax.rem(lax.broadcasted_iota(jnp.int32, (ROWS, HD), 1), 2) == 0
    cosine = cos_ref[pl.ds(start, ROWS), :]
    sine = sin_ref[pl.ds(start, ROWS), :]
    for head in range(ref.shape[1] // HD):
        cols = slice(head * HD, (head + 1) * HD)
        x = ref[rows, cols].astype(jnp.float32) * factor * gain_ref[:, cols]
        dest_ref[goal, cols] = rotated(x, cosine, sine, even).astype(jnp.bfloat16)


def gather_block(chip, block, core, left, bounds, sums_ref, gains, tables, keys_ref, values_ref, place):
    first_a, last_a, first_b, last_b = bounds
    cos_ref, sin_ref = tables
    for parity in range(2):
        tile = left + 2 * chip + parity
        slot = jnp.where(core == parity, 0, 1)
        key_rows = pl.ds(pl.multiple_of(slot * 2 * ROWS, 2 * ROWS), ROWS)
        value_rows = pl.ds(pl.multiple_of(slot * 2 * ROWS + ROWS, ROWS), ROWS)
        goal = slice((place + parity) * ROWS, (place + parity + 1) * ROWS)
        values_ref[goal, :] = block[value_rows, :]

        @pl.when(jnp.logical_and(tile >= first_a, tile <= last_b))
        def _(parity=parity, tile=tile, key_rows=key_rows, goal=goal):
            first = jnp.where(tile <= last_a, first_a, first_b)
            start = pl.multiple_of((tile - first) * ROWS, ROWS)
            if chip in KEY_LINES:
                own, mate = (sums_ref[line : line + 1, :] for line in KEY_LINES[chip])
            else:
                spare = block[4 * ROWS : 4 * ROWS + SPARE, 0:ROWS].astype(jnp.float32)
                own, mate = (
                    spare[3 * i : 3 * i + 1] + spare[3 * i + 1 : 3 * i + 2] + spare[3 * i + 2 : 3 * i + 3]
                    for i in range(2)
                )
            total = jnp.where(core == parity, own, mate)
            turn(block, key_rows, by_rows(total), gains, cos_ref, sin_ref, start, keys_ref, goal)


def near_kernel(chips, item_ref, here_ref, *rest):
    sums_ref, k_gain_ref, q_gain_ref, cos_ref, sin_ref, q_own_ref, q_mate_ref = rest[:7]
    blocks = rest[7 : 7 + len(chips)]
    keys_ref, values_ref, own_turned_ref, mate_turned_ref = rest[7 + len(chips) :]
    core = lax.rem(here_ref[0], 2)
    left = here_ref[0] - core
    half = keys_ref.shape[1]
    bounds = (*extent(item_ref, left), *extent(item_ref, left + 1))
    part = pl.ds(pl.multiple_of(core * half, HD), half)
    k_gains, q_gains = k_gain_ref.at[:, part], q_gain_ref.at[:, part]
    for which, (source, rows, line, goal) in enumerate(
        (
            (q_own_ref, slice(0, ROWS), 1, own_turned_ref),
            (q_mate_ref, slice(2 * ROWS, 3 * ROWS), 6, mate_turned_ref),
        )
    ):
        is_a = core == which
        first = jnp.where(is_a, bounds[0], bounds[2])
        tile = jnp.where(is_a, left, left + 1)
        start = pl.multiple_of((tile - first) * ROWS, ROWS)
        factor = by_rows(sums_ref[line : line + 1, :])
        turn(source, rows, factor, q_gains, cos_ref, sin_ref, start, goal, slice(None))
    for index, (chip, block) in enumerate(zip(chips, blocks)):
        gather_block(
            chip, block, core, left, bounds, sums_ref, k_gains, (cos_ref, sin_ref),
            keys_ref, values_ref, 2 * index,
        )


def attend(mate, item_ref, count_ref, here_ref, q_ref, keys_ref, values_ref, out_ref):
    core = lax.rem(here_ref[0], 2)
    left = here_ref[0] - core
    tile = left + (1 - core if mate else core)
    first, last = extent(item_ref, tile)
    window = pl.ds(pl.multiple_of((first - left + 6) * ROWS, ROWS), SPAN * ROWS)
    tiles = item_ref.shape[0]
    lanes = lax.broadcasted_iota(jnp.int32, (ROWS, ROWS), 1)
    live = []
    for slot in range(SPAN):
        count = count_ref[jnp.minimum(first + slot, tiles - 1)]
        live.append(lanes < jnp.where(first + slot <= last, count, 0))
    for head in range(q_ref.shape[1] // HD):
        cols = slice(head * HD, (head + 1) * HD)
        s = lax.dot_general(
            q_ref[:, cols],
            keys_ref[window, cols],
            (((1,), (1,)), ((), ())),
            preferred_element_type=jnp.float32,
        )
        parts = [
            jnp.where(live[slot], s[:, slot * ROWS : (slot + 1) * ROWS] * SCALE, NEG)
            for slot in range(SPAN)
        ]
        top = functools.reduce(jnp.maximum, parts)
        top = jnp.max(top, axis=1, keepdims=True)
        parts = [jnp.exp(part - top) for part in parts]
        total = jnp.sum(functools.reduce(jnp.add, parts), axis=1, keepdims=True)
        weights = jnp.concatenate([part.astype(jnp.bfloat16) for part in parts], axis=1)
        mixed = jnp.dot(weights, values_ref[window, cols], preferred_element_type=jnp.float32)
        out_ref[:, cols] = mixed / total


def far_kernel(near_chips, far_chips, item_ref, count_ref, here_ref, *rest):
    sums_ref, k_gain_ref, cos_ref, sin_ref, q_ref, near_keys_ref, near_values_ref = rest[:7]
    blocks = rest[7 : 7 + len(far_chips)]
    out_ref, keys_ref, values_ref = rest[7 + len(far_chips) :]
    core = lax.rem(here_ref[0], 2)
    left = here_ref[0] - core
    half = keys_ref.shape[1]
    bounds = (*extent(item_ref, left), *extent(item_ref, left + 1))
    k_gains = k_gain_ref.at[:, pl.ds(pl.multiple_of(core * half, HD), half)]
    for index, chip in enumerate(near_chips):
        source = slice(2 * index * ROWS, 2 * (index + 1) * ROWS)
        goal = slice(2 * (chip + 3) * ROWS, 2 * (chip + 4) * ROWS)
        keys_ref[goal, :] = near_keys_ref[source, :]
        values_ref[goal, :] = near_values_ref[source, :]
    for chip, block in zip(far_chips, blocks):
        gather_block(
            chip, block, core, left, bounds, sums_ref, k_gains, (cos_ref, sin_ref),
            keys_ref, values_ref, 2 * (chip + 3),
        )
    attend(True, item_ref, count_ref, here_ref, q_ref, keys_ref, values_ref, out_ref)


def join_kernel(here_ref, own_ref, other_ref, text_ref, out_ref):
    core = lax.rem(here_ref[0], 2)
    width = own_ref.shape[1]
    mine = pl.multiple_of(core * width, HD)
    theirs = pl.multiple_of((1 - core) * width, HD)
    out_ref[:, pl.ds(mine, width)] = (own_ref[...] + text_ref[:, pl.ds(mine, width)]).astype(
        jnp.bfloat16
    )
    out_ref[:, pl.ds(theirs, width)] = (other_ref[...] + text_ref[:, pl.ds(theirs, width)]).astype(
        jnp.bfloat16
    )


def call(kernel, out_shape, specs, scratch=(), flops=1000000, limit=40):
    return pl.pallas_call(
        kernel,
        out_shape=out_shape,
        in_specs=specs,
        out_specs=jax.tree.map(lambda _: pl.BlockSpec(memory_space=pltpu.VMEM), out_shape),
        scratch_shapes=list(scratch),
        compiler_params=pltpu.CompilerParams(vmem_limit_bytes=limit << 20),
        cost_estimate=pl.CostEstimate(flops=flops, bytes_accessed=4000000, transcendentals=0),
    )


def per_device(
    self_query,
    self_key,
    self_value,
    cross_query,
    text_key,
    text_value,
    query_gain,
    key_gain,
    cross_gain,
    text_gain,
    tile_item,
    row_count,
    text_len,
):
    smem = pl.BlockSpec(memory_space=pltpu.SMEM)
    vmem = pl.BlockSpec(memory_space=pltpu.VMEM)
    f32 = jnp.float32
    width = self_query.shape[1]
    half = width // 2
    here = lax.axis_index("tile").astype(jnp.int32)
    core = lax.rem(here, 2)
    where = here.reshape(1)

    bf16 = jnp.bfloat16
    hbm = pl.BlockSpec(memory_space=pltpu.HBM)
    kv, theirs, q_mine, sums = call(
        pack_kernel,
        (
            jax.ShapeDtypeStruct((2 * ROWS, half), bf16),
            jax.ShapeDtypeStruct((3 * ROWS, half), bf16),
            jax.ShapeDtypeStruct((ROWS, half), bf16),
            jax.ShapeDtypeStruct((8, ROWS), f32),
        ),
        [smem] + [hbm] * 5,
        scratch=[pltpu.VMEM((ROWS, width), bf16)] * 4
        + [pltpu.VMEM((2 * ROWS, width), bf16), pltpu.SemaphoreType.DMA((5,))],
        limit=60,
    )(where, self_query, self_key, self_value, cross_query, text_key)
    got = swapped(theirs)
    peers = lax.axis_size("tile")
    low_pair, high_pair = (0, 1), (peers - 2, peers - 1)
    table = jax.ShapeDtypeStruct((8, ROWS), f32)
    sums = call(mate_kernel, table, [vmem] * 2)(sums, swapped(sums))
    block = jnp.concatenate([kv, got[: 2 * ROWS], jnp.zeros((SPARE, half), bf16)], axis=0)
    left_sums = shifted(sums, 2, high_pair)
    right_sums = shifted(sums, -2, low_pair)
    block, left_sums, right_sums = lax.optimization_barrier((block, left_sums, right_sums))
    left = shifted(block, 2, high_pair)
    right = shifted(block, -2, low_pair)
    table = jax.ShapeDtypeStruct((16, ROWS), f32)
    sums = call(table_kernel, table, [vmem] * 3)(sums, left_sums, right_sums)
    sums = lax.psum(sums, "head")
    left, right, sums = lax.optimization_barrier((left, right, sums))
    spare = jax.ShapeDtypeStruct((SPARE, half), bf16)
    left_pieces, right_pieces = call(pieces_kernel, (spare, spare), [vmem])(sums)
    left = lax.dynamic_update_slice(left, left_pieces, (4 * ROWS, 0))
    right = lax.dynamic_update_slice(right, right_pieces, (4 * ROWS, 0))
    right3 = shifted(left, -8, low_pair)
    left3 = shifted(right, 8, high_pair)
    left2 = shifted(left, 2)
    right2 = shifted(right, -2)

    text_out = call(
        cross_kernel, jax.ShapeDtypeStruct((ROWS, width), f32), [smem] * 3 + [vmem] * 6, flops=400000000
    )(
        tile_item,
        text_len,
        where,
        sums,
        cross_query,
        text_key,
        text_value,
        cross_gain[None, :],
        text_gain[None, :],
    )
    q_gain, k_gain = query_gain[None, :], key_gain[None, :]
    text_out, q_gain, k_gain = lax.optimization_barrier((text_out, q_gain, k_gain))

    cosine, sine = (jnp.asarray(t) for t in rope_tables())
    arrived = {-3: left3, -2: left2, -1: left, 0: block, 1: right, 2: right2, 3: right3}
    near_chips, far_chips = (-1, 0, 1), (-3, -2, 2, 3)
    near_rows = 2 * len(near_chips) * ROWS
    near_keys, near_values, q_own, q_mate = call(
        functools.partial(near_kernel, near_chips),
        (jax.ShapeDtypeStruct((near_rows, half), bf16),) * 2
        + (jax.ShapeDtypeStruct((ROWS, half), bf16),) * 2,
        [smem] * 2 + [vmem] * (7 + len(near_chips)),
        flops=200000000,
    )(
        tile_item,
        where,
        sums,
        k_gain,
        q_gain,
        cosine,
        sine,
        q_mine,
        got,
        *[arrived[chip] for chip in near_chips],
    )
    window = jax.ShapeDtypeStruct((14 * ROWS, half), bf16)
    mate_out, keys, values = call(
        functools.partial(far_kernel, near_chips, far_chips),
        (jax.ShapeDtypeStruct((ROWS, half), f32), window, window),
        [smem] * 3 + [vmem] * (7 + len(far_chips)),
        flops=300000000,
    )(
        tile_item,
        row_count,
        where,
        sums,
        k_gain,
        cosine,
        sine,
        q_mate,
        near_keys,
        near_values,
        *[arrived[chip] for chip in far_chips],
    )
    rest = swapped(mate_out)
    own = call(
        functools.partial(attend, False),
        jax.ShapeDtypeStruct((ROWS, half), f32),
        [smem] * 3 + [vmem] * 3,
        flops=300000000,
    )(tile_item, row_count, where, q_own, keys, values)
    return call(
        join_kernel, jax.ShapeDtypeStruct((ROWS, width), bf16), [smem] + [vmem] * 3
    )(where, own, rest, text_out)


def solution(mesh):
    spread = P("tile", "head")
    in_specs = (spread,) * 6 + (P("head"),) * 4 + (P(),) * 3
    return jax.shard_map(
        per_device, mesh=mesh, in_specs=in_specs, out_specs=spread, check_vma=False
    )
```

```python
import functools
import math

import jax
import jax.numpy as jnp
import numpy as np
from jax import lax
from jax.experimental import pallas as pl
from jax.experimental.pallas import tpu as pltpu
from jax.sharding import PartitionSpec as P

D = 5120
HD = 128
HGT = 30
WID = 52
SPAN = 7
ROWS = 128
EPSILON = 1e-06
SCALE = 1.0 / math.sqrt(HD)
NEG = -1e30
KEY_LINES = {0: (0, 1), -1: (2, 3), 1: (4, 5), -3: (8, 9), -2: (10, 11), 2: (12, 13), 3: (14, 15)}
QUERY_LINES = (6, 7)
CROSS_LINE = 16
TEXT_LINES = (17, 18)
SPARE = 16
TILE_ROWS = 2 * ROWS + SPARE


def rope_tables():
    spatial = HD // 6
    temporal = HD // 2 - 2 * spatial
    positions = np.arange(SPAN * ROWS)

    def freq(amount):
        exponent = np.arange(amount, dtype=np.float64) * 2.0 / (2 * amount)
        return (1.0 / 10000.0**exponent).astype(np.float32)

    def part(values, amount):
        return values.astype(np.float32)[:, None] * freq(amount)[None, :]

    angle = np.concatenate(
        [
            part(positions // (HGT * WID), temporal),
            part(positions // WID % HGT, spatial),
            part(positions % WID, spatial),
        ],
        axis=1,
    ).astype(np.float64)
    cosine = np.repeat(np.cos(angle), 2, axis=1).astype(np.float32)
    sine = np.stack([-np.sin(angle), np.sin(angle)], axis=2)
    return cosine, sine.reshape(SPAN * ROWS, HD).astype(np.float32)


def shifted(value, by, wrapped=()):
    peers = lax.axis_size("tile")
    pairs = [(i, i + by) for i in range(peers) if 0 <= i + by < peers]
    return lax.ppermute(value, "tile", pairs + [(i, (i + by) % peers) for i in wrapped])


def swapped(value):
    peers = lax.axis_size("tile")
    return lax.ppermute(value, "tile", [(i, i ^ 1) for i in range(peers)])


def by_rows(total_row):
    factor = lax.rsqrt(total_row / D + EPSILON)
    return jnp.transpose(jnp.broadcast_to(factor, (ROWS, ROWS)))


def rotated(normal, cosine, sine, even):
    partner = jnp.where(even, pltpu.roll(normal, HD - 1, 1), pltpu.roll(normal, 1, 1))
    return normal * cosine + partner * sine


def prefix_live(shape, count):
    return lax.broadcasted_iota(jnp.int32, shape, 1) < count


def pack_kernel(
    here_ref, q_hbm, k_hbm, v_hbm, c_hbm, t_hbm, kv_ref, theirs_ref, q_mine_ref, sums_ref,
    q_ref, k_ref, v_ref, c_ref, t_ref, arrived
):
    pairs = ((k_hbm, k_ref), (v_hbm, v_ref), (q_hbm, q_ref), (c_hbm, c_ref), (t_hbm, t_ref))
    copies = [
        pltpu.make_async_copy(source, target, arrived.at[index])
        for index, (source, target) in enumerate(pairs)
    ]
    for copy in copies:
        copy.start()
    core = lax.rem(here_ref[0], 2)
    half = theirs_ref.shape[1]

    def total(ref, first):
        rows = None
        for head in range(ref.shape[1] // HD):
            x = ref[first : first + ROWS, head * HD : (head + 1) * HD].astype(jnp.float32)
            rows = x * x if rows is None else rows + x * x
        return jnp.sum(jnp.transpose(rows), axis=0, keepdims=True)

    def split(ref, mine_ref, mine_first, first):
        low, high = ref[:, :half], ref[:, half:]
        mine_ref[mine_first : mine_first + ROWS, :] = jnp.where(core == 0, low, high)
        theirs_ref[first : first + ROWS, :] = jnp.where(core == 0, high, low)

    sums_ref[...] = jnp.zeros((8, ROWS), jnp.float32)
    copies[0].wait()
    split(k_ref, kv_ref, 0, 0)
    k_total = total(k_ref, 0)
    copies[1].wait()
    split(v_ref, kv_ref, ROWS, ROWS)
    copies[2].wait()
    split(q_ref, q_mine_ref, 0, TILE_ROWS)
    q_total = total(q_ref, 0)
    sums_ref[0:1, :] = k_total
    sums_ref[1:2, :] = q_total
    rows = []
    for rest in (k_total, q_total):
        for _ in range(3):
            rows.append(rest.astype(jnp.bfloat16).astype(jnp.float32))
            rest = rest - rows[-1]
    rows.append(jnp.zeros((SPARE - len(rows), ROWS), jnp.float32))
    spare = jnp.concatenate(rows, axis=0).astype(jnp.bfloat16)
    for ref in (kv_ref, theirs_ref):
        ref[2 * ROWS : TILE_ROWS, 0:ROWS] = spare
        ref[2 * ROWS : TILE_ROWS, ROWS:] = jnp.zeros((SPARE, half - ROWS), jnp.bfloat16)
    copies[3].wait()
    sums_ref[2:3, :] = total(c_ref, 0)
    copies[4].wait()
    sums_ref[3:4, :] = total(t_ref, 0)
    sums_ref[4:5, :] = total(t_ref, ROWS)


def pieced(spare_ref, first):
    rows = spare_ref[...].astype(jnp.float32)
    return rows[first : first + 1] + rows[first + 1 : first + 2] + rows[first + 2 : first + 3]


def close_kernel(own_ref, mate_ref, left_own_ref, left_mate_ref, right_own_ref, right_mate_ref, out_ref):
    out_ref[0:1, :] = own_ref[0:1, :]
    out_ref[1:2, :] = pieced(mate_ref, 0)
    out_ref[2:3, :] = pieced(left_own_ref, 0)
    out_ref[3:4, :] = pieced(left_mate_ref, 0)
    out_ref[4:5, :] = pieced(right_own_ref, 0)
    out_ref[5:6, :] = pieced(right_mate_ref, 0)
    out_ref[6:7, :] = own_ref[1:2, :]
    out_ref[7:8, :] = pieced(mate_ref, 3)


def table_kernel(own_ref, close_ref, left_ref, right_ref, out_ref):
    out_ref[0:8, :] = close_ref[...]
    out_ref[8:10, :] = left_ref[2:4, :]
    out_ref[10:12, :] = left_ref[0:2, :]
    out_ref[12:14, :] = right_ref[0:2, :]
    out_ref[14:16, :] = right_ref[4:6, :]
    out_ref[16:24, :] = jnp.zeros((8, ROWS), jnp.float32)
    out_ref[16:19, :] = own_ref[2:5, :]


def cross_kernel(item_ref, len_ref, here_ref, sums_ref, q_ref, k_ref, v_ref, qg_ref, kg_ref, out_ref):
    count = len_ref[item_ref[here_ref[0]]]
    q_factor = by_rows(sums_ref[CROSS_LINE : CROSS_LINE + 1, :])
    k_factor = [by_rows(sums_ref[line : line + 1, :]) for line in TEXT_LINES]
    live = prefix_live((ROWS, 2 * ROWS), count)
    for head in range(q_ref.shape[1] // HD):
        cols = slice(head * HD, (head + 1) * HD)
        q = (q_ref[:, cols].astype(jnp.float32) * q_factor * qg_ref[:, cols]).astype(jnp.bfloat16)
        keys = [
            (
                k_ref[h * ROWS : (h + 1) * ROWS, cols].astype(jnp.float32)
                * k_factor[h]
                * kg_ref[:, cols]
            ).astype(jnp.bfloat16)
            for h in range(2)
        ]
        k = jnp.concatenate(keys, axis=0)
        s = lax.dot_general(q, k, (((1,), (1,)), ((), ())), preferred_element_type=jnp.float32)
        s = jnp.where(live, s * SCALE, NEG)
        w = jnp.exp(s - jnp.max(s, axis=1, keepdims=True))
        total = jnp.sum(w, axis=1, keepdims=True)
        o = jnp.dot(w.astype(jnp.bfloat16), v_ref[:, cols], preferred_element_type=jnp.float32)
        out_ref[:, cols] = o / total


def extent(item_ref, tile):
    tiles = item_ref.shape[0]
    item = item_ref[tile]
    before = jnp.int32(0)
    after = jnp.int32(0)
    for d in range(1, SPAN):
        lower = item_ref[jnp.maximum(tile - d, 0)] == item
        upper = item_ref[jnp.minimum(tile + d, tiles - 1)] == item
        before += jnp.where(jnp.logical_and(lower, tile - d >= 0), 1, 0)
        after += jnp.where(jnp.logical_and(upper, tile + d < tiles), 1, 0)
    return tile - before, tile + after


def turn(ref, rows, factor, gain_ref, cos_ref, sin_ref, start, dest_ref, goal):
    even = lax.rem(lax.broadcasted_iota(jnp.int32, (ROWS, HD), 1), 2) == 0
    cosine = cos_ref[pl.ds(start, ROWS), :]
    sine = sin_ref[pl.ds(start, ROWS), :]
    for head in range(ref.shape[1] // HD):
        cols = slice(head * HD, (head + 1) * HD)
        x = ref[rows, cols].astype(jnp.float32) * factor * gain_ref[:, cols]
        dest_ref[goal, cols] = rotated(x, cosine, sine, even).astype(jnp.bfloat16)


def gather_block(chip, block, core, left, bounds, sums_ref, gains, tables, keys_ref, values_ref, place):
    first_a, last_a, first_b, last_b = bounds
    cos_ref, sin_ref = tables
    for parity in range(2):
        tile = left + 2 * chip + parity
        slot = jnp.where(core == parity, 0, 1)
        key_rows = pl.ds(pl.multiple_of(slot * TILE_ROWS, SPARE), ROWS)
        value_rows = pl.ds(pl.multiple_of(slot * TILE_ROWS + ROWS, SPARE), ROWS)
        goal = slice((place + parity) * ROWS, (place + parity + 1) * ROWS)
        values_ref[goal, :] = block[value_rows, :]

        @pl.when(jnp.logical_and(tile >= first_a, tile <= last_b))
        def _(parity=parity, tile=tile, key_rows=key_rows, goal=goal):
            first = jnp.where(tile <= last_a, first_a, first_b)
            start = pl.multiple_of((tile - first) * ROWS, ROWS)
            own, mate = (sums_ref[line : line + 1, :] for line in KEY_LINES[chip])
            total = jnp.where(core == parity, own, mate)
            turn(block, key_rows, by_rows(total), gains, cos_ref, sin_ref, start, keys_ref, goal)


def near_kernel(chips, item_ref, here_ref, *rest):
    sums_ref, k_gain_ref, q_gain_ref, cos_ref, sin_ref, q_own_ref, q_mate_ref = rest[:7]
    blocks = rest[7 : 7 + len(chips)]
    keys_ref, values_ref, own_turned_ref, mate_turned_ref = rest[7 + len(chips) :]
    core = lax.rem(here_ref[0], 2)
    left = here_ref[0] - core
    half = keys_ref.shape[1]
    bounds = (*extent(item_ref, left), *extent(item_ref, left + 1))
    part = pl.ds(pl.multiple_of(core * half, HD), half)
    k_gains, q_gains = k_gain_ref.at[:, part], q_gain_ref.at[:, part]
    for which, (source, rows, line, goal) in enumerate(
        (
            (q_own_ref, slice(0, ROWS), QUERY_LINES[0], own_turned_ref),
            (q_mate_ref, slice(TILE_ROWS, TILE_ROWS + ROWS), QUERY_LINES[1], mate_turned_ref),
        )
    ):
        is_a = core == which
        first = jnp.where(is_a, bounds[0], bounds[2])
        tile = jnp.where(is_a, left, left + 1)
        start = pl.multiple_of((tile - first) * ROWS, ROWS)
        factor = by_rows(sums_ref[line : line + 1, :])
        turn(source, rows, factor, q_gains, cos_ref, sin_ref, start, goal, slice(None))
    for index, (chip, block) in enumerate(zip(chips, blocks)):
        gather_block(
            chip, block, core, left, bounds, sums_ref, k_gains, (cos_ref, sin_ref),
            keys_ref, values_ref, 2 * index,
        )


def attend(mate, item_ref, count_ref, here_ref, q_ref, keys_ref, values_ref, out_ref):
    core = lax.rem(here_ref[0], 2)
    left = here_ref[0] - core
    tile = left + (1 - core if mate else core)
    first, last = extent(item_ref, tile)
    window = pl.ds(pl.multiple_of((first - left + 6) * ROWS, ROWS), SPAN * ROWS)
    tiles = item_ref.shape[0]
    lanes = lax.broadcasted_iota(jnp.int32, (ROWS, ROWS), 1)
    live = []
    for slot in range(SPAN):
        count = count_ref[jnp.minimum(first + slot, tiles - 1)]
        live.append(lanes < jnp.where(first + slot <= last, count, 0))
    for head in range(q_ref.shape[1] // HD):
        cols = slice(head * HD, (head + 1) * HD)
        s = lax.dot_general(
            q_ref[:, cols],
            keys_ref[window, cols],
            (((1,), (1,)), ((), ())),
            preferred_element_type=jnp.float32,
        )
        parts = [
            jnp.where(live[slot], s[:, slot * ROWS : (slot + 1) * ROWS] * SCALE, NEG)
            for slot in range(SPAN)
        ]
        top = functools.reduce(jnp.maximum, parts)
        top = jnp.max(top, axis=1, keepdims=True)
        parts = [jnp.exp(part - top) for part in parts]
        total = jnp.sum(functools.reduce(jnp.add, parts), axis=1, keepdims=True)
        weights = jnp.concatenate([part.astype(jnp.bfloat16) for part in parts], axis=1)
        mixed = jnp.dot(weights, values_ref[window, cols], preferred_element_type=jnp.float32)
        out_ref[:, cols] = mixed / total


def far_kernel(near_chips, far_chips, item_ref, count_ref, here_ref, *rest):
    sums_ref, k_gain_ref, cos_ref, sin_ref, q_ref, near_keys_ref, near_values_ref = rest[:7]
    blocks = rest[7 : 7 + len(far_chips)]
    out_ref, keys_ref, values_ref = rest[7 + len(far_chips) :]
    core = lax.rem(here_ref[0], 2)
    left = here_ref[0] - core
    half = keys_ref.shape[1]
    bounds = (*extent(item_ref, left), *extent(item_ref, left + 1))
    k_gains = k_gain_ref.at[:, pl.ds(pl.multiple_of(core * half, HD), half)]
    for index, chip in enumerate(near_chips):
        source = slice(2 * index * ROWS, 2 * (index + 1) * ROWS)
        goal = slice(2 * (chip + 3) * ROWS, 2 * (chip + 4) * ROWS)
        keys_ref[goal, :] = near_keys_ref[source, :]
        values_ref[goal, :] = near_values_ref[source, :]
    for chip, block in zip(far_chips, blocks):
        gather_block(
            chip, block, core, left, bounds, sums_ref, k_gains, (cos_ref, sin_ref),
            keys_ref, values_ref, 2 * (chip + 3),
        )
    attend(True, item_ref, count_ref, here_ref, q_ref, keys_ref, values_ref, out_ref)


def join_kernel(here_ref, own_ref, other_ref, text_ref, out_ref):
    core = lax.rem(here_ref[0], 2)
    width = own_ref.shape[1]
    mine = pl.multiple_of(core * width, HD)
    theirs = pl.multiple_of((1 - core) * width, HD)
    out_ref[:, pl.ds(mine, width)] = (own_ref[...] + text_ref[:, pl.ds(mine, width)]).astype(
        jnp.bfloat16
    )
    out_ref[:, pl.ds(theirs, width)] = (other_ref[...] + text_ref[:, pl.ds(theirs, width)]).astype(
        jnp.bfloat16
    )


def call(kernel, out_shape, specs, scratch=(), flops=1000000, limit=40):
    return pl.pallas_call(
        kernel,
        out_shape=out_shape,
        in_specs=specs,
        out_specs=jax.tree.map(lambda _: pl.BlockSpec(memory_space=pltpu.VMEM), out_shape),
        scratch_shapes=list(scratch),
        compiler_params=pltpu.CompilerParams(vmem_limit_bytes=limit << 20),
        cost_estimate=pl.CostEstimate(flops=flops, bytes_accessed=4000000, transcendentals=0),
    )


def per_device(
    self_query,
    self_key,
    self_value,
    cross_query,
    text_key,
    text_value,
    query_gain,
    key_gain,
    cross_gain,
    text_gain,
    tile_item,
    row_count,
    text_len,
):
    smem = pl.BlockSpec(memory_space=pltpu.SMEM)
    vmem = pl.BlockSpec(memory_space=pltpu.VMEM)
    f32 = jnp.float32
    width = self_query.shape[1]
    half = width // 2
    here = lax.axis_index("tile").astype(jnp.int32)
    core = lax.rem(here, 2)
    where = here.reshape(1)

    bf16 = jnp.bfloat16
    hbm = pl.BlockSpec(memory_space=pltpu.HBM)
    kv, theirs, q_mine, sums = call(
        pack_kernel,
        (
            jax.ShapeDtypeStruct((TILE_ROWS, half), bf16),
            jax.ShapeDtypeStruct((TILE_ROWS + ROWS, half), bf16),
            jax.ShapeDtypeStruct((ROWS, half), bf16),
            jax.ShapeDtypeStruct((8, ROWS), f32),
        ),
        [smem] + [hbm] * 5,
        scratch=[pltpu.VMEM((ROWS, width), bf16)] * 4
        + [pltpu.VMEM((2 * ROWS, width), bf16), pltpu.SemaphoreType.DMA((5,))],
        limit=60,
    )(where, self_query, self_key, self_value, cross_query, text_key)
    got = swapped(theirs)
    peers = lax.axis_size("tile")
    low_pair, high_pair = (0, 1), (peers - 2, peers - 1)
    block = jnp.concatenate([kv, got[:TILE_ROWS]], axis=0)
    left = shifted(block, 2, high_pair)
    right = shifted(block, -2, low_pair)

    def spare(tile):
        return pl.BlockSpec((SPARE, ROWS), lambda i: ((tile * TILE_ROWS + 2 * ROWS) // SPARE, 0))

    few = pl.BlockSpec((8, ROWS), lambda i: (0, 0))
    close = pl.pallas_call(
        close_kernel,
        grid=(1,),
        out_shape=jax.ShapeDtypeStruct((8, ROWS), f32),
        in_specs=[few, spare(0), spare(0), spare(1), spare(0), spare(1)],
        out_specs=few,
    )(sums, got, left, left, right, right)
    left_sums = shifted(close, 4)
    right_sums = shifted(close, -4)
    left, right, left_sums, right_sums = lax.optimization_barrier(
        (left, right, left_sums, right_sums)
    )
    right3 = shifted(left, -8, low_pair)
    left3 = shifted(right, 8, high_pair)
    left2 = shifted(left, 2)
    right2 = shifted(right, -2)
    sums = call(table_kernel, jax.ShapeDtypeStruct((24, ROWS), f32), [vmem] * 4)(
        sums, close, left_sums, right_sums
    )
    sums = lax.psum(sums, "head")

    text_out = call(
        cross_kernel, jax.ShapeDtypeStruct((ROWS, width), f32), [smem] * 3 + [vmem] * 6, flops=400000000
    )(
        tile_item,
        text_len,
        where,
        sums,
        cross_query,
        text_key,
        text_value,
        cross_gain[None, :],
        text_gain[None, :],
    )
    q_gain, k_gain = query_gain[None, :], key_gain[None, :]
    text_out, q_gain, k_gain = lax.optimization_barrier((text_out, q_gain, k_gain))

    cosine, sine = (jnp.asarray(t) for t in rope_tables())
    arrived = {-3: left3, -2: left2, -1: left, 0: block, 1: right, 2: right2, 3: right3}
    near_chips, far_chips = (-1, 0, 1), (-3, -2, 2, 3)
    near_rows = 2 * len(near_chips) * ROWS
    near_keys, near_values, q_own, q_mate = call(
        functools.partial(near_kernel, near_chips),
        (jax.ShapeDtypeStruct((near_rows, half), bf16),) * 2
        + (jax.ShapeDtypeStruct((ROWS, half), bf16),) * 2,
        [smem] * 2 + [vmem] * (7 + len(near_chips)),
        flops=200000000,
    )(
        tile_item,
        where,
        sums,
        k_gain,
        q_gain,
        cosine,
        sine,
        q_mine,
        got,
        *[arrived[chip] for chip in near_chips],
    )
    window = jax.ShapeDtypeStruct((14 * ROWS, half), bf16)
    mate_out, keys, values = call(
        functools.partial(far_kernel, near_chips, far_chips),
        (jax.ShapeDtypeStruct((ROWS, half), f32), window, window),
        [smem] * 3 + [vmem] * (7 + len(far_chips)),
        flops=300000000,
    )(
        tile_item,
        row_count,
        where,
        sums,
        k_gain,
        cosine,
        sine,
        q_mate,
        near_keys,
        near_values,
        *[arrived[chip] for chip in far_chips],
    )
    rest = swapped(mate_out)
    own = call(
        functools.partial(attend, False),
        jax.ShapeDtypeStruct((ROWS, half), f32),
        [smem] * 3 + [vmem] * 3,
        flops=300000000,
    )(tile_item, row_count, where, q_own, keys, values)
    return call(
        join_kernel, jax.ShapeDtypeStruct((ROWS, width), bf16), [smem] + [vmem] * 3
    )(where, own, rest, text_out)


def solution(mesh):
    spread = P("tile", "head")
    in_specs = (spread,) * 6 + (P("head"),) * 4 + (P(),) * 3
    return jax.shard_map(
        per_device, mesh=mesh, in_specs=in_specs, out_specs=spread, check_vma=False
    )
```

```python
import functools
import math

import jax
import jax.numpy as jnp
import numpy as np
from jax import lax
from jax.experimental import pallas as pl
from jax.experimental.pallas import tpu as pltpu
from jax.sharding import PartitionSpec as P

D = 5120
HD = 128
HGT = 30
WID = 52
SPAN = 7
ROWS = 128
EPSILON = 1e-06
SCALE = 1.0 / math.sqrt(HD)
NEG = -1e30
KEY_LINES = {-1: (7, 8), 0: (0, 5), 1: (9, 10)}
SPARE = 16


def rope_tables():
    spatial = HD // 6
    temporal = HD // 2 - 2 * spatial
    positions = np.arange(SPAN * ROWS)

    def freq(amount):
        exponent = np.arange(amount, dtype=np.float64) * 2.0 / (2 * amount)
        return (1.0 / 10000.0**exponent).astype(np.float32)

    def part(values, amount):
        return values.astype(np.float32)[:, None] * freq(amount)[None, :]

    angle = np.concatenate(
        [
            part(positions // (HGT * WID), temporal),
            part(positions // WID % HGT, spatial),
            part(positions % WID, spatial),
        ],
        axis=1,
    ).astype(np.float64)
    cosine = np.repeat(np.cos(angle), 2, axis=1).astype(np.float32)
    sine = np.stack([-np.sin(angle), np.sin(angle)], axis=2)
    return cosine, sine.reshape(SPAN * ROWS, HD).astype(np.float32)


def shifted(value, by, wrapped=()):
    peers = lax.axis_size("tile")
    pairs = [(i, i + by) for i in range(peers) if 0 <= i + by < peers]
    return lax.ppermute(value, "tile", pairs + [(i, (i + by) % peers) for i in wrapped])


def swapped(value):
    peers = lax.axis_size("tile")
    return lax.ppermute(value, "tile", [(i, i ^ 1) for i in range(peers)])


def by_rows(total_row):
    factor = lax.rsqrt(total_row / D + EPSILON)
    return jnp.transpose(jnp.broadcast_to(factor, (ROWS, ROWS)))


def rotated(normal, cosine, sine, even):
    partner = jnp.where(even, pltpu.roll(normal, HD - 1, 1), pltpu.roll(normal, 1, 1))
    return normal * cosine + partner * sine


def prefix_live(shape, count):
    return lax.broadcasted_iota(jnp.int32, shape, 1) < count


def pieces(*totals):
    rows = []
    for rest in totals:
        for _ in range(3):
            rows.append(rest.astype(jnp.bfloat16).astype(jnp.float32))
            rest = rest - rows[-1]
    rows.append(jnp.zeros((SPARE - len(rows), ROWS), jnp.float32))
    return jnp.concatenate(rows, axis=0).astype(jnp.bfloat16)


def joined(rows, first):
    return rows[first : first + 1] + rows[first + 1 : first + 2] + rows[first + 2 : first + 3]


def pack_kernel(
    here_ref, q_hbm, k_hbm, v_hbm, c_hbm, t_hbm, kv_ref, theirs_ref, q_mine_ref, sums_ref,
    q_ref, k_ref, v_ref, c_ref, t_ref, arrived
):
    pairs = ((k_hbm, k_ref), (v_hbm, v_ref), (q_hbm, q_ref), (c_hbm, c_ref), (t_hbm, t_ref))
    copies = [
        pltpu.make_async_copy(source, target, arrived.at[index])
        for index, (source, target) in enumerate(pairs)
    ]
    for copy in copies:
        copy.start()
    core = lax.rem(here_ref[0], 2)
    half = theirs_ref.shape[1]

    def total(ref, first):
        rows = None
        for head in range(ref.shape[1] // HD):
            x = ref[first : first + ROWS, head * HD : (head + 1) * HD].astype(jnp.float32)
            rows = x * x if rows is None else rows + x * x
        return jnp.sum(jnp.transpose(rows), axis=0, keepdims=True)

    def split(ref, mine_ref, first, index):
        low, high = ref[:, :half], ref[:, half:]
        mine_ref[first : first + ROWS, :] = jnp.where(core == 0, low, high)
        theirs_ref[index * ROWS : (index + 1) * ROWS, :] = jnp.where(core == 0, high, low)

    sums_ref[...] = jnp.zeros((8, ROWS), jnp.float32)
    copies[0].wait()
    split(k_ref, kv_ref, 0, 0)
    k_total = total(k_ref, 0)
    copies[1].wait()
    split(v_ref, kv_ref, ROWS, 1)
    copies[2].wait()
    split(q_ref, q_mine_ref, 0, 2)
    q_total = total(q_ref, 0)
    sums_ref[0:1, :] = k_total
    sums_ref[1:2, :] = q_total
    theirs_ref[3 * ROWS :, 0:ROWS] = pieces(k_total, q_total)
    theirs_ref[3 * ROWS :, ROWS:] = jnp.zeros((SPARE, half - ROWS), jnp.bfloat16)
    copies[3].wait()
    sums_ref[2:3, :] = total(c_ref, 0)
    copies[4].wait()
    sums_ref[3:4, :] = total(t_ref, 0)
    sums_ref[4:5, :] = total(t_ref, ROWS)


def mate_kernel(own_ref, got_ref, out_ref):
    rows = got_ref[3 * ROWS : 3 * ROWS + SPARE, 0:ROWS].astype(jnp.float32)
    out_ref[...] = own_ref[...]
    out_ref[5:6, :] = joined(rows, 0)
    out_ref[6:7, :] = joined(rows, 3)


def table_kernel(own_ref, left_ref, right_ref, out_ref):
    out_ref[0:8, :] = own_ref[...]
    out_ref[8:16, :] = jnp.zeros((8, ROWS), jnp.float32)
    out_ref[7:8, :] = left_ref[0:1, :]
    out_ref[8:9, :] = left_ref[5:6, :]
    out_ref[9:10, :] = right_ref[0:1, :]
    out_ref[10:11, :] = right_ref[5:6, :]


def pieces_kernel(sums_ref, left_ref, right_ref):
    for chip, out_ref in ((-1, left_ref), (1, right_ref)):
        out_ref[...] = jnp.zeros(out_ref.shape, jnp.bfloat16)
        out_ref[:, 0:ROWS] = pieces(*(sums_ref[line : line + 1, :] for line in KEY_LINES[chip]))


def cross_kernel(item_ref, len_ref, here_ref, sums_ref, q_ref, k_ref, v_ref, qg_ref, kg_ref, out_ref):
    count = len_ref[item_ref[here_ref[0]]]
    q_factor = by_rows(sums_ref[2:3, :])
    k_factor = [by_rows(sums_ref[3:4, :]), by_rows(sums_ref[4:5, :])]
    live = prefix_live((ROWS, 2 * ROWS), count)
    for head in range(q_ref.shape[1] // HD):
        cols = slice(head * HD, (head + 1) * HD)
        q = (q_ref[:, cols].astype(jnp.float32) * q_factor * qg_ref[:, cols]).astype(jnp.bfloat16)
        keys = [
            (
                k_ref[h * ROWS : (h + 1) * ROWS, cols].astype(jnp.float32)
                * k_factor[h]
                * kg_ref[:, cols]
            ).astype(jnp.bfloat16)
            for h in range(2)
        ]
        k = jnp.concatenate(keys, axis=0)
        s = lax.dot_general(q, k, (((1,), (1,)), ((), ())), preferred_element_type=jnp.float32)
        s = jnp.where(live, s * SCALE, NEG)
        w = jnp.exp(s - jnp.max(s, axis=1, keepdims=True))
        total = jnp.sum(w, axis=1, keepdims=True)
        o = jnp.dot(w.astype(jnp.bfloat16), v_ref[:, cols], preferred_element_type=jnp.float32)
        out_ref[:, cols] = o / total


def extent(item_ref, tile):
    tiles = item_ref.shape[0]
    item = item_ref[tile]
    before = jnp.int32(0)
    after = jnp.int32(0)
    for d in range(1, SPAN):
        lower = item_ref[jnp.maximum(tile - d, 0)] == item
        upper = item_ref[jnp.minimum(tile + d, tiles - 1)] == item
        before += jnp.where(jnp.logical_and(lower, tile - d >= 0), 1, 0)
        after += jnp.where(jnp.logical_and(upper, tile + d < tiles), 1, 0)
    return tile - before, tile + after


def turn(ref, rows, factor, gain_ref, cos_ref, sin_ref, start, dest_ref, goal):
    even = lax.rem(lax.broadcasted_iota(jnp.int32, (ROWS, HD), 1), 2) == 0
    cosine = cos_ref[pl.ds(start, ROWS), :]
    sine = sin_ref[pl.ds(start, ROWS), :]
    for head in range(ref.shape[1] // HD):
        cols = slice(head * HD, (head + 1) * HD)
        x = ref[rows, cols].astype(jnp.float32) * factor * gain_ref[:, cols]
        dest_ref[goal, cols] = rotated(x, cosine, sine, even).astype(jnp.bfloat16)


def gather_block(chip, block, core, left, bounds, sums_ref, gains, tables, keys_ref, values_ref, place):
    first_a, last_a, first_b, last_b = bounds
    cos_ref, sin_ref = tables
    for parity in range(2):
        tile = left + 2 * chip + parity
        slot = jnp.where(core == parity, 0, 1)
        key_rows = pl.ds(pl.multiple_of(slot * 2 * ROWS, 2 * ROWS), ROWS)
        value_rows = pl.ds(pl.multiple_of(slot * 2 * ROWS + ROWS, ROWS), ROWS)
        goal = slice((place + parity) * ROWS, (place + parity + 1) * ROWS)
        values_ref[goal, :] = block[value_rows, :]

        @pl.when(jnp.logical_and(tile >= first_a, tile <= last_b))
        def _(parity=parity, tile=tile, key_rows=key_rows, goal=goal):
            first = jnp.where(tile <= last_a, first_a, first_b)
            start = pl.multiple_of((tile - first) * ROWS, ROWS)
            if chip in KEY_LINES:
                own, mate = (sums_ref[line : line + 1, :] for line in KEY_LINES[chip])
            else:
                spare = block[4 * ROWS : 4 * ROWS + SPARE, 0:ROWS].astype(jnp.float32)
                own, mate = joined(spare, 0), joined(spare, 3)
            total = jnp.where(core == parity, own, mate)
            turn(block, key_rows, by_rows(total), gains, cos_ref, sin_ref, start, keys_ref, goal)


def near_kernel(chips, item_ref, here_ref, *rest):
    sums_ref, k_gain_ref, q_gain_ref, cos_ref, sin_ref, q_own_ref, q_mate_ref = rest[:7]
    blocks = rest[7 : 7 + len(chips)]
    keys_ref, values_ref, own_turned_ref, mate_turned_ref = rest[7 + len(chips) :]
    core = lax.rem(here_ref[0], 2)
    left = here_ref[0] - core
    half = keys_ref.shape[1]
    bounds = (*extent(item_ref, left), *extent(item_ref, left + 1))
    part = pl.ds(pl.multiple_of(core * half, HD), half)
    k_gains, q_gains = k_gain_ref.at[:, part], q_gain_ref.at[:, part]
    for which, (source, rows, line, goal) in enumerate(
        (
            (q_own_ref, slice(0, ROWS), 1, own_turned_ref),
            (q_mate_ref, slice(2 * ROWS, 3 * ROWS), 6, mate_turned_ref),
        )
    ):
        is_a = core == which
        first = jnp.where(is_a, bounds[0], bounds[2])
        tile = jnp.where(is_a, left, left + 1)
        start = pl.multiple_of((tile - first) * ROWS, ROWS)
        factor = by_rows(sums_ref[line : line + 1, :])
        turn(source, rows, factor, q_gains, cos_ref, sin_ref, start, goal, slice(None))
    for index, (chip, block) in enumerate(zip(chips, blocks)):
        gather_block(
            chip, block, core, left, bounds, sums_ref, k_gains, (cos_ref, sin_ref),
            keys_ref, values_ref, 2 * index,
        )


def attend(mate, item_ref, count_ref, here_ref, q_ref, keys_ref, values_ref, out_ref):
    core = lax.rem(here_ref[0], 2)
    left = here_ref[0] - core
    tile = left + (1 - core if mate else core)
    first, last = extent(item_ref, tile)
    window = pl.ds(pl.multiple_of((first - left + 6) * ROWS, ROWS), SPAN * ROWS)
    tiles = item_ref.shape[0]
    lanes = lax.broadcasted_iota(jnp.int32, (ROWS, ROWS), 1)
    live = []
    for slot in range(SPAN):
        count = count_ref[jnp.minimum(first + slot, tiles - 1)]
        live.append(lanes < jnp.where(first + slot <= last, count, 0))
    for head in range(q_ref.shape[1] // HD):
        cols = slice(head * HD, (head + 1) * HD)
        s = lax.dot_general(
            q_ref[:, cols],
            keys_ref[window, cols],
            (((1,), (1,)), ((), ())),
            preferred_element_type=jnp.float32,
        )
        parts = [
            jnp.where(live[slot], s[:, slot * ROWS : (slot + 1) * ROWS] * SCALE, NEG)
            for slot in range(SPAN)
        ]
        top = functools.reduce(jnp.maximum, parts)
        top = jnp.max(top, axis=1, keepdims=True)
        parts = [jnp.exp(part - top) for part in parts]
        total = jnp.sum(functools.reduce(jnp.add, parts), axis=1, keepdims=True)
        weights = jnp.concatenate([part.astype(jnp.bfloat16) for part in parts], axis=1)
        mixed = jnp.dot(weights, values_ref[window, cols], preferred_element_type=jnp.float32)
        out_ref[:, cols] = mixed / total


def far_kernel(near_chips, far_chips, item_ref, count_ref, here_ref, *rest):
    sums_ref, k_gain_ref, cos_ref, sin_ref, q_ref, near_keys_ref, near_values_ref = rest[:7]
    blocks = rest[7 : 7 + len(far_chips)]
    out_ref, keys_ref, values_ref = rest[7 + len(far_chips) :]
    core = lax.rem(here_ref[0], 2)
    left = here_ref[0] - core
    half = keys_ref.shape[1]
    bounds = (*extent(item_ref, left), *extent(item_ref, left + 1))
    k_gains = k_gain_ref.at[:, pl.ds(pl.multiple_of(core * half, HD), half)]
    for index, chip in enumerate(near_chips):
        source = slice(2 * index * ROWS, 2 * (index + 1) * ROWS)
        goal = slice(2 * (chip + 3) * ROWS, 2 * (chip + 4) * ROWS)
        keys_ref[goal, :] = near_keys_ref[source, :]
        values_ref[goal, :] = near_values_ref[source, :]
    for chip, block in zip(far_chips, blocks):
        gather_block(
            chip, block, core, left, bounds, sums_ref, k_gains, (cos_ref, sin_ref),
            keys_ref, values_ref, 2 * (chip + 3),
        )
    attend(True, item_ref, count_ref, here_ref, q_ref, keys_ref, values_ref, out_ref)


def join_kernel(here_ref, own_ref, other_ref, text_ref, out_ref):
    core = lax.rem(here_ref[0], 2)
    width = own_ref.shape[1]
    mine = pl.multiple_of(core * width, HD)
    theirs = pl.multiple_of((1 - core) * width, HD)
    out_ref[:, pl.ds(mine, width)] = (own_ref[...] + text_ref[:, pl.ds(mine, width)]).astype(
        jnp.bfloat16
    )
    out_ref[:, pl.ds(theirs, width)] = (other_ref[...] + text_ref[:, pl.ds(theirs, width)]).astype(
        jnp.bfloat16
    )


def call(kernel, out_shape, specs, scratch=(), flops=1000000, limit=40):
    return pl.pallas_call(
        kernel,
        out_shape=out_shape,
        in_specs=specs,
        out_specs=jax.tree.map(lambda _: pl.BlockSpec(memory_space=pltpu.VMEM), out_shape),
        scratch_shapes=list(scratch),
        compiler_params=pltpu.CompilerParams(vmem_limit_bytes=limit << 20),
        cost_estimate=pl.CostEstimate(flops=flops, bytes_accessed=4000000, transcendentals=0),
    )


def per_device(
    self_query,
    self_key,
    self_value,
    cross_query,
    text_key,
    text_value,
    query_gain,
    key_gain,
    cross_gain,
    text_gain,
    tile_item,
    row_count,
    text_len,
):
    smem = pl.BlockSpec(memory_space=pltpu.SMEM)
    vmem = pl.BlockSpec(memory_space=pltpu.VMEM)
    f32 = jnp.float32
    width = self_query.shape[1]
    half = width // 2
    here = lax.axis_index("tile").astype(jnp.int32)
    core = lax.rem(here, 2)
    where = here.reshape(1)

    bf16 = jnp.bfloat16
    hbm = pl.BlockSpec(memory_space=pltpu.HBM)
    kv, theirs, q_mine, sums = call(
        pack_kernel,
        (
            jax.ShapeDtypeStruct((2 * ROWS, half), bf16),
            jax.ShapeDtypeStruct((3 * ROWS + SPARE, half), bf16),
            jax.ShapeDtypeStruct((ROWS, half), bf16),
            jax.ShapeDtypeStruct((8, ROWS), f32),
        ),
        [smem] + [hbm] * 5,
        scratch=[pltpu.VMEM((ROWS, width), bf16)] * 4
        + [pltpu.VMEM((2 * ROWS, width), bf16), pltpu.SemaphoreType.DMA((5,))],
        limit=60,
    )(where, self_query, self_key, self_value, cross_query, text_key)
    got = swapped(theirs)
    peers = lax.axis_size("tile")
    low_pair, high_pair = (0, 1), (peers - 2, peers - 1)
    sums = call(mate_kernel, jax.ShapeDtypeStruct((8, ROWS), f32), [vmem] * 2)(sums, got)
    left_sums = shifted(sums, 2, high_pair)
    right_sums = shifted(sums, -2, low_pair)
    block = jnp.concatenate([kv, got[: 2 * ROWS], jnp.zeros((SPARE, half), bf16)], axis=0)
    block, left_sums, right_sums = lax.optimization_barrier((block, left_sums, right_sums))
    left = shifted(block, 2, high_pair)
    right = shifted(block, -2, low_pair)
    table = jax.ShapeDtypeStruct((16, ROWS), f32)
    sums = call(table_kernel, table, [vmem] * 3)(sums, left_sums, right_sums)
    sums = lax.psum(sums, "head")
    left, right, sums = lax.optimization_barrier((left, right, sums))
    spare = jax.ShapeDtypeStruct((SPARE, half), bf16)
    left_pieces, right_pieces = call(pieces_kernel, (spare, spare), [vmem])(sums)
    left = lax.dynamic_update_slice(left, left_pieces, (4 * ROWS, 0))
    right = lax.dynamic_update_slice(right, right_pieces, (4 * ROWS, 0))
    right3 = shifted(left, -8, low_pair)
    left3 = shifted(right, 8, high_pair)
    left2 = shifted(left, 2)
    right2 = shifted(right, -2)

    text_out = call(
        cross_kernel, jax.ShapeDtypeStruct((ROWS, width), f32), [smem] * 3 + [vmem] * 6, flops=400000000
    )(
        tile_item,
        text_len,
        where,
        sums,
        cross_query,
        text_key,
        text_value,
        cross_gain[None, :],
        text_gain[None, :],
    )
    q_gain, k_gain = query_gain[None, :], key_gain[None, :]
    text_out, q_gain, k_gain = lax.optimization_barrier((text_out, q_gain, k_gain))

    cosine, sine = (jnp.asarray(t) for t in rope_tables())
    arrived = {-3: left3, -2: left2, -1: left, 0: block, 1: right, 2: right2, 3: right3}
    near_chips, far_chips = (-1, 0, 1), (-3, -2, 2, 3)
    near_rows = 2 * len(near_chips) * ROWS
    near_keys, near_values, q_own, q_mate = call(
        functools.partial(near_kernel, near_chips),
        (jax.ShapeDtypeStruct((near_rows, half), bf16),) * 2
        + (jax.ShapeDtypeStruct((ROWS, half), bf16),) * 2,
        [smem] * 2 + [vmem] * (7 + len(near_chips)),
        flops=200000000,
    )(
        tile_item,
        where,
        sums,
        k_gain,
        q_gain,
        cosine,
        sine,
        q_mine,
        got,
        *[arrived[chip] for chip in near_chips],
    )
    window = jax.ShapeDtypeStruct((14 * ROWS, half), bf16)
    mate_out, keys, values = call(
        functools.partial(far_kernel, near_chips, far_chips),
        (jax.ShapeDtypeStruct((ROWS, half), f32), window, window),
        [smem] * 3 + [vmem] * (7 + len(far_chips)),
        flops=300000000,
    )(
        tile_item,
        row_count,
        where,
        sums,
        k_gain,
        cosine,
        sine,
        q_mate,
        near_keys,
        near_values,
        *[arrived[chip] for chip in far_chips],
    )
    rest = swapped(mate_out)
    own = call(
        functools.partial(attend, False),
        jax.ShapeDtypeStruct((ROWS, half), f32),
        [smem] * 3 + [vmem] * 3,
        flops=300000000,
    )(tile_item, row_count, where, q_own, keys, values)
    return call(
        join_kernel, jax.ShapeDtypeStruct((ROWS, width), bf16), [smem] + [vmem] * 3
    )(where, own, rest, text_out)


def solution(mesh):
    spread = P("tile", "head")
    in_specs = (spread,) * 6 + (P("head"),) * 4 + (P(),) * 3
    return jax.shard_map(
        per_device, mesh=mesh, in_specs=in_specs, out_specs=spread, check_vma=False
    )
```

```python
import functools
import math

import jax
import jax.numpy as jnp
import numpy as np
from jax import lax
from jax.experimental import pallas as pl
from jax.experimental.pallas import tpu as pltpu
from jax.sharding import PartitionSpec as P

D = 5120
HD = 128
HGT = 30
WID = 52
SPAN = 7
ROWS = 128
EPSILON = 1e-06
SCALE = 1.0 / math.sqrt(HD)
NEG = -1e30
OWN_LINES, SIDE_LINES, QUERY_LINES = (0, 5), (7, 8), (1, 6)
SPARE = 16
HALF_ROWS = 2 * ROWS + SPARE
PART_ROWS = 4 * ROWS + SPARE


def rope_tables():
    spatial = HD // 6
    temporal = HD // 2 - 2 * spatial
    positions = np.arange(SPAN * ROWS)

    def freq(amount):
        exponent = np.arange(amount, dtype=np.float64) * 2.0 / (2 * amount)
        return (1.0 / 10000.0**exponent).astype(np.float32)

    def part(values, amount):
        return values.astype(np.float32)[:, None] * freq(amount)[None, :]

    angle = np.concatenate(
        [
            part(positions // (HGT * WID), temporal),
            part(positions // WID % HGT, spatial),
            part(positions % WID, spatial),
        ],
        axis=1,
    ).astype(np.float64)
    cosine = np.repeat(np.cos(angle), 2, axis=1).astype(np.float32)
    sine = np.stack([-np.sin(angle), np.sin(angle)], axis=2)
    return cosine, sine.reshape(SPAN * ROWS, HD).astype(np.float32)


def shifted(value, by, wrapped=()):
    peers = lax.axis_size("tile")
    pairs = []
    for i in range(peers):
        goal = i - by if i % 2 else i + by
        if 0 <= goal < peers or i in wrapped:
            pairs.append((i, goal % peers))
    return lax.ppermute(value, "tile", pairs)


def swapped(value):
    peers = lax.axis_size("tile")
    return lax.ppermute(value, "tile", [(i, i ^ 1) for i in range(peers)])


def by_rows(total_row):
    factor = lax.rsqrt(total_row / D + EPSILON)
    return jnp.transpose(jnp.broadcast_to(factor, (ROWS, ROWS)))


def rotated(normal, cosine, sine, even):
    partner = jnp.where(even, pltpu.roll(normal, HD - 1, 1), pltpu.roll(normal, 1, 1))
    return normal * cosine + partner * sine


def prefix_live(shape, count):
    return lax.broadcasted_iota(jnp.int32, shape, 1) < count


def pieces(*totals):
    rows = []
    for rest in totals:
        for _ in range(3):
            rows.append(rest.astype(jnp.bfloat16).astype(jnp.float32))
            rest = rest - rows[-1]
    rows.append(jnp.zeros((SPARE - len(rows), ROWS), jnp.float32))
    return jnp.concatenate(rows, axis=0).astype(jnp.bfloat16)


def joined(rows, first):
    return rows[first : first + 1] + rows[first + 1 : first + 2] + rows[first + 2 : first + 3]


def pack_kernel(
    here_ref, q_hbm, k_hbm, v_hbm, c_hbm, t_hbm, theirs_ref, q_mine_ref, sums_ref,
    q_ref, k_ref, v_ref, c_ref, t_ref, arrived
):
    pairs = ((k_hbm, k_ref), (v_hbm, v_ref), (q_hbm, q_ref), (c_hbm, c_ref), (t_hbm, t_ref))
    copies = [
        pltpu.make_async_copy(source, target, arrived.at[index])
        for index, (source, target) in enumerate(pairs)
    ]
    for copy in copies:
        copy.start()
    core = lax.rem(here_ref[0], 2)
    half = theirs_ref.shape[1]

    def total(ref, first):
        rows = None
        for head in range(ref.shape[1] // HD):
            x = ref[first : first + ROWS, head * HD : (head + 1) * HD].astype(jnp.float32)
            rows = x * x if rows is None else rows + x * x
        return jnp.sum(jnp.transpose(rows), axis=0, keepdims=True)

    def split(ref, first):
        for side in range(2):
            row = side * HALF_ROWS + first
            theirs_ref[row : row + ROWS, :] = ref[:, side * half : (side + 1) * half]

    sums_ref[...] = jnp.zeros((8, ROWS), jnp.float32)
    copies[0].wait()
    split(k_ref, 0)
    k_total = total(k_ref, 0)
    copies[1].wait()
    split(v_ref, ROWS)
    copies[2].wait()
    low, high = q_ref[:, :half], q_ref[:, half:]
    q_mine_ref[...] = jnp.where(core == 0, low, high)
    theirs_ref[2 * HALF_ROWS :, :] = jnp.where(core == 0, high, low)
    q_total = total(q_ref, 0)
    sums_ref[0:1, :] = k_total
    sums_ref[1:2, :] = q_total
    for side in range(2):
        rows = slice(side * HALF_ROWS + 2 * ROWS, (side + 1) * HALF_ROWS)
        theirs_ref[rows, 0:ROWS] = pieces(k_total, q_total)
        theirs_ref[rows, ROWS:] = jnp.zeros((SPARE, half - ROWS), jnp.bfloat16)
    copies[3].wait()
    sums_ref[2:3, :] = total(c_ref, 0)
    copies[4].wait()
    sums_ref[3:4, :] = total(t_ref, 0)
    sums_ref[4:5, :] = total(t_ref, ROWS)


def mate_kernel(own_ref, got_ref, out_ref):
    rows = got_ref[2 * ROWS : HALF_ROWS, 0:ROWS].astype(jnp.float32)
    out_ref[...] = own_ref[...]
    out_ref[5:6, :] = joined(rows, 0)
    out_ref[6:7, :] = joined(rows, 3)


def table_kernel(own_ref, side_ref, out_ref):
    out_ref[0:8, :] = own_ref[...]
    out_ref[8:16, :] = jnp.zeros((8, ROWS), jnp.float32)
    out_ref[7:8, :] = side_ref[0:1, :]
    out_ref[8:9, :] = side_ref[5:6, :]


def pieces_kernel(sums_ref, out_ref):
    out_ref[...] = jnp.zeros(out_ref.shape, jnp.bfloat16)
    out_ref[:, 0:ROWS] = pieces(*(sums_ref[line : line + 1, :] for line in SIDE_LINES))


def part_kernel(here_ref, *rest):
    blocks, out_ref, arrived = rest[:-2], rest[-2], rest[-1]
    side = 1 - lax.rem(here_ref[0], 2)
    copies = []
    for index, block in enumerate(blocks):
        first = index * PART_ROWS
        for slot in range(2):
            row = pl.multiple_of((2 * slot + side) * HALF_ROWS, SPARE)
            goal = first + slot * 2 * ROWS
            copies.append((block.at[pl.ds(row, 2 * ROWS)], out_ref.at[goal : goal + 2 * ROWS]))
        goal = first + 4 * ROWS
        copies.append((block.at[2 * ROWS : HALF_ROWS], out_ref.at[goal : goal + SPARE]))
    copies = [pltpu.make_async_copy(*pair, arrived.at[i]) for i, pair in enumerate(copies)]
    for copy in copies:
        copy.start()
    for copy in copies:
        copy.wait()


def cross_kernel(item_ref, len_ref, here_ref, sums_ref, q_ref, k_ref, v_ref, qg_ref, kg_ref, out_ref):
    count = len_ref[item_ref[here_ref[0]]]
    q_factor = by_rows(sums_ref[2:3, :])
    k_factor = [by_rows(sums_ref[3:4, :]), by_rows(sums_ref[4:5, :])]
    live = prefix_live((ROWS, 2 * ROWS), count)
    for head in range(q_ref.shape[1] // HD):
        cols = slice(head * HD, (head + 1) * HD)
        q = (q_ref[:, cols].astype(jnp.float32) * q_factor * qg_ref[:, cols]).astype(jnp.bfloat16)
        keys = [
            (
                k_ref[h * ROWS : (h + 1) * ROWS, cols].astype(jnp.float32)
                * k_factor[h]
                * kg_ref[:, cols]
            ).astype(jnp.bfloat16)
            for h in range(2)
        ]
        k = jnp.concatenate(keys, axis=0)
        s = lax.dot_general(q, k, (((1,), (1,)), ((), ())), preferred_element_type=jnp.float32)
        s = jnp.where(live, s * SCALE, NEG)
        w = jnp.exp(s - jnp.max(s, axis=1, keepdims=True))
        total = jnp.sum(w, axis=1, keepdims=True)
        o = jnp.dot(w.astype(jnp.bfloat16), v_ref[:, cols], preferred_element_type=jnp.float32)
        out_ref[:, cols] = o / total


def extent(item_ref, tile):
    tiles = item_ref.shape[0]
    item = item_ref[tile]
    before = jnp.int32(0)
    after = jnp.int32(0)
    for d in range(1, SPAN):
        lower = item_ref[jnp.maximum(tile - d, 0)] == item
        upper = item_ref[jnp.minimum(tile + d, tiles - 1)] == item
        before += jnp.where(jnp.logical_and(lower, tile - d >= 0), 1, 0)
        after += jnp.where(jnp.logical_and(upper, tile + d < tiles), 1, 0)
    return tile - before, tile + after


def turn(ref, rows, factor, gain_ref, cos_ref, sin_ref, start, dest_ref, goal):
    even = lax.rem(lax.broadcasted_iota(jnp.int32, (ROWS, HD), 1), 2) == 0
    cosine = cos_ref[pl.ds(start, ROWS), :]
    sine = sin_ref[pl.ds(start, ROWS), :]
    for head in range(ref.shape[1] // HD):
        cols = slice(head * HD, (head + 1) * HD)
        x = ref[rows, cols].astype(jnp.float32) * factor * gain_ref[:, cols]
        dest_ref[goal, cols] = rotated(x, cosine, sine, even).astype(jnp.bfloat16)


def gather(chip, rows_of, totals, block, core, left, bounds, gains, tables, keys_ref, values_ref, first_chip):
    first_a, last_a, first_b, last_b = bounds
    for parity in range(2):
        tile = left + 2 * chip + parity
        slot, row = rows_of(parity)
        key_rows = pl.ds(pl.multiple_of(row, SPARE), ROWS)
        value_rows = pl.ds(pl.multiple_of(row + ROWS, SPARE), ROWS)
        goal = pl.ds(pl.multiple_of((2 * (chip - first_chip) + parity) * ROWS, ROWS), ROWS)
        values_ref[goal, :] = block[value_rows, :]

        @pl.when(jnp.logical_and(tile >= first_a, tile <= last_b))
        def _(tile=tile, slot=slot, key_rows=key_rows, goal=goal):
            first = jnp.where(tile <= last_a, first_a, first_b)
            start = pl.multiple_of((tile - first) * ROWS, ROWS)
            total = jnp.where(slot == 0, *totals())
            turn(block, key_rows, by_rows(total), gains, *tables, start, keys_ref, goal)


def kept_rows(core):
    def rows_of(parity):
        slot = jnp.where(core == parity, 0, 1)
        return slot, (2 * slot + core) * HALF_ROWS

    return rows_of


def part_rows(core, index):
    def rows_of(parity):
        slot = jnp.where(core == parity, 1, 0)
        return slot, index * PART_ROWS + slot * 2 * ROWS

    return rows_of


def lines(ref, pair):
    return lambda: tuple(ref[line : line + 1, :] for line in pair)


def spares(ref, first):
    def totals():
        rows = ref[first : first + SPARE, 0:ROWS].astype(jnp.float32)
        return joined(rows, 0), joined(rows, 3)

    return totals


def near_kernel(
    item_ref, here_ref, sums_ref, mate_sums_ref, k_gain_ref, q_gain_ref, cos_ref, sin_ref, q_own_ref, got_ref,
    block_ref, kept_ref, part_ref, keys_ref, values_ref, own_turned_ref, mate_turned_ref
):
    core = lax.rem(here_ref[0], 2)
    left = here_ref[0] - core
    sign = 2 * core - 1
    half = keys_ref.shape[1]
    bounds = (*extent(item_ref, left), *extent(item_ref, left + 1))
    columns = pl.ds(pl.multiple_of(core * half, HD), half)
    k_gains, q_gains = k_gain_ref.at[:, columns], q_gain_ref.at[:, columns]
    tables = (cos_ref, sin_ref)
    for which, (source, rows, line, goal) in enumerate(
        (
            (q_own_ref, slice(0, ROWS), QUERY_LINES[0], own_turned_ref),
            (got_ref, slice(2 * HALF_ROWS, 2 * HALF_ROWS + ROWS), QUERY_LINES[1], mate_turned_ref),
        )
    ):
        is_a = core == which
        first = jnp.where(is_a, bounds[0], bounds[2])
        tile = jnp.where(is_a, left, left + 1)
        start = pl.multiple_of((tile - first) * ROWS, ROWS)
        factor = by_rows(sums_ref[line : line + 1, :])
        turn(source, rows, factor, q_gains, *tables, start, goal, slice(None))
    for chip, rows_of, totals, block in (
        (0, kept_rows(core), lines(sums_ref, OWN_LINES), block_ref),
        (sign, kept_rows(core), lines(sums_ref, SIDE_LINES), kept_ref),
        (-sign, part_rows(core, 0), lines(mate_sums_ref, SIDE_LINES), part_ref),
    ):
        gather(chip, rows_of, totals, block, core, left, bounds, k_gains, tables, keys_ref, values_ref, -1)


def attend(mate, item_ref, count_ref, here_ref, q_ref, keys_ref, values_ref, out_ref):
    core = lax.rem(here_ref[0], 2)
    left = here_ref[0] - core
    tile = left + (1 - core if mate else core)
    first, last = extent(item_ref, tile)
    window = pl.ds(pl.multiple_of((first - left + 6) * ROWS, ROWS), SPAN * ROWS)
    tiles = item_ref.shape[0]
    lanes = lax.broadcasted_iota(jnp.int32, (ROWS, ROWS), 1)
    live = []
    for slot in range(SPAN):
        count = count_ref[jnp.minimum(first + slot, tiles - 1)]
        live.append(lanes < jnp.where(first + slot <= last, count, 0))
    for head in range(q_ref.shape[1] // HD):
        cols = slice(head * HD, (head + 1) * HD)
        s = lax.dot_general(
            q_ref[:, cols],
            keys_ref[window, cols],
            (((1,), (1,)), ((), ())),
            preferred_element_type=jnp.float32,
        )
        parts = [
            jnp.where(live[slot], s[:, slot * ROWS : (slot + 1) * ROWS] * SCALE, NEG)
            for slot in range(SPAN)
        ]
        top = functools.reduce(jnp.maximum, parts)
        top = jnp.max(top, axis=1, keepdims=True)
        parts = [jnp.exp(part - top) for part in parts]
        total = jnp.sum(functools.reduce(jnp.add, parts), axis=1, keepdims=True)
        weights = jnp.concatenate([part.astype(jnp.bfloat16) for part in parts], axis=1)
        mixed = jnp.dot(weights, values_ref[window, cols], preferred_element_type=jnp.float32)
        out_ref[:, cols] = mixed / total


def far_kernel(
    item_ref, count_ref, here_ref, k_gain_ref, cos_ref, sin_ref, q_ref, near_keys_ref, near_values_ref,
    second_ref, third_ref, part_ref, out_ref, keys_ref, values_ref
):
    core = lax.rem(here_ref[0], 2)
    left = here_ref[0] - core
    sign = 2 * core - 1
    half = keys_ref.shape[1]
    bounds = (*extent(item_ref, left), *extent(item_ref, left + 1))
    k_gains = k_gain_ref.at[:, pl.ds(pl.multiple_of(core * half, HD), half)]
    near = slice(4 * ROWS, 10 * ROWS)
    keys_ref[near, :] = near_keys_ref[...]
    values_ref[near, :] = near_values_ref[...]
    for chip, rows_of, totals, block in (
        (2 * sign, kept_rows(core), spares(second_ref, 2 * ROWS), second_ref),
        (-3 * sign, kept_rows(core), spares(third_ref, 2 * ROWS), third_ref),
        (-2 * sign, part_rows(core, 0), spares(part_ref, 4 * ROWS), part_ref),
        (3 * sign, part_rows(core, 1), spares(part_ref, PART_ROWS + 4 * ROWS), part_ref),
    ):
        gather(
            chip, rows_of, totals, block, core, left, bounds, k_gains, (cos_ref, sin_ref), keys_ref, values_ref, -3
        )
    attend(True, item_ref, count_ref, here_ref, q_ref, keys_ref, values_ref, out_ref)


def join_kernel(here_ref, own_ref, other_ref, text_ref, out_ref):
    core = lax.rem(here_ref[0], 2)
    width = own_ref.shape[1]
    mine = pl.multiple_of(core * width, HD)
    theirs = pl.multiple_of((1 - core) * width, HD)
    out_ref[:, pl.ds(mine, width)] = (own_ref[...] + text_ref[:, pl.ds(mine, width)]).astype(
        jnp.bfloat16
    )
    out_ref[:, pl.ds(theirs, width)] = (other_ref[...] + text_ref[:, pl.ds(theirs, width)]).astype(
        jnp.bfloat16
    )


def call(kernel, out_shape, specs, scratch=(), flops=1000000, limit=40):
    return pl.pallas_call(
        kernel,
        out_shape=out_shape,
        in_specs=specs,
        out_specs=jax.tree.map(lambda _: pl.BlockSpec(memory_space=pltpu.VMEM), out_shape),
        scratch_shapes=list(scratch),
        compiler_params=pltpu.CompilerParams(vmem_limit_bytes=limit << 20),
        cost_estimate=pl.CostEstimate(flops=flops, bytes_accessed=4000000, transcendentals=0),
    )


def per_device(
    self_query,
    self_key,
    self_value,
    cross_query,
    text_key,
    text_value,
    query_gain,
    key_gain,
    cross_gain,
    text_gain,
    tile_item,
    row_count,
    text_len,
):
    smem = pl.BlockSpec(memory_space=pltpu.SMEM)
    vmem = pl.BlockSpec(memory_space=pltpu.VMEM)
    f32 = jnp.float32
    width = self_query.shape[1]
    half = width // 2
    here = lax.axis_index("tile").astype(jnp.int32)
    core = lax.rem(here, 2)
    where = here.reshape(1)

    bf16 = jnp.bfloat16
    hbm = pl.BlockSpec(memory_space=pltpu.HBM)
    theirs, q_mine, sums = call(
        pack_kernel,
        (
            jax.ShapeDtypeStruct((2 * HALF_ROWS + ROWS, half), bf16),
            jax.ShapeDtypeStruct((ROWS, half), bf16),
            jax.ShapeDtypeStruct((8, ROWS), f32),
        ),
        [smem] + [hbm] * 5,
        scratch=[pltpu.VMEM((ROWS, width), bf16)] * 4
        + [pltpu.VMEM((2 * ROWS, width), bf16), pltpu.SemaphoreType.DMA((5,))],
        limit=60,
    )(where, self_query, self_key, self_value, cross_query, text_key)
    got = swapped(theirs)
    peers = lax.axis_size("tile")
    ends = (peers - 2, 1)
    sums = call(mate_kernel, jax.ShapeDtypeStruct((8, ROWS), f32), [vmem] * 2)(sums, got)
    side_sums = shifted(sums, 2, ends)
    block = jnp.concatenate([theirs[: 2 * HALF_ROWS], got[: 2 * HALF_ROWS]], axis=0)
    block, side_sums = lax.optimization_barrier((block, side_sums))
    side = shifted(block, 2, ends)
    sums = call(table_kernel, jax.ShapeDtypeStruct((16, ROWS), f32), [vmem] * 2)(sums, side_sums)
    sums = lax.psum(sums, "head")
    side, sums = lax.optimization_barrier((side, sums))
    marks = call(pieces_kernel, jax.ShapeDtypeStruct((SPARE, half), bf16), [vmem])(sums)
    side = lax.dynamic_update_slice(side, marks, (2 * ROWS, 0))
    second = shifted(side, 2)
    third = shifted(side, -8, (0, peers - 1))

    def parts(*blocks):
        return swapped(
            call(
                part_kernel,
                jax.ShapeDtypeStruct((len(blocks) * PART_ROWS, half), bf16),
                [smem] + [hbm] * len(blocks),
                scratch=[pltpu.SemaphoreType.DMA((3 * len(blocks),))],
            )(where, *blocks)
        )

    near_part = parts(side)
    mate_sums = swapped(sums)

    text_out = call(
        cross_kernel, jax.ShapeDtypeStruct((ROWS, width), f32), [smem] * 3 + [vmem] * 6, flops=400000000
    )(
        tile_item,
        text_len,
        where,
        sums,
        cross_query,
        text_key,
        text_value,
        cross_gain[None, :],
        text_gain[None, :],
    )
    q_gain, k_gain = query_gain[None, :], key_gain[None, :]
    text_out, q_gain, k_gain = lax.optimization_barrier((text_out, q_gain, k_gain))

    cosine, sine = (jnp.asarray(t) for t in rope_tables())
    near_keys, near_values, q_own, q_mate = call(
        near_kernel,
        (jax.ShapeDtypeStruct((6 * ROWS, half), bf16),) * 2 + (jax.ShapeDtypeStruct((ROWS, half), bf16),) * 2,
        [smem] * 2 + [vmem] * 11,
        flops=200000000,
    )(
        tile_item, where, sums, mate_sums, k_gain, q_gain, cosine, sine, q_mine, got, block, side, near_part
    )
    second, third, near_keys, near_values, text_out = lax.optimization_barrier(
        (second, third, near_keys, near_values, text_out)
    )
    far_part = parts(second, third)
    window = jax.ShapeDtypeStruct((14 * ROWS, half), bf16)
    mate_out, keys, values = call(
        far_kernel,
        (jax.ShapeDtypeStruct((ROWS, half), f32), window, window),
        [smem] * 3 + [vmem] * 9,
        flops=300000000,
    )(
        tile_item, row_count, where, k_gain, cosine, sine, q_mate, near_keys, near_values, second, third, far_part
    )
    rest = swapped(mate_out)
    own = call(
        functools.partial(attend, False),
        jax.ShapeDtypeStruct((ROWS, half), f32),
        [smem] * 3 + [vmem] * 3,
        flops=300000000,
    )(tile_item, row_count, where, q_own, keys, values)
    return call(
        join_kernel, jax.ShapeDtypeStruct((ROWS, width), bf16), [smem] + [vmem] * 3
    )(where, own, rest, text_out)


def solution(mesh):
    spread = P("tile", "head")
    in_specs = (spread,) * 6 + (P("head"),) * 4 + (P(),) * 3
    return jax.shard_map(
        per_device, mesh=mesh, in_specs=in_specs, out_specs=spread, check_vma=False
    )
```

```python
import functools
import math

import jax
import jax.numpy as jnp
import numpy as np
from jax import lax
from jax.experimental import pallas as pl
from jax.experimental.pallas import tpu as pltpu
from jax.sharding import PartitionSpec as P

D = 5120
HD = 128
HGT = 30
WID = 52
SPAN = 7
ROWS = 128
EPSILON = 1e-06
SCALE = 1.0 / math.sqrt(HD)
NEG = -1e30
OWN_LINES, SIDE_LINES, QUERY_LINES = (0, 5), (7, 8), (1, 6)
SPARE = 16
HALF_ROWS = 2 * ROWS + SPARE
PART_ROWS = 4 * ROWS + SPARE


def rope_tables():
    spatial = HD // 6
    temporal = HD // 2 - 2 * spatial
    positions = np.arange(SPAN * ROWS)

    def freq(amount):
        exponent = np.arange(amount, dtype=np.float64) * 2.0 / (2 * amount)
        return (1.0 / 10000.0**exponent).astype(np.float32)

    def part(values, amount):
        return values.astype(np.float32)[:, None] * freq(amount)[None, :]

    angle = np.concatenate(
        [
            part(positions // (HGT * WID), temporal),
            part(positions // WID % HGT, spatial),
            part(positions % WID, spatial),
        ],
        axis=1,
    ).astype(np.float64)
    cosine = np.repeat(np.cos(angle), 2, axis=1).astype(np.float32)
    sine = np.stack([-np.sin(angle), np.sin(angle)], axis=2)
    return cosine, sine.reshape(SPAN * ROWS, HD).astype(np.float32)


def shifted(value, by, wrapped=()):
    peers = lax.axis_size("tile")
    pairs = []
    for i in range(peers):
        goal = i - by if i % 2 else i + by
        if 0 <= goal < peers or i in wrapped:
            pairs.append((i, goal % peers))
    return lax.ppermute(value, "tile", pairs)


def swapped(value):
    peers = lax.axis_size("tile")
    return lax.ppermute(value, "tile", [(i, i ^ 1) for i in range(peers)])


def by_rows(total_row):
    factor = lax.rsqrt(total_row / D + EPSILON)
    return jnp.transpose(jnp.broadcast_to(factor, (ROWS, ROWS)))


def rotated(normal, cosine, sine, even):
    partner = jnp.where(even, pltpu.roll(normal, HD - 1, 1), pltpu.roll(normal, 1, 1))
    return normal * cosine + partner * sine


def prefix_live(shape, count):
    return lax.broadcasted_iota(jnp.int32, shape, 1) < count


def pieces(*totals):
    rows = []
    for rest in totals:
        for _ in range(3):
            rows.append(rest.astype(jnp.bfloat16).astype(jnp.float32))
            rest = rest - rows[-1]
    rows.append(jnp.zeros((SPARE - len(rows), ROWS), jnp.float32))
    return jnp.concatenate(rows, axis=0).astype(jnp.bfloat16)


def joined(rows, first):
    return rows[first : first + 1] + rows[first + 1 : first + 2] + rows[first + 2 : first + 3]


def pack_kernel(
    here_ref, q_hbm, k_hbm, v_hbm, c_hbm, t_hbm, theirs_ref, q_mine_ref, sums_ref,
    q_ref, k_ref, v_ref, c_ref, t_ref, arrived
):
    pairs = ((k_hbm, k_ref), (v_hbm, v_ref), (q_hbm, q_ref), (c_hbm, c_ref), (t_hbm, t_ref))
    copies = [
        pltpu.make_async_copy(source, target, arrived.at[index])
        for index, (source, target) in enumerate(pairs)
    ]
    for copy in copies:
        copy.start()
    core = lax.rem(here_ref[0], 2)
    half = theirs_ref.shape[1]

    def total(ref, first):
        rows = None
        for head in range(ref.shape[1] // HD):
            x = ref[first : first + ROWS, head * HD : (head + 1) * HD].astype(jnp.float32)
            rows = x * x if rows is None else rows + x * x
        return jnp.sum(jnp.transpose(rows), axis=0, keepdims=True)

    def split(ref, first):
        for side in range(2):
            row = side * HALF_ROWS + first
            theirs_ref[row : row + ROWS, :] = ref[:, side * half : (side + 1) * half]

    sums_ref[...] = jnp.zeros((8, ROWS), jnp.float32)
    copies[0].wait()
    split(k_ref, 0)
    k_total = total(k_ref, 0)
    copies[1].wait()
    split(v_ref, ROWS)
    copies[2].wait()
    low, high = q_ref[:, :half], q_ref[:, half:]
    q_mine_ref[...] = jnp.where(core == 0, low, high)
    theirs_ref[2 * HALF_ROWS :, :] = jnp.where(core == 0, high, low)
    q_total = total(q_ref, 0)
    sums_ref[0:1, :] = k_total
    sums_ref[1:2, :] = q_total
    for side in range(2):
        rows = slice(side * HALF_ROWS + 2 * ROWS, (side + 1) * HALF_ROWS)
        theirs_ref[rows, 0:ROWS] = pieces(k_total, q_total)
        theirs_ref[rows, ROWS:] = jnp.zeros((SPARE, half - ROWS), jnp.bfloat16)
    copies[3].wait()
    sums_ref[2:3, :] = total(c_ref, 0)
    copies[4].wait()
    sums_ref[3:4, :] = total(t_ref, 0)
    sums_ref[4:5, :] = total(t_ref, ROWS)


def mate_kernel(own_ref, got_ref, out_ref):
    rows = got_ref[2 * ROWS : HALF_ROWS, 0:ROWS].astype(jnp.float32)
    out_ref[...] = own_ref[...]
    out_ref[5:6, :] = joined(rows, 0)
    out_ref[6:7, :] = joined(rows, 3)


def table_kernel(own_ref, side_ref, out_ref):
    out_ref[0:8, :] = own_ref[...]
    out_ref[8:16, :] = jnp.zeros((8, ROWS), jnp.float32)
    out_ref[7:8, :] = side_ref[0:1, :]
    out_ref[8:9, :] = side_ref[5:6, :]


def pieces_kernel(sums_ref, out_ref):
    out_ref[...] = jnp.zeros(out_ref.shape, jnp.bfloat16)
    out_ref[:, 0:ROWS] = pieces(*(sums_ref[line : line + 1, :] for line in SIDE_LINES))


def part_kernel(here_ref, *rest):
    blocks, out_ref, arrived = rest[:-2], rest[-2], rest[-1]
    side = 1 - lax.rem(here_ref[0], 2)
    copies = []
    for index, block in enumerate(blocks):
        first = index * PART_ROWS
        for slot in range(2):
            row = pl.multiple_of((2 * slot + side) * HALF_ROWS, SPARE)
            goal = first + slot * 2 * ROWS
            copies.append((block.at[pl.ds(row, 2 * ROWS)], out_ref.at[goal : goal + 2 * ROWS]))
        goal = first + 4 * ROWS
        copies.append((block.at[2 * ROWS : HALF_ROWS], out_ref.at[goal : goal + SPARE]))
    copies = [pltpu.make_async_copy(*pair, arrived.at[i]) for i, pair in enumerate(copies)]
    for copy in copies:
        copy.start()
    for copy in copies:
        copy.wait()


def cross_kernel(item_ref, len_ref, here_ref, sums_ref, q_ref, k_ref, v_ref, qg_ref, kg_ref, out_ref):
    count = len_ref[item_ref[here_ref[0]]]
    q_factor = by_rows(sums_ref[2:3, :])
    k_factor = [by_rows(sums_ref[3:4, :]), by_rows(sums_ref[4:5, :])]
    live = prefix_live((ROWS, 2 * ROWS), count)
    for head in range(q_ref.shape[1] // HD):
        cols = slice(head * HD, (head + 1) * HD)
        q = (q_ref[:, cols].astype(jnp.float32) * q_factor * qg_ref[:, cols]).astype(jnp.bfloat16)
        keys = [
            (
                k_ref[h * ROWS : (h + 1) * ROWS, cols].astype(jnp.float32)
                * k_factor[h]
                * kg_ref[:, cols]
            ).astype(jnp.bfloat16)
            for h in range(2)
        ]
        k = jnp.concatenate(keys, axis=0)
        s = lax.dot_general(q, k, (((1,), (1,)), ((), ())), preferred_element_type=jnp.float32)
        s = jnp.where(live, s * SCALE, NEG)
        w = jnp.exp(s - jnp.max(s, axis=1, keepdims=True))
        total = jnp.sum(w, axis=1, keepdims=True)
        o = jnp.dot(w.astype(jnp.bfloat16), v_ref[:, cols], preferred_element_type=jnp.float32)
        out_ref[:, cols] = o / total


def extent(item_ref, tile):
    tiles = item_ref.shape[0]
    item = item_ref[tile]
    before = jnp.int32(0)
    after = jnp.int32(0)
    for d in range(1, SPAN):
        lower = item_ref[jnp.maximum(tile - d, 0)] == item
        upper = item_ref[jnp.minimum(tile + d, tiles - 1)] == item
        before += jnp.where(jnp.logical_and(lower, tile - d >= 0), 1, 0)
        after += jnp.where(jnp.logical_and(upper, tile + d < tiles), 1, 0)
    return tile - before, tile + after


def turn(ref, rows, factor, gain_ref, cos_ref, sin_ref, start, dest_ref, goal):
    even = lax.rem(lax.broadcasted_iota(jnp.int32, (ROWS, HD), 1), 2) == 0
    cosine = cos_ref[pl.ds(start, ROWS), :]
    sine = sin_ref[pl.ds(start, ROWS), :]
    for head in range(ref.shape[1] // HD):
        cols = slice(head * HD, (head + 1) * HD)
        x = ref[rows, cols].astype(jnp.float32) * factor * gain_ref[:, cols]
        dest_ref[goal, cols] = rotated(x, cosine, sine, even).astype(jnp.bfloat16)


def gather(chip, rows_of, totals, block, core, left, bounds, gains, tables, keys_ref, values_ref, first_chip):
    first_a, last_a, first_b, last_b = bounds
    for parity in range(2):
        tile = left + 2 * chip + parity
        slot, row = rows_of(parity)
        key_rows = pl.ds(pl.multiple_of(row, SPARE), ROWS)
        value_rows = pl.ds(pl.multiple_of(row + ROWS, SPARE), ROWS)
        goal = pl.ds(pl.multiple_of((2 * (chip - first_chip) + parity) * ROWS, ROWS), ROWS)
        values_ref[goal, :] = block[value_rows, :]

        @pl.when(jnp.logical_and(tile >= first_a, tile <= last_b))
        def _(tile=tile, slot=slot, key_rows=key_rows, goal=goal):
            first = jnp.where(tile <= last_a, first_a, first_b)
            start = pl.multiple_of((tile - first) * ROWS, ROWS)
            total = jnp.where(slot == 0, *totals())
            turn(block, key_rows, by_rows(total), gains, *tables, start, keys_ref, goal)


def kept_rows(core):
    def rows_of(parity):
        slot = jnp.where(core == parity, 0, 1)
        return slot, (2 * slot + core) * HALF_ROWS

    return rows_of


def part_rows(core, index):
    def rows_of(parity):
        slot = jnp.where(core == parity, 1, 0)
        return slot, index * PART_ROWS + slot * 2 * ROWS

    return rows_of


def lines(ref, pair):
    return lambda: tuple(ref[line : line + 1, :] for line in pair)


def spares(ref, first):
    def totals():
        rows = ref[first : first + SPARE, 0:ROWS].astype(jnp.float32)
        return joined(rows, 0), joined(rows, 3)

    return totals


def block_kernel(own_ref, mate_ref, out_ref, arrived):
    tile = 2 * HALF_ROWS
    copies = [
        pltpu.make_async_copy(ref.at[0:tile], out_ref.at[slot * tile : (slot + 1) * tile], arrived.at[slot])
        for slot, ref in enumerate((own_ref, mate_ref))
    ]
    for copy in copies:
        copy.start()
    for copy in copies:
        copy.wait()


def near_kernel(
    item_ref, here_ref, sums_ref, mate_sums_ref, k_gain_ref, q_gain_ref, cos_ref, sin_ref, q_own_ref, got_ref,
    block_ref, kept_ref, part_ref, keys_ref, values_ref, own_turned_ref, mate_turned_ref
):
    core = lax.rem(here_ref[0], 2)
    left = here_ref[0] - core
    sign = 2 * core - 1
    half = keys_ref.shape[1]
    bounds = (*extent(item_ref, left), *extent(item_ref, left + 1))
    columns = pl.ds(pl.multiple_of(core * half, HD), half)
    k_gains, q_gains = k_gain_ref.at[:, columns], q_gain_ref.at[:, columns]
    tables = (cos_ref, sin_ref)
    for which, (source, rows, line, goal) in enumerate(
        (
            (q_own_ref, slice(0, ROWS), QUERY_LINES[0], own_turned_ref),
            (got_ref, slice(2 * HALF_ROWS, 2 * HALF_ROWS + ROWS), QUERY_LINES[1], mate_turned_ref),
        )
    ):
        is_a = core == which
        first = jnp.where(is_a, bounds[0], bounds[2])
        tile = jnp.where(is_a, left, left + 1)
        start = pl.multiple_of((tile - first) * ROWS, ROWS)
        factor = by_rows(sums_ref[line : line + 1, :])
        turn(source, rows, factor, q_gains, *tables, start, goal, slice(None))
    for chip, rows_of, totals, block in (
        (0, kept_rows(core), lines(sums_ref, OWN_LINES), block_ref),
        (sign, kept_rows(core), lines(sums_ref, SIDE_LINES), kept_ref),
        (-sign, part_rows(core, 0), lines(mate_sums_ref, SIDE_LINES), part_ref),
    ):
        gather(chip, rows_of, totals, block, core, left, bounds, k_gains, tables, keys_ref, values_ref, -1)


def attend(mate, item_ref, count_ref, here_ref, q_ref, keys_ref, values_ref, out_ref):
    core = lax.rem(here_ref[0], 2)
    left = here_ref[0] - core
    tile = left + (1 - core if mate else core)
    first, last = extent(item_ref, tile)
    window = pl.ds(pl.multiple_of((first - left + 6) * ROWS, ROWS), SPAN * ROWS)
    tiles = item_ref.shape[0]
    lanes = lax.broadcasted_iota(jnp.int32, (ROWS, ROWS), 1)
    live = []
    for slot in range(SPAN):
        count = count_ref[jnp.minimum(first + slot, tiles - 1)]
        live.append(lanes < jnp.where(first + slot <= last, count, 0))
    for head in range(q_ref.shape[1] // HD):
        cols = slice(head * HD, (head + 1) * HD)
        s = lax.dot_general(
            q_ref[:, cols],
            keys_ref[window, cols],
            (((1,), (1,)), ((), ())),
            preferred_element_type=jnp.float32,
        )
        parts = [
            jnp.where(live[slot], s[:, slot * ROWS : (slot + 1) * ROWS] * SCALE, NEG)
            for slot in range(SPAN)
        ]
        top = functools.reduce(jnp.maximum, parts)
        top = jnp.max(top, axis=1, keepdims=True)
        parts = [jnp.exp(part - top) for part in parts]
        total = jnp.sum(functools.reduce(jnp.add, parts), axis=1, keepdims=True)
        weights = jnp.concatenate([part.astype(jnp.bfloat16) for part in parts], axis=1)
        mixed = jnp.dot(weights, values_ref[window, cols], preferred_element_type=jnp.float32)
        out_ref[:, cols] = mixed / total


def far_kernel(
    item_ref, count_ref, here_ref, k_gain_ref, cos_ref, sin_ref, q_ref, near_keys_ref, near_values_ref,
    second_ref, third_ref, part_ref, out_ref, keys_ref, values_ref, arrived
):
    core = lax.rem(here_ref[0], 2)
    left = here_ref[0] - core
    sign = 2 * core - 1
    half = keys_ref.shape[1]
    bounds = (*extent(item_ref, left), *extent(item_ref, left + 1))
    k_gains = k_gain_ref.at[:, pl.ds(pl.multiple_of(core * half, HD), half)]
    near = slice(4 * ROWS, 10 * ROWS)
    copies = [
        pltpu.make_async_copy(near_keys_ref, keys_ref.at[near], arrived.at[0]),
        pltpu.make_async_copy(near_values_ref, values_ref.at[near], arrived.at[1]),
    ]
    for copy in copies:
        copy.start()
    for chip, rows_of, totals, block in (
        (2 * sign, kept_rows(core), spares(second_ref, 2 * ROWS), second_ref),
        (-3 * sign, kept_rows(core), spares(third_ref, 2 * ROWS), third_ref),
        (-2 * sign, part_rows(core, 0), spares(part_ref, 4 * ROWS), part_ref),
        (3 * sign, part_rows(core, 1), spares(part_ref, PART_ROWS + 4 * ROWS), part_ref),
    ):
        gather(
            chip, rows_of, totals, block, core, left, bounds, k_gains, (cos_ref, sin_ref), keys_ref, values_ref, -3
        )
    for copy in copies:
        copy.wait()
    attend(True, item_ref, count_ref, here_ref, q_ref, keys_ref, values_ref, out_ref)


def join_kernel(here_ref, own_ref, other_ref, text_ref, out_ref):
    core = lax.rem(here_ref[0], 2)
    width = own_ref.shape[1]
    mine = pl.multiple_of(core * width, HD)
    theirs = pl.multiple_of((1 - core) * width, HD)
    out_ref[:, pl.ds(mine, width)] = (own_ref[...] + text_ref[:, pl.ds(mine, width)]).astype(
        jnp.bfloat16
    )
    out_ref[:, pl.ds(theirs, width)] = (other_ref[...] + text_ref[:, pl.ds(theirs, width)]).astype(
        jnp.bfloat16
    )


def call(kernel, out_shape, specs, scratch=(), flops=1000000, limit=40):
    return pl.pallas_call(
        kernel,
        out_shape=out_shape,
        in_specs=specs,
        out_specs=jax.tree.map(lambda _: pl.BlockSpec(memory_space=pltpu.VMEM), out_shape),
        scratch_shapes=list(scratch),
        compiler_params=pltpu.CompilerParams(vmem_limit_bytes=limit << 20),
        cost_estimate=pl.CostEstimate(flops=flops, bytes_accessed=4000000, transcendentals=0),
    )


def per_device(
    self_query,
    self_key,
    self_value,
    cross_query,
    text_key,
    text_value,
    query_gain,
    key_gain,
    cross_gain,
    text_gain,
    tile_item,
    row_count,
    text_len,
):
    smem = pl.BlockSpec(memory_space=pltpu.SMEM)
    vmem = pl.BlockSpec(memory_space=pltpu.VMEM)
    f32 = jnp.float32
    width = self_query.shape[1]
    half = width // 2
    here = lax.axis_index("tile").astype(jnp.int32)
    core = lax.rem(here, 2)
    where = here.reshape(1)

    bf16 = jnp.bfloat16
    hbm = pl.BlockSpec(memory_space=pltpu.HBM)
    theirs, q_mine, sums = call(
        pack_kernel,
        (
            jax.ShapeDtypeStruct((2 * HALF_ROWS + ROWS, half), bf16),
            jax.ShapeDtypeStruct((ROWS, half), bf16),
            jax.ShapeDtypeStruct((8, ROWS), f32),
        ),
        [smem] + [hbm] * 5,
        scratch=[pltpu.VMEM((ROWS, width), bf16)] * 4
        + [pltpu.VMEM((2 * ROWS, width), bf16), pltpu.SemaphoreType.DMA((5,))],
        limit=60,
    )(where, self_query, self_key, self_value, cross_query, text_key)
    got = swapped(theirs)
    peers = lax.axis_size("tile")
    ends = (peers - 2, 1)
    sums = call(mate_kernel, jax.ShapeDtypeStruct((8, ROWS), f32), [vmem] * 2)(sums, got)
    side_sums = shifted(sums, 2, ends)
    block = call(
        block_kernel,
        jax.ShapeDtypeStruct((4 * HALF_ROWS, half), bf16),
        [hbm] * 2,
        scratch=[pltpu.SemaphoreType.DMA((2,))],
    )(theirs, got)
    block, side_sums = lax.optimization_barrier((block, side_sums))
    side = shifted(block, 2, ends)
    sums = call(table_kernel, jax.ShapeDtypeStruct((16, ROWS), f32), [vmem] * 2)(sums, side_sums)
    sums = lax.psum(sums, "head")
    side, sums = lax.optimization_barrier((side, sums))
    marks = call(pieces_kernel, jax.ShapeDtypeStruct((SPARE, half), bf16), [vmem])(sums)
    side = lax.dynamic_update_slice(side, marks, (2 * ROWS, 0))
    second = shifted(side, 2)
    third = shifted(side, -8, (0, peers - 1))

    def parts(*blocks):
        return swapped(
            call(
                part_kernel,
                jax.ShapeDtypeStruct((len(blocks) * PART_ROWS, half), bf16),
                [smem] + [hbm] * len(blocks),
                scratch=[pltpu.SemaphoreType.DMA((3 * len(blocks),))],
            )(where, *blocks)
        )

    near_part = parts(side)
    mate_sums = swapped(sums)

    text_out = call(
        cross_kernel, jax.ShapeDtypeStruct((ROWS, width), f32), [smem] * 3 + [vmem] * 6, flops=400000000
    )(
        tile_item,
        text_len,
        where,
        sums,
        cross_query,
        text_key,
        text_value,
        cross_gain[None, :],
        text_gain[None, :],
    )
    q_gain, k_gain = query_gain[None, :], key_gain[None, :]
    text_out, q_gain, k_gain = lax.optimization_barrier((text_out, q_gain, k_gain))

    cosine, sine = (jnp.asarray(t) for t in rope_tables())
    near_keys, near_values, q_own, q_mate = call(
        near_kernel,
        (jax.ShapeDtypeStruct((6 * ROWS, half), bf16),) * 2 + (jax.ShapeDtypeStruct((ROWS, half), bf16),) * 2,
        [smem] * 2 + [vmem] * 11,
        flops=200000000,
    )(
        tile_item, where, sums, mate_sums, k_gain, q_gain, cosine, sine, q_mine, got, block, side, near_part
    )
    second, third, near_keys, near_values, text_out = lax.optimization_barrier(
        (second, third, near_keys, near_values, text_out)
    )
    far_part = parts(second, third)
    window = jax.ShapeDtypeStruct((14 * ROWS, half), bf16)
    mate_out, keys, values = call(
        far_kernel,
        (jax.ShapeDtypeStruct((ROWS, half), f32), window, window),
        [smem] * 3 + [vmem] * 9,
        scratch=[pltpu.SemaphoreType.DMA((2,))],
        flops=300000000,
    )(
        tile_item, row_count, where, k_gain, cosine, sine, q_mate, near_keys, near_values, second, third, far_part
    )
    rest = swapped(mate_out)
    own = call(
        functools.partial(attend, False),
        jax.ShapeDtypeStruct((ROWS, half), f32),
        [smem] * 3 + [vmem] * 3,
        flops=300000000,
    )(tile_item, row_count, where, q_own, keys, values)
    return call(
        join_kernel, jax.ShapeDtypeStruct((ROWS, width), bf16), [smem] + [vmem] * 3
    )(where, own, rest, text_out)


def solution(mesh):
    spread = P("tile", "head")
    in_specs = (spread,) * 6 + (P("head"),) * 4 + (P(),) * 3
    return jax.shard_map(
        per_device, mesh=mesh, in_specs=in_specs, out_specs=spread, check_vma=False
    )
```

```python
import functools
import math

import jax
import jax.numpy as jnp
import numpy as np
from jax import lax
from jax.experimental import pallas as pl
from jax.experimental.pallas import tpu as pltpu
from jax.sharding import PartitionSpec as P

D = 5120
HD = 128
HGT = 30
WID = 52
SPAN = 7
ROWS = 128
EPSILON = 1e-06
SCALE = math.log2(math.e) / math.sqrt(HD)
NEG = -1e30
OWN_LINES, SIDE_LINES, QUERY_LINES = (0, 5), (7, 8), (1, 6)
SPARE = 16
HALF_ROWS = 2 * ROWS + SPARE
PART_ROWS = 4 * ROWS + SPARE


def rope_tables():
    spatial = HD // 6
    temporal = HD // 2 - 2 * spatial
    positions = np.arange(SPAN * ROWS)

    def freq(amount):
        exponent = np.arange(amount, dtype=np.float64) * 2.0 / (2 * amount)
        return (1.0 / 10000.0**exponent).astype(np.float32)

    def part(values, amount):
        return values.astype(np.float32)[:, None] * freq(amount)[None, :]

    angle = np.concatenate(
        [
            part(positions // (HGT * WID), temporal),
            part(positions // WID % HGT, spatial),
            part(positions % WID, spatial),
        ],
        axis=1,
    ).astype(np.float64)
    cosine = np.repeat(np.cos(angle), 2, axis=1).astype(np.float32)
    sine = np.stack([-np.sin(angle), np.sin(angle)], axis=2)
    return cosine, sine.reshape(SPAN * ROWS, HD).astype(np.float32)


def shifted(value, by, extra=()):
    peers = lax.axis_size("tile")
    pairs = [(i, i - by if i % 2 else i + by) for i in range(peers)]
    pairs = [pair for pair in pairs if 0 <= pair[1] < peers]
    return lax.ppermute(value, "tile", pairs + list(extra))


def swapped(value):
    peers = lax.axis_size("tile")
    return lax.ppermute(value, "tile", [(i, i ^ 1) for i in range(peers)])


def by_rows(total_row):
    factor = lax.rsqrt(total_row / D + EPSILON)
    return jnp.transpose(jnp.broadcast_to(factor, (ROWS, ROWS)))


def rotated(normal, cosine, sine, even):
    partner = jnp.where(even, pltpu.roll(normal, HD - 1, 1), pltpu.roll(normal, 1, 1))
    return normal * cosine + partner * sine


def prefix_live(shape, count):
    return lax.broadcasted_iota(jnp.int32, shape, 1) < count


def pieces(*totals):
    rows = []
    for rest in totals:
        for _ in range(3):
            rows.append(rest.astype(jnp.bfloat16).astype(jnp.float32))
            rest = rest - rows[-1]
    rows.append(jnp.zeros((SPARE - len(rows), ROWS), jnp.float32))
    return jnp.concatenate(rows, axis=0).astype(jnp.bfloat16)


def joined(rows, first):
    return rows[first : first + 1] + rows[first + 1 : first + 2] + rows[first + 2 : first + 3]


def pack_kernel(
    here_ref, q_hbm, k_hbm, v_hbm, c_hbm, t_hbm, theirs_ref, q_mine_ref, sums_ref,
    q_ref, k_ref, v_ref, c_ref, t_ref, arrived
):
    pairs = ((k_hbm, k_ref), (v_hbm, v_ref), (q_hbm, q_ref), (c_hbm, c_ref), (t_hbm, t_ref))
    copies = [
        pltpu.make_async_copy(source, target, arrived.at[index])
        for index, (source, target) in enumerate(pairs)
    ]
    for copy in copies:
        copy.start()
    core = lax.rem(here_ref[0], 2)
    half = theirs_ref.shape[1]

    def total(ref, first):
        rows = None
        for head in range(ref.shape[1] // HD):
            x = ref[first : first + ROWS, head * HD : (head + 1) * HD].astype(jnp.float32)
            rows = x * x if rows is None else rows + x * x
        return jnp.sum(jnp.transpose(rows), axis=0, keepdims=True)

    def split(ref, first):
        for side in range(2):
            row = side * HALF_ROWS + first
            theirs_ref[row : row + ROWS, :] = ref[:, side * half : (side + 1) * half]

    sums_ref[...] = jnp.zeros((8, ROWS), jnp.float32)
    copies[0].wait()
    split(k_ref, 0)
    k_total = total(k_ref, 0)
    copies[1].wait()
    split(v_ref, ROWS)
    copies[2].wait()
    low, high = q_ref[:, :half], q_ref[:, half:]
    q_mine_ref[...] = jnp.where(core == 0, low, high)
    theirs_ref[2 * HALF_ROWS :, :] = jnp.where(core == 0, high, low)
    q_total = total(q_ref, 0)
    sums_ref[0:1, :] = k_total
    sums_ref[1:2, :] = q_total
    for side in range(2):
        rows = slice(side * HALF_ROWS + 2 * ROWS, (side + 1) * HALF_ROWS)
        theirs_ref[rows, 0:ROWS] = pieces(k_total, q_total)
        theirs_ref[rows, ROWS:] = jnp.zeros((SPARE, half - ROWS), jnp.bfloat16)
    copies[3].wait()
    sums_ref[2:3, :] = total(c_ref, 0)
    copies[4].wait()
    sums_ref[3:4, :] = total(t_ref, 0)
    sums_ref[4:5, :] = total(t_ref, ROWS)


def mate_kernel(own_ref, got_ref, out_ref):
    rows = got_ref[2 * ROWS : HALF_ROWS, 0:ROWS].astype(jnp.float32)
    out_ref[...] = own_ref[...]
    out_ref[5:6, :] = joined(rows, 0)
    out_ref[6:7, :] = joined(rows, 3)


def table_kernel(own_ref, side_ref, out_ref):
    out_ref[0:8, :] = own_ref[...]
    out_ref[8:16, :] = jnp.zeros((8, ROWS), jnp.float32)
    out_ref[7:8, :] = side_ref[0:1, :]
    out_ref[8:9, :] = side_ref[5:6, :]


def pieces_kernel(sums_ref, out_ref):
    out_ref[...] = jnp.zeros(out_ref.shape, jnp.bfloat16)
    out_ref[:, 0:ROWS] = pieces(*(sums_ref[line : line + 1, :] for line in SIDE_LINES))


def part_kernel(here_ref, *rest):
    blocks, out_ref, arrived = rest[:-2], rest[-2], rest[-1]
    side = 1 - lax.rem(here_ref[0], 2)
    copies = []
    for index, block in enumerate(blocks):
        first = index * PART_ROWS
        for slot in range(2):
            row = pl.multiple_of((2 * slot + side) * HALF_ROWS, SPARE)
            goal = first + slot * 2 * ROWS
            copies.append((block.at[pl.ds(row, 2 * ROWS)], out_ref.at[goal : goal + 2 * ROWS]))
        goal = first + 4 * ROWS
        copies.append((block.at[2 * ROWS : HALF_ROWS], out_ref.at[goal : goal + SPARE]))
    copies = [pltpu.make_async_copy(*pair, arrived.at[i]) for i, pair in enumerate(copies)]
    for copy in copies:
        copy.start()
    for copy in copies:
        copy.wait()


def cross_kernel(item_ref, len_ref, here_ref, sums_ref, q_ref, k_ref, v_ref, qg_ref, kg_ref, out_ref):
    count = len_ref[item_ref[here_ref[0]]]
    q_factor = by_rows(sums_ref[2:3, :])
    k_factor = [by_rows(sums_ref[3:4, :]), by_rows(sums_ref[4:5, :])]
    live = prefix_live((ROWS, 2 * ROWS), count)
    for head in range(q_ref.shape[1] // HD):
        cols = slice(head * HD, (head + 1) * HD)
        q = (q_ref[:, cols].astype(jnp.float32) * q_factor * qg_ref[:, cols]).astype(jnp.bfloat16)
        keys = [
            (
                k_ref[h * ROWS : (h + 1) * ROWS, cols].astype(jnp.float32)
                * k_factor[h]
                * kg_ref[:, cols]
            ).astype(jnp.bfloat16)
            for h in range(2)
        ]
        k = jnp.concatenate(keys, axis=0)
        s = lax.dot_general(q, k, (((1,), (1,)), ((), ())), preferred_element_type=jnp.float32)
        s = jnp.where(live, s, NEG)
        w = jnp.exp2((s - jnp.max(s, axis=1, keepdims=True)) * SCALE)
        total = jnp.sum(w, axis=1, keepdims=True)
        o = jnp.dot(w.astype(jnp.bfloat16), v_ref[:, cols], preferred_element_type=jnp.float32)
        out_ref[:, cols] = o / total


def extent(item_ref, tile):
    tiles = item_ref.shape[0]
    item = item_ref[tile]
    before = jnp.int32(0)
    after = jnp.int32(0)
    for d in range(1, SPAN):
        lower = item_ref[jnp.maximum(tile - d, 0)] == item
        upper = item_ref[jnp.minimum(tile + d, tiles - 1)] == item
        before += jnp.where(jnp.logical_and(lower, tile - d >= 0), 1, 0)
        after += jnp.where(jnp.logical_and(upper, tile + d < tiles), 1, 0)
    return tile - before, tile + after


def turn(ref, rows, factor, gain_ref, cos_ref, sin_ref, start, dest_ref, goal):
    even = lax.rem(lax.broadcasted_iota(jnp.int32, (ROWS, HD), 1), 2) == 0
    cosine = cos_ref[pl.ds(start, ROWS), :]
    sine = sin_ref[pl.ds(start, ROWS), :]
    for head in range(ref.shape[1] // HD):
        cols = slice(head * HD, (head + 1) * HD)
        x = ref[rows, cols].astype(jnp.float32) * factor * gain_ref[:, cols]
        dest_ref[goal, cols] = rotated(x, cosine, sine, even).astype(jnp.bfloat16)


def gather(chip, rows_of, totals, block, core, left, bounds, gains, tables, keys_ref, values_ref, first_chip):
    first_a, last_a, first_b, last_b = bounds
    for parity in range(2):
        tile = left + 2 * chip + parity
        slot, row = rows_of(parity)
        key_rows = pl.ds(pl.multiple_of(row, SPARE), ROWS)
        value_rows = pl.ds(pl.multiple_of(row + ROWS, SPARE), ROWS)
        goal = pl.ds(pl.multiple_of((2 * (chip - first_chip) + parity) * ROWS, ROWS), ROWS)
        values_ref[goal, :] = block[value_rows, :]

        @pl.when(jnp.logical_and(tile >= first_a, tile <= last_b))
        def _(tile=tile, slot=slot, key_rows=key_rows, goal=goal):
            first = jnp.where(tile <= last_a, first_a, first_b)
            start = pl.multiple_of((tile - first) * ROWS, ROWS)
            total = jnp.where(slot == 0, *totals())
            turn(block, key_rows, by_rows(total), gains, *tables, start, keys_ref, goal)


def kept_rows(core, turned=0):
    def rows_of(parity):
        slot = jnp.where(core == parity, turned, 1 - turned)
        return slot, (2 * slot + core) * HALF_ROWS

    return rows_of


def part_rows(core, index, turned=0):
    def rows_of(parity):
        slot = jnp.where(core == parity, 1 - turned, turned)
        return slot, index * PART_ROWS + slot * 2 * ROWS

    return rows_of


def lines(ref, pair):
    return lambda: tuple(ref[line : line + 1, :] for line in pair)


def spares(ref, first):
    def totals():
        rows = ref[first : first + SPARE, 0:ROWS].astype(jnp.float32)
        return joined(rows, 0), joined(rows, 3)

    return totals


def near_kernel(
    item_ref, here_ref, sums_ref, mate_sums_ref, k_gain_ref, q_gain_ref, cos_ref, sin_ref, q_own_ref, got_ref,
    block_ref, kept_ref, part_ref, keys_ref, values_ref, own_turned_ref, mate_turned_ref
):
    core = lax.rem(here_ref[0], 2)
    left = here_ref[0] - core
    sign = 2 * core - 1
    half = keys_ref.shape[1]
    bounds = (*extent(item_ref, left), *extent(item_ref, left + 1))
    columns = pl.ds(pl.multiple_of(core * half, HD), half)
    k_gains, q_gains = k_gain_ref.at[:, columns], q_gain_ref.at[:, columns]
    tables = (cos_ref, sin_ref)
    for which, (source, rows, line, goal) in enumerate(
        (
            (q_own_ref, slice(0, ROWS), QUERY_LINES[0], own_turned_ref),
            (got_ref, slice(2 * HALF_ROWS, 2 * HALF_ROWS + ROWS), QUERY_LINES[1], mate_turned_ref),
        )
    ):
        is_a = core == which
        first = jnp.where(is_a, bounds[0], bounds[2])
        tile = jnp.where(is_a, left, left + 1)
        start = pl.multiple_of((tile - first) * ROWS, ROWS)
        factor = by_rows(sums_ref[line : line + 1, :])
        turn(source, rows, factor, q_gains, *tables, start, goal, slice(None))
    for chip, rows_of, totals, block in (
        (0, kept_rows(core), lines(sums_ref, OWN_LINES), block_ref),
        (sign, kept_rows(core), lines(sums_ref, SIDE_LINES), kept_ref),
        (-sign, part_rows(core, 0), lines(mate_sums_ref, SIDE_LINES), part_ref),
    ):
        gather(chip, rows_of, totals, block, core, left, bounds, k_gains, tables, keys_ref, values_ref, -1)


def attend(mate, item_ref, count_ref, here_ref, q_ref, keys_ref, values_ref, out_ref):
    core = lax.rem(here_ref[0], 2)
    left = here_ref[0] - core
    tile = left + (1 - core if mate else core)
    first, last = extent(item_ref, tile)
    window = pl.ds(pl.multiple_of((first - left + 6) * ROWS, ROWS), SPAN * ROWS)
    tiles = item_ref.shape[0]
    lanes = lax.broadcasted_iota(jnp.int32, (ROWS, ROWS), 1)
    live = []
    for slot in range(SPAN):
        count = count_ref[jnp.minimum(first + slot, tiles - 1)]
        live.append(lanes < jnp.where(first + slot <= last, count, 0))
    for head in range(q_ref.shape[1] // HD):
        cols = slice(head * HD, (head + 1) * HD)
        s = lax.dot_general(
            q_ref[:, cols],
            keys_ref[window, cols],
            (((1,), (1,)), ((), ())),
            preferred_element_type=jnp.float32,
        )
        parts = [
            jnp.where(live[slot], s[:, slot * ROWS : (slot + 1) * ROWS], NEG)
            for slot in range(SPAN)
        ]
        top = functools.reduce(jnp.maximum, parts)
        top = jnp.max(top, axis=1, keepdims=True)
        parts = [jnp.exp2((part - top) * SCALE) for part in parts]
        total = jnp.sum(functools.reduce(jnp.add, parts), axis=1, keepdims=True)
        weights = jnp.concatenate([part.astype(jnp.bfloat16) for part in parts], axis=1)
        mixed = jnp.dot(weights, values_ref[window, cols], preferred_element_type=jnp.float32)
        out_ref[:, cols] = mixed / total


def far_kernel(
    item_ref, count_ref, here_ref, k_gain_ref, cos_ref, sin_ref, q_ref, near_keys_ref, near_values_ref,
    second_ref, third_ref, part_ref, out_ref, keys_ref, values_ref
):
    core = lax.rem(here_ref[0], 2)
    left = here_ref[0] - core
    sign = 2 * core - 1
    half = keys_ref.shape[1]
    bounds = (*extent(item_ref, left), *extent(item_ref, left + 1))
    k_gains = k_gain_ref.at[:, pl.ds(pl.multiple_of(core * half, HD), half)]
    low_end = jnp.where(left == 6, 1, 0)
    high_end = jnp.where(left == item_ref.shape[0] - 8, 1, 0)
    near = slice(4 * ROWS, 10 * ROWS)
    keys_ref[near, :] = near_keys_ref[...]
    values_ref[near, :] = near_values_ref[...]
    for chip, rows_of, totals, block in (
        (2 * sign, kept_rows(core), spares(second_ref, 2 * ROWS), second_ref),
        (-3 * sign, kept_rows(core, jnp.where(sign > 0, low_end, high_end)), spares(third_ref, 2 * ROWS), third_ref),
        (-2 * sign, part_rows(core, 0), spares(part_ref, 4 * ROWS), part_ref),
        (3 * sign, part_rows(core, 1, jnp.where(sign > 0, high_end, low_end)), spares(part_ref, PART_ROWS + 4 * ROWS), part_ref),
    ):
        gather(
            chip, rows_of, totals, block, core, left, bounds, k_gains, (cos_ref, sin_ref), keys_ref, values_ref, -3
        )
    attend(True, item_ref, count_ref, here_ref, q_ref, keys_ref, values_ref, out_ref)


def join_kernel(here_ref, own_ref, other_ref, text_ref, out_ref):
    core = lax.rem(here_ref[0], 2)
    width = own_ref.shape[1]
    mine = pl.multiple_of(core * width, HD)
    theirs = pl.multiple_of((1 - core) * width, HD)
    out_ref[:, pl.ds(mine, width)] = (own_ref[...] + text_ref[:, pl.ds(mine, width)]).astype(
        jnp.bfloat16
    )
    out_ref[:, pl.ds(theirs, width)] = (other_ref[...] + text_ref[:, pl.ds(theirs, width)]).astype(
        jnp.bfloat16
    )


def call(kernel, out_shape, specs, scratch=(), flops=1000000, limit=40):
    return pl.pallas_call(
        kernel,
        out_shape=out_shape,
        in_specs=specs,
        out_specs=jax.tree.map(lambda _: pl.BlockSpec(memory_space=pltpu.VMEM), out_shape),
        scratch_shapes=list(scratch),
        compiler_params=pltpu.CompilerParams(vmem_limit_bytes=limit << 20),
        cost_estimate=pl.CostEstimate(flops=flops, bytes_accessed=4000000, transcendentals=0),
    )


def per_device(
    self_query,
    self_key,
    self_value,
    cross_query,
    text_key,
    text_value,
    query_gain,
    key_gain,
    cross_gain,
    text_gain,
    tile_item,
    row_count,
    text_len,
):
    smem = pl.BlockSpec(memory_space=pltpu.SMEM)
    vmem = pl.BlockSpec(memory_space=pltpu.VMEM)
    f32 = jnp.float32
    width = self_query.shape[1]
    half = width // 2
    here = lax.axis_index("tile").astype(jnp.int32)
    core = lax.rem(here, 2)
    where = here.reshape(1)

    bf16 = jnp.bfloat16
    hbm = pl.BlockSpec(memory_space=pltpu.HBM)
    theirs, q_mine, sums = call(
        pack_kernel,
        (
            jax.ShapeDtypeStruct((2 * HALF_ROWS + ROWS, half), bf16),
            jax.ShapeDtypeStruct((ROWS, half), bf16),
            jax.ShapeDtypeStruct((8, ROWS), f32),
        ),
        [smem] + [hbm] * 5,
        scratch=[pltpu.VMEM((ROWS, width), bf16)] * 4
        + [pltpu.VMEM((2 * ROWS, width), bf16), pltpu.SemaphoreType.DMA((5,))],
        limit=60,
    )(where, self_query, self_key, self_value, cross_query, text_key)
    got = swapped(theirs)
    peers = lax.axis_size("tile")
    sums = call(mate_kernel, jax.ShapeDtypeStruct((8, ROWS), f32), [vmem] * 2)(sums, got)
    side_sums = shifted(sums, 2)
    block = jnp.concatenate([theirs[: 2 * HALF_ROWS], got[: 2 * HALF_ROWS]], axis=0)
    block, side_sums = lax.optimization_barrier((block, side_sums))
    side = shifted(block, 2)
    sums = call(table_kernel, jax.ShapeDtypeStruct((16, ROWS), f32), [vmem] * 2)(sums, side_sums)
    sums = lax.psum(sums, "head")
    side, sums = lax.optimization_barrier((side, sums))
    marks = call(pieces_kernel, jax.ShapeDtypeStruct((SPARE, half), bf16), [vmem])(sums)
    side = lax.dynamic_update_slice(side, marks, (2 * ROWS, 0))
    second = shifted(side, 2)
    third = shifted(side, -8, ((2, 7), (peers - 3, peers - 8)))

    def parts(*blocks):
        return swapped(
            call(
                part_kernel,
                jax.ShapeDtypeStruct((len(blocks) * PART_ROWS, half), bf16),
                [smem] + [hbm] * len(blocks),
                scratch=[pltpu.SemaphoreType.DMA((3 * len(blocks),))],
            )(where, *blocks)
        )

    near_part = parts(side)
    mate_sums = swapped(sums)

    text_out = call(
        cross_kernel, jax.ShapeDtypeStruct((ROWS, width), f32), [smem] * 3 + [vmem] * 6, flops=400000000
    )(
        tile_item,
        text_len,
        where,
        sums,
        cross_query,
        text_key,
        text_value,
        cross_gain[None, :],
        text_gain[None, :],
    )
    q_gain, k_gain = query_gain[None, :], key_gain[None, :]
    text_out, q_gain, k_gain = lax.optimization_barrier((text_out, q_gain, k_gain))

    cosine, sine = (jnp.asarray(t) for t in rope_tables())
    near_keys, near_values, q_own, q_mate = call(
        near_kernel,
        (jax.ShapeDtypeStruct((6 * ROWS, half), bf16),) * 2 + (jax.ShapeDtypeStruct((ROWS, half), bf16),) * 2,
        [smem] * 2 + [vmem] * 11,
        flops=200000000,
    )(
        tile_item, where, sums, mate_sums, k_gain, q_gain, cosine, sine, q_mine, got, block, side, near_part
    )
    second, third, near_keys, near_values, text_out = lax.optimization_barrier(
        (second, third, near_keys, near_values, text_out)
    )
    far_part = parts(second, third)
    window = jax.ShapeDtypeStruct((14 * ROWS, half), bf16)
    mate_out, keys, values = call(
        far_kernel,
        (jax.ShapeDtypeStruct((ROWS, half), f32), window, window),
        [smem] * 3 + [vmem] * 9,
        flops=300000000,
    )(
        tile_item, row_count, where, k_gain, cosine, sine, q_mate, near_keys, near_values, second, third, far_part
    )
    rest = swapped(mate_out)
    own = call(
        functools.partial(attend, False),
        jax.ShapeDtypeStruct((ROWS, half), f32),
        [smem] * 3 + [vmem] * 3,
        flops=300000000,
    )(tile_item, row_count, where, q_own, keys, values)
    return call(
        join_kernel, jax.ShapeDtypeStruct((ROWS, width), bf16), [smem] + [vmem] * 3
    )(where, own, rest, text_out)


def solution(mesh):
    spread = P("tile", "head")
    in_specs = (spread,) * 6 + (P("head"),) * 4 + (P(),) * 3
    return jax.shard_map(
        per_device, mesh=mesh, in_specs=in_specs, out_specs=spread, check_vma=False
    )
```

```python
import functools
import math

import jax
import jax.numpy as jnp
import numpy as np
from jax import lax
from jax.experimental import pallas as pl
from jax.experimental.pallas import tpu as pltpu
from jax.sharding import PartitionSpec as P

D = 5120
HD = 128
HGT = 30
WID = 52
SPAN = 7
ROWS = 128
EPSILON = 1e-06
SCALE = math.log2(math.e) / math.sqrt(HD)
NEG = -1e30
OWN_LINES, SIDE_LINES, QUERY_LINES = (0, 5), (7, 8), (1, 6)
SPARE = 16
HALF_ROWS = 2 * ROWS + SPARE
PART_ROWS = 4 * ROWS + SPARE


def rope_tables():
    spatial = HD // 6
    temporal = HD // 2 - 2 * spatial
    positions = np.arange(SPAN * ROWS)

    def freq(amount):
        exponent = np.arange(amount, dtype=np.float64) * 2.0 / (2 * amount)
        return (1.0 / 10000.0**exponent).astype(np.float32)

    def part(values, amount):
        return values.astype(np.float32)[:, None] * freq(amount)[None, :]

    angle = np.concatenate(
        [
            part(positions // (HGT * WID), temporal),
            part(positions // WID % HGT, spatial),
            part(positions % WID, spatial),
        ],
        axis=1,
    ).astype(np.float64)
    cosine = np.repeat(np.cos(angle), 2, axis=1).astype(np.float32)
    sine = np.stack([-np.sin(angle), np.sin(angle)], axis=2)
    return cosine, sine.reshape(SPAN * ROWS, HD).astype(np.float32)


def shifted(value, by, extra=()):
    peers = lax.axis_size("tile")
    pairs = [(i, i - by if i % 2 else i + by) for i in range(peers)]
    pairs = [pair for pair in pairs if 0 <= pair[1] < peers]
    return lax.ppermute(value, "tile", pairs + list(extra))


def swapped(value):
    peers = lax.axis_size("tile")
    return lax.ppermute(value, "tile", [(i, i ^ 1) for i in range(peers)])


def by_rows(total_row):
    factor = lax.rsqrt(total_row / D + EPSILON)
    return jnp.transpose(jnp.broadcast_to(factor, (ROWS, ROWS)))


def rotated(normal, cosine, sine, even):
    partner = jnp.where(even, pltpu.roll(normal, HD - 1, 1), pltpu.roll(normal, 1, 1))
    return normal * cosine + partner * sine


def prefix_live(shape, count):
    return lax.broadcasted_iota(jnp.int32, shape, 1) < count


def pieces(*totals):
    rows = []
    for rest in totals:
        for _ in range(3):
            rows.append(rest.astype(jnp.bfloat16).astype(jnp.float32))
            rest = rest - rows[-1]
    rows.append(jnp.zeros((SPARE - len(rows), ROWS), jnp.float32))
    return jnp.concatenate(rows, axis=0).astype(jnp.bfloat16)


def joined(rows, first):
    return rows[first : first + 1] + rows[first + 1 : first + 2] + rows[first + 2 : first + 3]


def square_sums(ref, first):
    rows = None
    for head in range(ref.shape[1] // HD):
        x = ref[first : first + ROWS, head * HD : (head + 1) * HD].astype(jnp.float32)
        rows = x * x if rows is None else rows + x * x
    return jnp.sum(jnp.transpose(rows), axis=0, keepdims=True)


def pack_kernel(
    here_ref, q_hbm, k_hbm, v_hbm, theirs_ref, q_mine_ref, sums_ref, q_ref, k_ref, v_ref, arrived
):
    pairs = ((k_hbm, k_ref), (v_hbm, v_ref), (q_hbm, q_ref))
    copies = [
        pltpu.make_async_copy(source, target, arrived.at[index])
        for index, (source, target) in enumerate(pairs)
    ]
    for copy in copies:
        copy.start()
    core = lax.rem(here_ref[0], 2)
    half = theirs_ref.shape[1]

    def split(ref, first):
        for side in range(2):
            row = side * HALF_ROWS + first
            theirs_ref[row : row + ROWS, :] = ref[:, side * half : (side + 1) * half]

    sums_ref[...] = jnp.zeros((8, ROWS), jnp.float32)
    copies[0].wait()
    split(k_ref, 0)
    k_total = square_sums(k_ref, 0)
    copies[1].wait()
    split(v_ref, ROWS)
    copies[2].wait()
    low, high = q_ref[:, :half], q_ref[:, half:]
    q_mine_ref[...] = jnp.where(core == 0, low, high)
    theirs_ref[2 * HALF_ROWS :, :] = jnp.where(core == 0, high, low)
    q_total = square_sums(q_ref, 0)
    sums_ref[0:1, :] = k_total
    sums_ref[1:2, :] = q_total
    for side in range(2):
        rows = slice(side * HALF_ROWS + 2 * ROWS, (side + 1) * HALF_ROWS)
        theirs_ref[rows, 0:ROWS] = pieces(k_total, q_total)
        theirs_ref[rows, ROWS:] = jnp.zeros((SPARE, half - ROWS), jnp.bfloat16)


def text_sums_kernel(c_ref, t_ref, out_ref):
    out_ref[0:1, :] = square_sums(c_ref, 0)
    out_ref[1:2, :] = square_sums(t_ref, 0)
    out_ref[2:3, :] = square_sums(t_ref, ROWS)
    out_ref[3:8, :] = jnp.zeros((5, ROWS), jnp.float32)


def mate_kernel(own_ref, got_ref, out_ref):
    rows = got_ref[2 * ROWS : HALF_ROWS, 0:ROWS].astype(jnp.float32)
    out_ref[...] = own_ref[...]
    out_ref[5:6, :] = joined(rows, 0)
    out_ref[6:7, :] = joined(rows, 3)


def table_kernel(own_ref, side_ref, text_ref, out_ref):
    out_ref[0:8, :] = own_ref[...]
    out_ref[2:5, :] = text_ref[0:3, :]
    out_ref[8:16, :] = jnp.zeros((8, ROWS), jnp.float32)
    out_ref[7:8, :] = side_ref[0:1, :]
    out_ref[8:9, :] = side_ref[5:6, :]


def pieces_kernel(sums_ref, out_ref):
    out_ref[...] = jnp.zeros(out_ref.shape, jnp.bfloat16)
    out_ref[:, 0:ROWS] = pieces(*(sums_ref[line : line + 1, :] for line in SIDE_LINES))


def part_kernel(here_ref, *rest):
    blocks, out_ref, arrived = rest[:-2], rest[-2], rest[-1]
    side = 1 - lax.rem(here_ref[0], 2)
    copies = []
    for index, block in enumerate(blocks):
        first = index * PART_ROWS
        for slot in range(2):
            row = pl.multiple_of((2 * slot + side) * HALF_ROWS, SPARE)
            goal = first + slot * 2 * ROWS
            copies.append((block.at[pl.ds(row, 2 * ROWS)], out_ref.at[goal : goal + 2 * ROWS]))
        goal = first + 4 * ROWS
        copies.append((block.at[2 * ROWS : HALF_ROWS], out_ref.at[goal : goal + SPARE]))
    copies = [pltpu.make_async_copy(*pair, arrived.at[i]) for i, pair in enumerate(copies)]
    for copy in copies:
        copy.start()
    for copy in copies:
        copy.wait()


def cross_kernel(item_ref, len_ref, here_ref, sums_ref, q_ref, k_ref, v_ref, qg_ref, kg_ref, out_ref):
    count = len_ref[item_ref[here_ref[0]]]
    q_factor = by_rows(sums_ref[2:3, :])
    k_factor = [by_rows(sums_ref[3:4, :]), by_rows(sums_ref[4:5, :])]
    live = prefix_live((ROWS, 2 * ROWS), count)
    for head in range(q_ref.shape[1] // HD):
        cols = slice(head * HD, (head + 1) * HD)
        q = (q_ref[:, cols].astype(jnp.float32) * q_factor * qg_ref[:, cols]).astype(jnp.bfloat16)
        keys = [
            (
                k_ref[h * ROWS : (h + 1) * ROWS, cols].astype(jnp.float32)
                * k_factor[h]
                * kg_ref[:, cols]
            ).astype(jnp.bfloat16)
            for h in range(2)
        ]
        k = jnp.concatenate(keys, axis=0)
        s = lax.dot_general(q, k, (((1,), (1,)), ((), ())), preferred_element_type=jnp.float32)
        s = jnp.where(live, s, NEG)
        w = jnp.exp2((s - jnp.max(s, axis=1, keepdims=True)) * SCALE)
        total = jnp.sum(w, axis=1, keepdims=True)
        o = jnp.dot(w.astype(jnp.bfloat16), v_ref[:, cols], preferred_element_type=jnp.float32)
        out_ref[:, cols] = o / total


def extent(item_ref, tile):
    tiles = item_ref.shape[0]
    item = item_ref[tile]
    before = jnp.int32(0)
    after = jnp.int32(0)
    for d in range(1, SPAN):
        lower = item_ref[jnp.maximum(tile - d, 0)] == item
        upper = item_ref[jnp.minimum(tile + d, tiles - 1)] == item
        before += jnp.where(jnp.logical_and(lower, tile - d >= 0), 1, 0)
        after += jnp.where(jnp.logical_and(upper, tile + d < tiles), 1, 0)
    return tile - before, tile + after


def turn(ref, rows, factor, gain_ref, cos_ref, sin_ref, start, dest_ref, goal):
    even = lax.rem(lax.broadcasted_iota(jnp.int32, (ROWS, HD), 1), 2) == 0
    cosine = cos_ref[pl.ds(start, ROWS), :]
    sine = sin_ref[pl.ds(start, ROWS), :]
    for head in range(ref.shape[1] // HD):
        cols = slice(head * HD, (head + 1) * HD)
        x = ref[rows, cols].astype(jnp.float32) * factor * gain_ref[:, cols]
        dest_ref[goal, cols] = rotated(x, cosine, sine, even).astype(jnp.bfloat16)


def gather(chip, rows_of, totals, block, core, left, bounds, gains, tables, keys_ref, values_ref, first_chip):
    first_a, last_a, first_b, last_b = bounds
    for parity in range(2):
        tile = left + 2 * chip + parity
        slot, row = rows_of(parity)
        key_rows = pl.ds(pl.multiple_of(row, SPARE), ROWS)
        value_rows = pl.ds(pl.multiple_of(row + ROWS, SPARE), ROWS)
        goal = pl.ds(pl.multiple_of((2 * (chip - first_chip) + parity) * ROWS, ROWS), ROWS)
        values_ref[goal, :] = block[value_rows, :]

        @pl.when(jnp.logical_and(tile >= first_a, tile <= last_b))
        def _(tile=tile, slot=slot, key_rows=key_rows, goal=goal):
            first = jnp.where(tile <= last_a, first_a, first_b)
            start = pl.multiple_of((tile - first) * ROWS, ROWS)
            total = jnp.where(slot == 0, *totals())
            turn(block, key_rows, by_rows(total), gains, *tables, start, keys_ref, goal)


def kept_rows(core, turned=0):
    def rows_of(parity):
        slot = jnp.where(core == parity, turned, 1 - turned)
        return slot, (2 * slot + core) * HALF_ROWS

    return rows_of


def part_rows(core, index, turned=0):
    def rows_of(parity):
        slot = jnp.where(core == parity, 1 - turned, turned)
        return slot, index * PART_ROWS + slot * 2 * ROWS

    return rows_of


def lines(ref, pair):
    return lambda: tuple(ref[line : line + 1, :] for line in pair)


def spares(ref, first):
    def totals():
        rows = ref[first : first + SPARE, 0:ROWS].astype(jnp.float32)
        return joined(rows, 0), joined(rows, 3)

    return totals


def near_kernel(
    item_ref, here_ref, sums_ref, mate_sums_ref, k_gain_ref, q_gain_ref, cos_ref, sin_ref, q_own_ref, got_ref,
    block_ref, kept_ref, part_ref, keys_ref, values_ref, own_turned_ref, mate_turned_ref
):
    core = lax.rem(here_ref[0], 2)
    left = here_ref[0] - core
    sign = 2 * core - 1
    half = keys_ref.shape[1]
    bounds = (*extent(item_ref, left), *extent(item_ref, left + 1))
    columns = pl.ds(pl.multiple_of(core * half, HD), half)
    k_gains, q_gains = k_gain_ref.at[:, columns], q_gain_ref.at[:, columns]
    tables = (cos_ref, sin_ref)
    for which, (source, rows, line, goal) in enumerate(
        (
            (q_own_ref, slice(0, ROWS), QUERY_LINES[0], own_turned_ref),
            (got_ref, slice(2 * HALF_ROWS, 2 * HALF_ROWS + ROWS), QUERY_LINES[1], mate_turned_ref),
        )
    ):
        is_a = core == which
        first = jnp.where(is_a, bounds[0], bounds[2])
        tile = jnp.where(is_a, left, left + 1)
        start = pl.multiple_of((tile - first) * ROWS, ROWS)
        factor = by_rows(sums_ref[line : line + 1, :])
        turn(source, rows, factor, q_gains, *tables, start, goal, slice(None))
    for chip, rows_of, totals, block in (
        (0, kept_rows(core), lines(sums_ref, OWN_LINES), block_ref),
        (sign, kept_rows(core), lines(sums_ref, SIDE_LINES), kept_ref),
        (-sign, part_rows(core, 0), lines(mate_sums_ref, SIDE_LINES), part_ref),
    ):
        gather(chip, rows_of, totals, block, core, left, bounds, k_gains, tables, keys_ref, values_ref, -1)


def attend(mate, item_ref, count_ref, here_ref, q_ref, keys_ref, values_ref, out_ref):
    core = lax.rem(here_ref[0], 2)
    left = here_ref[0] - core
    tile = left + (1 - core if mate else core)
    first, last = extent(item_ref, tile)
    window = pl.ds(pl.multiple_of((first - left + 6) * ROWS, ROWS), SPAN * ROWS)
    tiles = item_ref.shape[0]
    lanes = lax.broadcasted_iota(jnp.int32, (ROWS, ROWS), 1)
    live = []
    for slot in range(SPAN):
        count = count_ref[jnp.minimum(first + slot, tiles - 1)]
        live.append(lanes < jnp.where(first + slot <= last, count, 0))
    for head in range(q_ref.shape[1] // HD):
        cols = slice(head * HD, (head + 1) * HD)
        s = lax.dot_general(
            q_ref[:, cols],
            keys_ref[window, cols],
            (((1,), (1,)), ((), ())),
            preferred_element_type=jnp.float32,
        )
        parts = [
            jnp.where(live[slot], s[:, slot * ROWS : (slot + 1) * ROWS], NEG)
            for slot in range(SPAN)
        ]
        top = functools.reduce(jnp.maximum, parts)
        top = jnp.max(top, axis=1, keepdims=True)
        parts = [jnp.exp2((part - top) * SCALE) for part in parts]
        total = jnp.sum(functools.reduce(jnp.add, parts), axis=1, keepdims=True)
        weights = jnp.concatenate([part.astype(jnp.bfloat16) for part in parts], axis=1)
        mixed = jnp.dot(weights, values_ref[window, cols], preferred_element_type=jnp.float32)
        out_ref[:, cols] = mixed / total


def far_kernel(
    item_ref, count_ref, here_ref, k_gain_ref, cos_ref, sin_ref, q_ref, near_keys_ref, near_values_ref,
    second_ref, third_ref, part_ref, out_ref, keys_ref, values_ref
):
    core = lax.rem(here_ref[0], 2)
    left = here_ref[0] - core
    sign = 2 * core - 1
    half = keys_ref.shape[1]
    bounds = (*extent(item_ref, left), *extent(item_ref, left + 1))
    k_gains = k_gain_ref.at[:, pl.ds(pl.multiple_of(core * half, HD), half)]
    low_end = jnp.where(left == 6, 1, 0)
    high_end = jnp.where(left == item_ref.shape[0] - 8, 1, 0)
    near = slice(4 * ROWS, 10 * ROWS)
    keys_ref[near, :] = near_keys_ref[...]
    values_ref[near, :] = near_values_ref[...]
    for chip, rows_of, totals, block in (
        (2 * sign, kept_rows(core), spares(second_ref, 2 * ROWS), second_ref),
        (-3 * sign, kept_rows(core, jnp.where(sign > 0, low_end, high_end)), spares(third_ref, 2 * ROWS), third_ref),
        (-2 * sign, part_rows(core, 0), spares(part_ref, 4 * ROWS), part_ref),
        (3 * sign, part_rows(core, 1, jnp.where(sign > 0, high_end, low_end)), spares(part_ref, PART_ROWS + 4 * ROWS), part_ref),
    ):
        gather(
            chip, rows_of, totals, block, core, left, bounds, k_gains, (cos_ref, sin_ref), keys_ref, values_ref, -3
        )
    attend(True, item_ref, count_ref, here_ref, q_ref, keys_ref, values_ref, out_ref)


def join_kernel(here_ref, own_ref, other_ref, text_ref, out_ref):
    core = lax.rem(here_ref[0], 2)
    width = own_ref.shape[1]
    mine = pl.multiple_of(core * width, HD)
    theirs = pl.multiple_of((1 - core) * width, HD)
    out_ref[:, pl.ds(mine, width)] = (own_ref[...] + text_ref[:, pl.ds(mine, width)]).astype(
        jnp.bfloat16
    )
    out_ref[:, pl.ds(theirs, width)] = (other_ref[...] + text_ref[:, pl.ds(theirs, width)]).astype(
        jnp.bfloat16
    )


def call(kernel, out_shape, specs, scratch=(), flops=1000000, limit=40):
    return pl.pallas_call(
        kernel,
        out_shape=out_shape,
        in_specs=specs,
        out_specs=jax.tree.map(lambda _: pl.BlockSpec(memory_space=pltpu.VMEM), out_shape),
        scratch_shapes=list(scratch),
        compiler_params=pltpu.CompilerParams(vmem_limit_bytes=limit << 20),
        cost_estimate=pl.CostEstimate(flops=flops, bytes_accessed=4000000, transcendentals=0),
    )


def per_device(
    self_query,
    self_key,
    self_value,
    cross_query,
    text_key,
    text_value,
    query_gain,
    key_gain,
    cross_gain,
    text_gain,
    tile_item,
    row_count,
    text_len,
):
    smem = pl.BlockSpec(memory_space=pltpu.SMEM)
    vmem = pl.BlockSpec(memory_space=pltpu.VMEM)
    f32 = jnp.float32
    width = self_query.shape[1]
    half = width // 2
    here = lax.axis_index("tile").astype(jnp.int32)
    core = lax.rem(here, 2)
    where = here.reshape(1)

    bf16 = jnp.bfloat16
    hbm = pl.BlockSpec(memory_space=pltpu.HBM)
    theirs, q_mine, sums = call(
        pack_kernel,
        (
            jax.ShapeDtypeStruct((2 * HALF_ROWS + ROWS, half), bf16),
            jax.ShapeDtypeStruct((ROWS, half), bf16),
            jax.ShapeDtypeStruct((8, ROWS), f32),
        ),
        [smem] + [hbm] * 3,
        scratch=[pltpu.VMEM((ROWS, width), bf16)] * 3 + [pltpu.SemaphoreType.DMA((3,))],
        limit=60,
    )(where, self_query, self_key, self_value)
    got = swapped(theirs)
    peers = lax.axis_size("tile")
    sums = call(mate_kernel, jax.ShapeDtypeStruct((8, ROWS), f32), [vmem] * 2)(sums, got)
    text_sums = call(text_sums_kernel, jax.ShapeDtypeStruct((8, ROWS), f32), [vmem] * 2)(cross_query, text_key)
    side_sums = shifted(sums, 2)
    block = jnp.concatenate([theirs[: 2 * HALF_ROWS], got[: 2 * HALF_ROWS]], axis=0)
    block, side_sums, text_sums = lax.optimization_barrier((block, side_sums, text_sums))
    side = shifted(block, 2)
    sums = call(table_kernel, jax.ShapeDtypeStruct((16, ROWS), f32), [vmem] * 3)(
        sums, side_sums, text_sums
    )
    sums = lax.psum(sums, "head")
    side, sums = lax.optimization_barrier((side, sums))
    marks = call(pieces_kernel, jax.ShapeDtypeStruct((SPARE, half), bf16), [vmem])(sums)
    side = lax.dynamic_update_slice(side, marks, (2 * ROWS, 0))
    second = shifted(side, 2)
    third = shifted(side, -8, ((2, 7), (peers - 3, peers - 8)))

    def parts(*blocks):
        return swapped(
            call(
                part_kernel,
                jax.ShapeDtypeStruct((len(blocks) * PART_ROWS, half), bf16),
                [smem] + [hbm] * len(blocks),
                scratch=[pltpu.SemaphoreType.DMA((3 * len(blocks),))],
            )(where, *blocks)
        )

    near_part = parts(side)
    mate_sums = swapped(sums)

    text_out = call(
        cross_kernel, jax.ShapeDtypeStruct((ROWS, width), f32), [smem] * 3 + [vmem] * 6, flops=400000000
    )(
        tile_item,
        text_len,
        where,
        sums,
        cross_query,
        text_key,
        text_value,
        cross_gain[None, :],
        text_gain[None, :],
    )
    q_gain, k_gain = query_gain[None, :], key_gain[None, :]
    text_out, q_gain, k_gain = lax.optimization_barrier((text_out, q_gain, k_gain))

    cosine, sine = (jnp.asarray(t) for t in rope_tables())
    near_keys, near_values, q_own, q_mate = call(
        near_kernel,
        (jax.ShapeDtypeStruct((6 * ROWS, half), bf16),) * 2 + (jax.ShapeDtypeStruct((ROWS, half), bf16),) * 2,
        [smem] * 2 + [vmem] * 11,
        flops=200000000,
    )(
        tile_item, where, sums, mate_sums, k_gain, q_gain, cosine, sine, q_mine, got, block, side, near_part
    )
    second, third, near_keys, near_values, text_out = lax.optimization_barrier(
        (second, third, near_keys, near_values, text_out)
    )
    far_part = parts(second, third)
    window = jax.ShapeDtypeStruct((14 * ROWS, half), bf16)
    mate_out, keys, values = call(
        far_kernel,
        (jax.ShapeDtypeStruct((ROWS, half), f32), window, window),
        [smem] * 3 + [vmem] * 9,
        flops=300000000,
    )(
        tile_item, row_count, where, k_gain, cosine, sine, q_mate, near_keys, near_values, second, third, far_part
    )
    rest = swapped(mate_out)
    own = call(
        functools.partial(attend, False),
        jax.ShapeDtypeStruct((ROWS, half), f32),
        [smem] * 3 + [vmem] * 3,
        flops=300000000,
    )(tile_item, row_count, where, q_own, keys, values)
    return call(
        join_kernel, jax.ShapeDtypeStruct((ROWS, width), bf16), [smem] + [vmem] * 3
    )(where, own, rest, text_out)


def solution(mesh):
    spread = P("tile", "head")
    in_specs = (spread,) * 6 + (P("head"),) * 4 + (P(),) * 3
    return jax.shard_map(
        per_device, mesh=mesh, in_specs=in_specs, out_specs=spread, check_vma=False
    )
```

```python
import functools
import math

import jax
import jax.numpy as jnp
import numpy as np
from jax import lax
from jax.experimental import pallas as pl
from jax.experimental.pallas import tpu as pltpu
from jax.sharding import PartitionSpec as P

D = 5120
HD = 128
HGT = 30
WID = 52
SPAN = 7
ROWS = 128
EPSILON = 1e-06
SCALE = math.log2(math.e) / math.sqrt(HD)
NEG = -1e30
OWN_LINES, SIDE_LINES, QUERY_LINES = (0, 5), (7, 8), (1, 6)
SPARE = 16
HALF_ROWS = 2 * ROWS + SPARE
PART_ROWS = 4 * ROWS + SPARE


def rope_tables():
    spatial = HD // 6
    temporal = HD // 2 - 2 * spatial
    positions = np.arange(SPAN * ROWS)

    def freq(amount):
        exponent = np.arange(amount, dtype=np.float64) * 2.0 / (2 * amount)
        return (1.0 / 10000.0**exponent).astype(np.float32)

    def part(values, amount):
        return values.astype(np.float32)[:, None] * freq(amount)[None, :]

    angle = np.concatenate(
        [
            part(positions // (HGT * WID), temporal),
            part(positions // WID % HGT, spatial),
            part(positions % WID, spatial),
        ],
        axis=1,
    ).astype(np.float64)
    cosine = np.repeat(np.cos(angle), 2, axis=1).astype(np.float32)
    sine = np.stack([-np.sin(angle), np.sin(angle)], axis=2)
    return cosine, sine.reshape(SPAN * ROWS, HD).astype(np.float32)


def shifted(value, by, extra=()):
    peers = lax.axis_size("tile")
    pairs = [(i, i - by if i % 2 else i + by) for i in range(peers)]
    pairs = [pair for pair in pairs if 0 <= pair[1] < peers]
    return lax.ppermute(value, "tile", pairs + list(extra))


def swapped(value):
    peers = lax.axis_size("tile")
    return lax.ppermute(value, "tile", [(i, i ^ 1) for i in range(peers)])


def by_rows(total_row):
    factor = lax.rsqrt(total_row / D + EPSILON)
    return jnp.transpose(jnp.broadcast_to(factor, (ROWS, ROWS)))


def rotated(normal, cosine, sine, even):
    partner = jnp.where(even, pltpu.roll(normal, HD - 1, 1), pltpu.roll(normal, 1, 1))
    return normal * cosine + partner * sine


def prefix_live(shape, count):
    return lax.broadcasted_iota(jnp.int32, shape, 1) < count


def pieces(*totals):
    rows = []
    for rest in totals:
        for _ in range(3):
            rows.append(rest.astype(jnp.bfloat16).astype(jnp.float32))
            rest = rest - rows[-1]
    rows.append(jnp.zeros((SPARE - len(rows), ROWS), jnp.float32))
    return jnp.concatenate(rows, axis=0).astype(jnp.bfloat16)


def joined(rows, first):
    return rows[first : first + 1] + rows[first + 1 : first + 2] + rows[first + 2 : first + 3]


def pack_kernel(
    here_ref, q_hbm, k_hbm, v_hbm, c_hbm, t_hbm, theirs_ref, own_ref, q_mine_ref, sums_ref,
    q_ref, k_ref, v_ref, c_ref, t_ref, arrived
):
    pairs = ((k_hbm, k_ref), (v_hbm, v_ref), (q_hbm, q_ref), (c_hbm, c_ref), (t_hbm, t_ref))
    copies = [
        pltpu.make_async_copy(source, target, arrived.at[index])
        for index, (source, target) in enumerate(pairs)
    ]
    for copy in copies:
        copy.start()
    core = lax.rem(here_ref[0], 2)
    half = theirs_ref.shape[1]

    def total(ref, first):
        rows = None
        for head in range(ref.shape[1] // HD):
            x = ref[first : first + ROWS, head * HD : (head + 1) * HD].astype(jnp.float32)
            rows = x * x if rows is None else rows + x * x
        return jnp.sum(jnp.transpose(rows), axis=0, keepdims=True)

    def split(ref, first):
        for side in range(2):
            row = side * HALF_ROWS + first
            part = ref[:, side * half : (side + 1) * half]
            theirs_ref[row : row + ROWS, :] = part
            own_ref[row : row + ROWS, :] = part

    sums_ref[...] = jnp.zeros((8, ROWS), jnp.float32)
    copies[0].wait()
    split(k_ref, 0)
    k_total = total(k_ref, 0)
    copies[1].wait()
    split(v_ref, ROWS)
    copies[2].wait()
    low, high = q_ref[:, :half], q_ref[:, half:]
    q_mine_ref[...] = jnp.where(core == 0, low, high)
    theirs_ref[2 * HALF_ROWS :, :] = jnp.where(core == 0, high, low)
    q_total = total(q_ref, 0)
    sums_ref[0:1, :] = k_total
    sums_ref[1:2, :] = q_total
    for side in range(2):
        rows = slice(side * HALF_ROWS + 2 * ROWS, (side + 1) * HALF_ROWS)
        for ref in (theirs_ref, own_ref):
            ref[rows, 0:ROWS] = pieces(k_total, q_total)
            ref[rows, ROWS:] = jnp.zeros((SPARE, half - ROWS), jnp.bfloat16)
    copies[3].wait()
    sums_ref[2:3, :] = total(c_ref, 0)
    copies[4].wait()
    sums_ref[3:4, :] = total(t_ref, 0)
    sums_ref[4:5, :] = total(t_ref, ROWS)


def mate_kernel(own_ref, got_ref, out_ref):
    rows = got_ref[2 * ROWS : HALF_ROWS, 0:ROWS].astype(jnp.float32)
    out_ref[...] = own_ref[...]
    out_ref[5:6, :] = joined(rows, 0)
    out_ref[6:7, :] = joined(rows, 3)


def table_kernel(own_ref, side_ref, out_ref):
    out_ref[0:8, :] = own_ref[...]
    out_ref[8:16, :] = jnp.zeros((8, ROWS), jnp.float32)
    out_ref[7:8, :] = side_ref[0:1, :]
    out_ref[8:9, :] = side_ref[5:6, :]


def pieces_kernel(sums_ref, out_ref):
    out_ref[...] = jnp.zeros(out_ref.shape, jnp.bfloat16)
    out_ref[:, 0:ROWS] = pieces(*(sums_ref[line : line + 1, :] for line in SIDE_LINES))


def part_kernel(here_ref, *rest):
    blocks, out_ref, arrived = rest[:-2], rest[-2], rest[-1]
    side = 1 - lax.rem(here_ref[0], 2)
    copies = []
    for index, block in enumerate(blocks):
        first = index * PART_ROWS
        for slot in range(2):
            row = pl.multiple_of((2 * slot + side) * HALF_ROWS, SPARE)
            goal = first + slot * 2 * ROWS
            copies.append((block.at[pl.ds(row, 2 * ROWS)], out_ref.at[goal : goal + 2 * ROWS]))
        goal = first + 4 * ROWS
        copies.append((block.at[2 * ROWS : HALF_ROWS], out_ref.at[goal : goal + SPARE]))
    copies = [pltpu.make_async_copy(*pair, arrived.at[i]) for i, pair in enumerate(copies)]
    for copy in copies:
        copy.start()
    for copy in copies:
        copy.wait()


def cross_kernel(item_ref, len_ref, here_ref, sums_ref, q_ref, k_ref, v_ref, qg_ref, kg_ref, out_ref):
    count = len_ref[item_ref[here_ref[0]]]
    q_factor = by_rows(sums_ref[2:3, :])
    k_factor = [by_rows(sums_ref[3:4, :]), by_rows(sums_ref[4:5, :])]
    live = prefix_live((ROWS, 2 * ROWS), count)
    for head in range(q_ref.shape[1] // HD):
        cols = slice(head * HD, (head + 1) * HD)
        q = (q_ref[:, cols].astype(jnp.float32) * q_factor * qg_ref[:, cols]).astype(jnp.bfloat16)
        keys = [
            (
                k_ref[h * ROWS : (h + 1) * ROWS, cols].astype(jnp.float32)
                * k_factor[h]
                * kg_ref[:, cols]
            ).astype(jnp.bfloat16)
            for h in range(2)
        ]
        k = jnp.concatenate(keys, axis=0)
        s = lax.dot_general(q, k, (((1,), (1,)), ((), ())), preferred_element_type=jnp.float32)
        s = jnp.where(live, s, NEG)
        w = jnp.exp2((s - jnp.max(s, axis=1, keepdims=True)) * SCALE)
        total = jnp.sum(w, axis=1, keepdims=True)
        o = jnp.dot(w.astype(jnp.bfloat16), v_ref[:, cols], preferred_element_type=jnp.float32)
        out_ref[:, cols] = o / total


def extent(item_ref, tile):
    tiles = item_ref.shape[0]
    item = item_ref[tile]
    before = jnp.int32(0)
    after = jnp.int32(0)
    for d in range(1, SPAN):
        lower = item_ref[jnp.maximum(tile - d, 0)] == item
        upper = item_ref[jnp.minimum(tile + d, tiles - 1)] == item
        before += jnp.where(jnp.logical_and(lower, tile - d >= 0), 1, 0)
        after += jnp.where(jnp.logical_and(upper, tile + d < tiles), 1, 0)
    return tile - before, tile + after


def turn(ref, rows, factor, gain_ref, cos_ref, sin_ref, start, dest_ref, goal):
    even = lax.rem(lax.broadcasted_iota(jnp.int32, (ROWS, HD), 1), 2) == 0
    cosine = cos_ref[pl.ds(start, ROWS), :]
    sine = sin_ref[pl.ds(start, ROWS), :]
    for head in range(ref.shape[1] // HD):
        cols = slice(head * HD, (head + 1) * HD)
        x = ref[rows, cols].astype(jnp.float32) * factor * gain_ref[:, cols]
        dest_ref[goal, cols] = rotated(x, cosine, sine, even).astype(jnp.bfloat16)


def gather(chip, rows_of, totals, block, core, left, bounds, gains, tables, keys_ref, values_ref, first_chip):
    first_a, last_a, first_b, last_b = bounds
    for parity in range(2):
        tile = left + 2 * chip + parity
        slot, row = rows_of(parity)
        key_rows = pl.ds(pl.multiple_of(row, SPARE), ROWS)
        value_rows = pl.ds(pl.multiple_of(row + ROWS, SPARE), ROWS)
        goal = pl.ds(pl.multiple_of((2 * (chip - first_chip) + parity) * ROWS, ROWS), ROWS)
        values_ref[goal, :] = block[value_rows, :]

        @pl.when(jnp.logical_and(tile >= first_a, tile <= last_b))
        def _(tile=tile, slot=slot, key_rows=key_rows, goal=goal):
            first = jnp.where(tile <= last_a, first_a, first_b)
            start = pl.multiple_of((tile - first) * ROWS, ROWS)
            total = jnp.where(slot == 0, *totals())
            turn(block, key_rows, by_rows(total), gains, *tables, start, keys_ref, goal)


def kept_rows(core, turned=0):
    def rows_of(parity):
        slot = jnp.where(core == parity, turned, 1 - turned)
        return slot, (2 * slot + core) * HALF_ROWS

    return rows_of


def part_rows(core, index, turned=0):
    def rows_of(parity):
        slot = jnp.where(core == parity, 1 - turned, turned)
        return slot, index * PART_ROWS + slot * 2 * ROWS

    return rows_of


def lines(ref, pair):
    return lambda: tuple(ref[line : line + 1, :] for line in pair)


def spares(ref, first):
    def totals():
        rows = ref[first : first + SPARE, 0:ROWS].astype(jnp.float32)
        return joined(rows, 0), joined(rows, 3)

    return totals


def near_kernel(
    item_ref, here_ref, sums_ref, mate_sums_ref, k_gain_ref, q_gain_ref, cos_ref, sin_ref, q_own_ref, got_ref,
    block_ref, kept_ref, part_ref, keys_ref, values_ref, own_turned_ref, mate_turned_ref
):
    core = lax.rem(here_ref[0], 2)
    left = here_ref[0] - core
    sign = 2 * core - 1
    half = keys_ref.shape[1]
    bounds = (*extent(item_ref, left), *extent(item_ref, left + 1))
    columns = pl.ds(pl.multiple_of(core * half, HD), half)
    k_gains, q_gains = k_gain_ref.at[:, columns], q_gain_ref.at[:, columns]
    tables = (cos_ref, sin_ref)
    for which, (source, rows, line, goal) in enumerate(
        (
            (q_own_ref, slice(0, ROWS), QUERY_LINES[0], own_turned_ref),
            (got_ref, slice(2 * HALF_ROWS, 2 * HALF_ROWS + ROWS), QUERY_LINES[1], mate_turned_ref),
        )
    ):
        is_a = core == which
        first = jnp.where(is_a, bounds[0], bounds[2])
        tile = jnp.where(is_a, left, left + 1)
        start = pl.multiple_of((tile - first) * ROWS, ROWS)
        factor = by_rows(sums_ref[line : line + 1, :])
        turn(source, rows, factor, q_gains, *tables, start, goal, slice(None))
    for chip, rows_of, totals, block in (
        (0, kept_rows(core), lines(sums_ref, OWN_LINES), block_ref),
        (sign, kept_rows(core), lines(sums_ref, SIDE_LINES), kept_ref),
        (-sign, part_rows(core, 0), lines(mate_sums_ref, SIDE_LINES), part_ref),
    ):
        gather(chip, rows_of, totals, block, core, left, bounds, k_gains, tables, keys_ref, values_ref, -1)


def attend(mate, item_ref, count_ref, here_ref, q_ref, keys_ref, values_ref, out_ref):
    core = lax.rem(here_ref[0], 2)
    left = here_ref[0] - core
    tile = left + (1 - core if mate else core)
    first, last = extent(item_ref, tile)
    window = pl.ds(pl.multiple_of((first - left + 6) * ROWS, ROWS), SPAN * ROWS)
    tiles = item_ref.shape[0]
    lanes = lax.broadcasted_iota(jnp.int32, (ROWS, ROWS), 1)
    live = []
    for slot in range(SPAN):
        count = count_ref[jnp.minimum(first + slot, tiles - 1)]
        live.append(lanes < jnp.where(first + slot <= last, count, 0))
    for head in range(q_ref.shape[1] // HD):
        cols = slice(head * HD, (head + 1) * HD)
        s = lax.dot_general(
            q_ref[:, cols],
            keys_ref[window, cols],
            (((1,), (1,)), ((), ())),
            preferred_element_type=jnp.float32,
        )
        parts = [
            jnp.where(live[slot], s[:, slot * ROWS : (slot + 1) * ROWS], NEG)
            for slot in range(SPAN)
        ]
        top = functools.reduce(jnp.maximum, parts)
        top = jnp.max(top, axis=1, keepdims=True)
        parts = [jnp.exp2((part - top) * SCALE) for part in parts]
        total = jnp.sum(functools.reduce(jnp.add, parts), axis=1, keepdims=True)
        weights = jnp.concatenate([part.astype(jnp.bfloat16) for part in parts], axis=1)
        mixed = jnp.dot(weights, values_ref[window, cols], preferred_element_type=jnp.float32)
        out_ref[:, cols] = mixed / total


def far_kernel(
    item_ref, count_ref, here_ref, k_gain_ref, cos_ref, sin_ref, q_ref, near_keys_ref, near_values_ref,
    second_ref, third_ref, part_ref, out_ref, keys_ref, values_ref
):
    core = lax.rem(here_ref[0], 2)
    left = here_ref[0] - core
    sign = 2 * core - 1
    half = keys_ref.shape[1]
    bounds = (*extent(item_ref, left), *extent(item_ref, left + 1))
    k_gains = k_gain_ref.at[:, pl.ds(pl.multiple_of(core * half, HD), half)]
    low_end = jnp.where(left == 6, 1, 0)
    high_end = jnp.where(left == item_ref.shape[0] - 8, 1, 0)
    near = slice(4 * ROWS, 10 * ROWS)
    keys_ref[near, :] = near_keys_ref[...]
    values_ref[near, :] = near_values_ref[...]
    for chip, rows_of, totals, block in (
        (2 * sign, kept_rows(core), spares(second_ref, 2 * ROWS), second_ref),
        (-3 * sign, kept_rows(core, jnp.where(sign > 0, low_end, high_end)), spares(third_ref, 2 * ROWS), third_ref),
        (-2 * sign, part_rows(core, 0), spares(part_ref, 4 * ROWS), part_ref),
        (3 * sign, part_rows(core, 1, jnp.where(sign > 0, high_end, low_end)), spares(part_ref, PART_ROWS + 4 * ROWS), part_ref),
    ):
        gather(
            chip, rows_of, totals, block, core, left, bounds, k_gains, (cos_ref, sin_ref), keys_ref, values_ref, -3
        )
    attend(True, item_ref, count_ref, here_ref, q_ref, keys_ref, values_ref, out_ref)


def join_kernel(here_ref, own_ref, other_ref, text_ref, out_ref):
    core = lax.rem(here_ref[0], 2)
    width = own_ref.shape[1]
    mine = pl.multiple_of(core * width, HD)
    theirs = pl.multiple_of((1 - core) * width, HD)
    out_ref[:, pl.ds(mine, width)] = (own_ref[...] + text_ref[:, pl.ds(mine, width)]).astype(
        jnp.bfloat16
    )
    out_ref[:, pl.ds(theirs, width)] = (other_ref[...] + text_ref[:, pl.ds(theirs, width)]).astype(
        jnp.bfloat16
    )


def call(kernel, out_shape, specs, scratch=(), flops=1000000, limit=40):
    return pl.pallas_call(
        kernel,
        out_shape=out_shape,
        in_specs=specs,
        out_specs=jax.tree.map(lambda _: pl.BlockSpec(memory_space=pltpu.VMEM), out_shape),
        scratch_shapes=list(scratch),
        compiler_params=pltpu.CompilerParams(vmem_limit_bytes=limit << 20),
        cost_estimate=pl.CostEstimate(flops=flops, bytes_accessed=4000000, transcendentals=0),
    )


def per_device(
    self_query,
    self_key,
    self_value,
    cross_query,
    text_key,
    text_value,
    query_gain,
    key_gain,
    cross_gain,
    text_gain,
    tile_item,
    row_count,
    text_len,
):
    smem = pl.BlockSpec(memory_space=pltpu.SMEM)
    vmem = pl.BlockSpec(memory_space=pltpu.VMEM)
    f32 = jnp.float32
    width = self_query.shape[1]
    half = width // 2
    here = lax.axis_index("tile").astype(jnp.int32)
    core = lax.rem(here, 2)
    where = here.reshape(1)

    bf16 = jnp.bfloat16
    hbm = pl.BlockSpec(memory_space=pltpu.HBM)
    theirs, own_tile, q_mine, sums = call(
        pack_kernel,
        (
            jax.ShapeDtypeStruct((2 * HALF_ROWS + ROWS, half), bf16),
            jax.ShapeDtypeStruct((2 * HALF_ROWS, half), bf16),
            jax.ShapeDtypeStruct((ROWS, half), bf16),
            jax.ShapeDtypeStruct((8, ROWS), f32),
        ),
        [smem] + [hbm] * 5,
        scratch=[pltpu.VMEM((ROWS, width), bf16)] * 4
        + [pltpu.VMEM((2 * ROWS, width), bf16), pltpu.SemaphoreType.DMA((5,))],
        limit=60,
    )(where, self_query, self_key, self_value, cross_query, text_key)
    got = swapped(theirs)
    peers = lax.axis_size("tile")
    sums = call(mate_kernel, jax.ShapeDtypeStruct((8, ROWS), f32), [vmem] * 2)(sums, got)
    side_sums = shifted(sums, 2)
    block = jnp.concatenate([own_tile, got[: 2 * HALF_ROWS]], axis=0)
    block, side_sums = lax.optimization_barrier((block, side_sums))
    side = shifted(block, 2)
    sums = call(table_kernel, jax.ShapeDtypeStruct((16, ROWS), f32), [vmem] * 2)(sums, side_sums)
    sums = lax.psum(sums, "head")
    side, sums = lax.optimization_barrier((side, sums))
    marks = call(pieces_kernel, jax.ShapeDtypeStruct((SPARE, half), bf16), [vmem])(sums)
    side = lax.dynamic_update_slice(side, marks, (2 * ROWS, 0))
    second = shifted(side, 2)
    third = shifted(side, -8, ((2, 7), (peers - 3, peers - 8)))

    def parts(*blocks):
        return swapped(
            call(
                part_kernel,
                jax.ShapeDtypeStruct((len(blocks) * PART_ROWS, half), bf16),
                [smem] + [hbm] * len(blocks),
                scratch=[pltpu.SemaphoreType.DMA((3 * len(blocks),))],
            )(where, *blocks)
        )

    near_part = parts(side)
    mate_sums = swapped(sums)

    text_out = call(
        cross_kernel, jax.ShapeDtypeStruct((ROWS, width), f32), [smem] * 3 + [vmem] * 6, flops=400000000
    )(
        tile_item,
        text_len,
        where,
        sums,
        cross_query,
        text_key,
        text_value,
        cross_gain[None, :],
        text_gain[None, :],
    )
    q_gain, k_gain = query_gain[None, :], key_gain[None, :]
    text_out, q_gain, k_gain = lax.optimization_barrier((text_out, q_gain, k_gain))

    cosine, sine = (jnp.asarray(t) for t in rope_tables())
    near_keys, near_values, q_own, q_mate = call(
        near_kernel,
        (jax.ShapeDtypeStruct((6 * ROWS, half), bf16),) * 2 + (jax.ShapeDtypeStruct((ROWS, half), bf16),) * 2,
        [smem] * 2 + [vmem] * 11,
        flops=200000000,
    )(
        tile_item, where, sums, mate_sums, k_gain, q_gain, cosine, sine, q_mine, got, block, side, near_part
    )
    second, third, near_keys, near_values, text_out = lax.optimization_barrier(
        (second, third, near_keys, near_values, text_out)
    )
    far_part = parts(second, third)
    window = jax.ShapeDtypeStruct((14 * ROWS, half), bf16)
    mate_out, keys, values = call(
        far_kernel,
        (jax.ShapeDtypeStruct((ROWS, half), f32), window, window),
        [smem] * 3 + [vmem] * 9,
        flops=300000000,
    )(
        tile_item, row_count, where, k_gain, cosine, sine, q_mate, near_keys, near_values, second, third, far_part
    )
    rest = swapped(mate_out)
    own = call(
        functools.partial(attend, False),
        jax.ShapeDtypeStruct((ROWS, half), f32),
        [smem] * 3 + [vmem] * 3,
        flops=300000000,
    )(tile_item, row_count, where, q_own, keys, values)
    return call(
        join_kernel, jax.ShapeDtypeStruct((ROWS, width), bf16), [smem] + [vmem] * 3
    )(where, own, rest, text_out)


def solution(mesh):
    spread = P("tile", "head")
    in_specs = (spread,) * 6 + (P("head"),) * 4 + (P(),) * 3
    return jax.shard_map(
        per_device, mesh=mesh, in_specs=in_specs, out_specs=spread, check_vma=False
    )
```
